128 devices in a mesh: dom: 16 (over y, x), slab: 8 (over z, core).
Axes of the slice: x: 4, y: 4, z: 4, core: 2. Of those that a mesh axis runs over, the one named last changes fastest.
Arguments:
- particles: bfloat16 [8192, 320, 256], P('dom', 'slab'), may hold values from -8 to 8
- blocks: int32 [8192, 2], P('dom'), may hold values from 0 to 3, as said below
- references: bfloat16 [512, 320, 256], P(None, 'slab'), may hold values from -1 to 1
- inv_noise: float32 [320], P('slab'), may hold values from 0.5 to 2
- destination: int32 [320, 512], replicated, may hold values from 0 to 127, as said below
- row_index: int32 [320, 512], replicated, may hold values from 0 to 254
- fraction: float32 [320, 512], replicated, may hold values from 0 to 1
Outputs:
- volume_data: float32 [32768, 256], P(('dom', 'slab'))
- next_slab: bfloat16 [4096, 2048], P(None, 'slab')
The draws below stay inside these ranges and needn't reach their ends.
Inputs may be any that keep to these rules, and one draw needn't show every extreme that they name: Each particle names 2 different orientation blocks. destination is a device index in the order of the joined axes (dom, slab), dom major. Among the pieces whose group belongs to one index of slab and whose orientation belongs to one index of dom, no destination is named more than 16 times, and some destination exactly 16 times.
All inputs are finite; a program needn't handle non-finite values.
Results may differ from the reference program's by a relative error of at most 0.013.
Values may be sent and summed in bfloat16 or wider, within the bound.
A program may use at most 256 MiB of HBM per device.

```python
import math
import jax
import jax.numpy as jnp
from jax import lax

COEF = 128
G = 320
OB = 128
TOPB = 2
O = 512
P_DEV = 512
RD = 256
PARTS_SIZE = 8192
CAP = 16
N_DOM = 16
N_SLAB = 8
DEVICES = 128


def make_references(key):
    spread = 2.0 / math.sqrt(G * 2 * COEF)
    return spread * jnp.clip(jax.random.normal(key, (O, G, 2 * COEF), jnp.float32), -6.0, 6.0)


def make_blocks(key):
    number = O // OB
    scores = jax.random.randint(key, (PARTS_SIZE, number), 0, 1024) * number + jnp.arange(number, dtype=jnp.int32)[None, :]
    _, picked = lax.top_k(scores, TOPB)
    return picked.astype(jnp.int32)


def draw_references(key, part):
    return make_references(jax.random.fold_in(key, 7)).astype(jnp.bfloat16)


def draw_blocks(key, part):
    return make_blocks(jax.random.fold_in(key, 11))


def draw_particles(key, part):
    layout = (PARTS_SIZE, G, 2 * COEF)
    return jnp.clip(jax.random.normal(jax.random.fold_in(key, 3), layout, jnp.float32), -6.0, 6.0).astype(jnp.bfloat16)


def draw_destination(key, part):
    group_share = G // N_SLAB
    orient_share = O // N_DOM
    block_size = group_share * orient_share
    slot_count = DEVICES * CAP
    popular = (jax.random.randint(jax.random.fold_in(key, 21), (DEVICES,), 0, 4) == 0).astype(jnp.int32) * 4096

    def one_block(block_key):
        key_a, key_b, key_c = jax.random.split(block_key, 3)
        favored = jax.random.randint(key_a, (), 0, DEVICES)
        owners = jnp.arange(slot_count, dtype=jnp.int32) // CAP
        bonuses = popular[owners] + jnp.where(owners == favored, 16384, 0)
        scores = (bonuses + jax.random.randint(key_b, (slot_count,), 0, 4096)) * 65536 + jnp.arange(slot_count, dtype=jnp.int32)
        _, picked = lax.top_k(scores, block_size)
        shuffle = jax.random.permutation(key_c, block_size)
        return (picked // CAP)[shuffle].astype(jnp.int32)
    block_keys = jax.random.split(jax.random.fold_in(key, 23), DEVICES)
    table = jax.vmap(one_block)(block_keys)
    table = table.reshape(N_DOM, N_SLAB, orient_share, group_share).transpose(1, 3, 0, 2)
    return table.reshape(G, O)


def with_ends(values, own_key, smallest, largest):
    shape = values.shape
    index_at = [jax.random.randint(jax.random.fold_in(own_key, axis), (), 0, shape[axis]) for axis in range(len(shape))]
    values = values.at[tuple(index_at)].set(smallest)
    longest = shape.index(max(shape))
    index_at[longest] = (index_at[longest] + 1) % shape[longest]
    return values.at[tuple(index_at)].set(largest)


def levels(stream_key, shape, cuts, smallest, largest):
    loudness = 1.0
    for dim, parts in cuts:
        heights = jax.random.uniform(jax.random.fold_in(jax.random.fold_in(stream_key, 6), dim), (parts,), jnp.float32, smallest / len(cuts), largest / len(cuts))
        loudness = loudness * jnp.repeat(jnp.exp(heights), shape[dim] // parts).reshape((-1,) + (1,) * (len(shape) - 1 - dim))
    return loudness


def setup_inputs(seed: int = 0) -> dict:
    keys = jax.random.split(jax.random.key(seed), 8)
    return {
        "particles": draw_particles(jax.random.fold_in(keys[7], 71), 0),
        "blocks": draw_blocks(jax.random.fold_in(keys[7], 71), 0),
        "references": draw_references(jax.random.fold_in(keys[7], 71), 0),
        "inv_noise": jnp.clip(jnp.exp(math.log(2.0) - 1.3862944 * jax.random.uniform(keys[3], (G,), jnp.float32) ** levels(keys[3], (G,), ((0, 8),), -0.2, 0.2)), 0.5, 2.0),
        "destination": draw_destination(jax.random.fold_in(keys[7], 71), 0),
        "row_index": with_ends(jax.random.randint(keys[5], (G, O), 0, RD - 1), jax.random.fold_in(keys[5], 1), 0, (RD - 1) - 1).astype(jnp.int32),
        "fraction": jnp.clip(jax.random.uniform(keys[6], (G, O), jnp.float32, 0.0, 1.0), 0.0, 1.0),
    }


def reference(particles, blocks, references, inv_noise, destination, row_index, fraction):
    row_width = 2 * COEF
    weighted = (references.astype(jnp.float32) * inv_noise[None, :, None]).astype(jnp.bfloat16)
    weighted = weighted.reshape(O, G * row_width)
    block_of = jnp.arange(O, dtype=jnp.int32) // OB
    flat_rows = particles.reshape(N_DOM, P_DEV, G * row_width)
    owners = blocks.reshape(N_DOM, P_DEV, TOPB)

    def one_owner(running, packed):
        images, chosen = packed
        scores = jnp.dot(images, weighted.T, preferred_element_type=jnp.float32)
        allowed = jnp.any(chosen[:, :, None] == block_of[None, None, :], axis=1)
        masked = jnp.where(allowed, scores, -jnp.inf)
        highest = jnp.max(masked, axis=1, keepdims=True)
        weights = jnp.where(allowed, jnp.exp(masked - highest), 0.0)
        posterior = (weights / jnp.sum(weights, axis=1, keepdims=True)).astype(jnp.bfloat16)
        partial_value = jnp.dot(posterior.T, images, preferred_element_type=jnp.float32).astype(jnp.bfloat16)
        return running + partial_value.astype(jnp.float32), None

    slices, _ = lax.scan(one_owner, jnp.zeros((O, G * row_width), jnp.float32), (flat_rows, owners))
    pieces = slices.reshape(O, G, row_width)
    target = (destination * RD + row_index).T
    lower_part = (1.0 - fraction).T[:, :, None] * pieces
    upper_part = fraction.T[:, :, None] * pieces
    rows_total = RD * N_DOM * N_SLAB
    volume = jnp.zeros((rows_total + 1, row_width), jnp.float32)
    volume = volume.at[target].add(lower_part).at[target + 1].add(upper_part)[:rows_total]
    next_slab = volume.astype(jnp.bfloat16).reshape(N_DOM, N_SLAB, RD, row_width)
    next_slab = next_slab.transpose(0, 2, 1, 3).reshape(N_DOM * RD, N_SLAB * row_width)
    return volume, next_slab
```

```python
import jax
import jax.numpy as jnp
from jax import lax
from jax.sharding import PartitionSpec as P

OB = 128
RD = 256
CAP = 16


def send_slots(dests, devices):
    count = dests.shape[0]
    onehot = dests[:, None] == jnp.arange(devices, dtype=jnp.int32)[None, :]
    place = jnp.arange(count, dtype=jnp.int32)
    before = (place[None, :] < place[:, None]).astype(jnp.bfloat16)
    counts = jnp.dot(before, onehot.astype(jnp.bfloat16), preferred_element_type=jnp.float32)
    rank = jnp.sum(jnp.where(onehot, counts, 0.0), axis=1).astype(jnp.int32)
    return dests * CAP + rank


def received_slots(tables, dests, me):
    count = dests.shape[1]
    mask = dests == me
    place = jnp.arange(count, dtype=jnp.int32)
    before = (place[:, None] < place[None, :]).astype(jnp.bfloat16)
    rank = jnp.dot(mask.astype(jnp.bfloat16), before, preferred_element_type=jnp.float32)
    rank = jnp.where(mask, rank.astype(jnp.int32), -1)
    chosen = rank[:, None, :] == jnp.arange(CAP, dtype=jnp.int32)[None, :, None]
    found = [jnp.sum(jnp.where(chosen, t[:, None, :], 0), axis=2).reshape(-1) for t in tables]
    filled = jnp.any(chosen, axis=2).reshape(-1)
    return found, filled


def shards(particles, blocks, references, inv_noise, destination, row_index, fraction):
    particle_count, groups, row_width = particles.shape
    orients = references.shape[0]
    dom_size = lax.axis_size("dom")
    slab_size = lax.axis_size("slab")
    devices = dom_size * slab_size
    dom_pos = lax.axis_index("dom")
    slab_pos = lax.axis_index("slab")
    me = dom_pos * slab_size + slab_pos
    share = orients // dom_size
    weighted = (references.astype(jnp.float32) * inv_noise[None, :, None]).astype(jnp.bfloat16)
    partial_value = lax.dot_general(
        particles, weighted, (((1, 2), (1, 2)), ((), ())), preferred_element_type=jnp.float32
    )
    scores = lax.psum(partial_value, "slab")
    block_of = jnp.arange(orients, dtype=jnp.int32) // OB
    allowed = jnp.any(blocks[:, :, None] == block_of[None, None, :], axis=1)
    masked = jnp.where(allowed, scores, -jnp.inf)
    highest = jnp.max(masked, axis=1, keepdims=True)
    weights = jnp.where(allowed, jnp.exp(masked - highest), 0.0)
    posterior = (weights / jnp.sum(weights, axis=1, keepdims=True)).astype(jnp.bfloat16)
    slices = lax.dot_general(
        posterior,
        particles.reshape(particle_count, groups * row_width),
        (((0,), (0,)), ((), ())),
        preferred_element_type=jnp.float32,
    ).astype(jnp.bfloat16)
    mine = lax.psum_scatter(slices, "dom", scatter_dimension=0, tiled=True)
    pieces = mine.reshape(share * groups, row_width)

    my_dest = lax.dynamic_slice(
        destination, (slab_pos * groups, dom_pos * share), (groups, share)
    )
    slot = send_slots(my_dest.T.reshape(-1), devices)
    pack = jnp.arange(devices * CAP, dtype=jnp.int32)[:, None] == slot[None, :]
    packed = jnp.dot(
        pack.astype(jnp.bfloat16), pieces, preferred_element_type=jnp.float32
    ).astype(jnp.bfloat16)

    def by_source(table):
        table = table.reshape(slab_size, groups, dom_size, share).transpose(2, 0, 3, 1)
        return table.reshape(devices, share * groups)

    (row, part), filled = received_slots(
        (by_source(row_index), by_source(fraction)), by_source(destination), me
    )
    row = jnp.where(filled, row, -2)
    rows = jnp.arange(RD, dtype=jnp.int32)[:, None]
    insert = jnp.where(row[None, :] == rows, 1.0 - part[None, :], 0.0)
    insert = insert + jnp.where(row[None, :] + 1 == rows, part[None, :], 0.0)
    insert_high = insert.astype(jnp.bfloat16)
    insert_low = (insert - insert_high.astype(jnp.float32)).astype(jnp.bfloat16)

    got = lax.all_to_all(
        packed.reshape(devices, CAP, row_width), ("dom", "slab"), 0, 0, tiled=True
    ).reshape(devices * CAP, row_width)
    volume = jnp.dot(insert_high, got, preferred_element_type=jnp.float32)
    volume = volume + jnp.dot(insert_low, got, preferred_element_type=jnp.float32)
    next_slab = lax.all_gather(volume.astype(jnp.bfloat16), "dom", axis=0, tiled=True)
    return (volume, next_slab)


def solution(mesh):
    return jax.shard_map(
        shards,
        mesh=mesh,
        in_specs=(
            P("dom", "slab", None),
            P("dom", None),
            P(None, "slab", None),
            P("slab"),
            P(),
            P(),
            P(),
        ),
        out_specs=(P(("dom", "slab"), None), P(None, "slab")),
        check_vma=False,
    )
```

```python
import functools

import jax
import jax.numpy as jnp
from jax import lax
from jax.experimental import pallas as pl
from jax.experimental.pallas import tpu as pltpu
from jax.sharding import PartitionSpec as P

MESH = pl.DeviceIdType.MESH
OB = 128
RD = 256
CAP = 16
SIDE = 4
CHUNKS = 5
ROUTES = (("x", 1), ("x", -1), ("y", 1), ("y", -1))


class Torus:
    def __init__(self):
        dom = lax.axis_index("dom")
        self.slab = lax.axis_index("slab")
        self.at = {"y": lax.div(dom, SIDE), "x": lax.rem(dom, SIDE)}

    def neighbour(self, axis, step):
        at = dict(self.at)
        at[axis] = lax.rem(at[axis] + step + SIDE, SIDE)
        return (at["y"] * SIDE + at["x"], self.slab)


def other(axis):
    return "y" if axis == "x" else "x"


def sum_kernel(x_ref, post_ref, out_ref, images, partial, got1, got2, in_sem, send1, recv1, send2, recv2):
    torus = Torus()
    per_chunk = x_ref.shape[0] // (len(ROUTES) * CHUNKS)
    share = out_ref.shape[1]

    def fetch(q, i):
        first = (q * CHUNKS + i) * per_chunk
        return pltpu.make_async_copy(
            x_ref.at[pl.ds(first, per_chunk)], images.at[q, i], in_sem.at[q, i]
        )

    def block(q, stage, hop):
        axis, sign = ROUTES[q]
        axis = axis if stage == 1 else other(axis)
        return lax.rem(torus.at[axis] - sign * (1 + hop) + 2 * SIDE, SIDE)

    def hop1(q, hop, i):
        axis, sign = ROUTES[q]
        source = partial.at[q, i, block(q, 1, 0)] if hop == 0 else got1.at[q, hop - 1, i]
        return pltpu.make_async_remote_copy(
            src_ref=source,
            dst_ref=got1.at[q, hop, i],
            send_sem=send1.at[q, hop, i],
            recv_sem=recv1.at[q, hop, i],
            device_id=torus.neighbour(axis, sign),
            device_id_type=MESH,
        )

    def hop2(q, hop, i):
        axis, sign = ROUTES[q]
        source = got1.at[q, SIDE - 2, i, block(q, 2, 0)] if hop == 0 else got2.at[q, hop - 1, i]
        return pltpu.make_async_remote_copy(
            src_ref=source,
            dst_ref=got2.at[q, hop, i],
            send_sem=send2.at[q, hop, i],
            recv_sem=recv2.at[q, hop, i],
            device_id=torus.neighbour(other(axis), sign),
            device_id_type=MESH,
        )

    def added(a, b):
        return (a.astype(jnp.float32) + b.astype(jnp.float32)).astype(jnp.bfloat16)

    routes = range(len(ROUTES))
    for i in range(CHUNKS):
        for q in routes:
            fetch(q, i).start()
    barrier = pltpu.get_barrier_semaphore()
    for axis, sign in ROUTES:
        pl.semaphore_signal(
            barrier, inc=1, device_id=torus.neighbour(axis, sign), device_id_type=MESH
        )
    pl.semaphore_wait(barrier, len(ROUTES))

    @pl.loop(0, CHUNKS)
    def _(i):
        for q in routes:
            fetch(q, i).wait()
            for j in range(per_chunk):
                value = jnp.dot(
                    post_ref[...], images[q, i, j], preferred_element_type=jnp.float32
                ).astype(jnp.bfloat16)
                for yy in range(SIDE):
                    for xx in range(SIDE):
                        first, second = (xx, yy) if ROUTES[q][0] == "x" else (yy, xx)
                        begin = (yy * SIDE + xx) * share
                        partial[q, i, first, second, j] = value[begin : begin + share]
            hop1(q, 0, i).start()

    for hop in range(SIDE - 2):

        @pl.loop(0, CHUNKS)
        def _(i):
            for q in routes:
                hop1(q, hop, i).wait_recv()
                got1[q, hop, i] = added(got1[q, hop, i], partial[q, i, block(q, 1, hop + 1)])
                hop1(q, hop + 1, i).start()

    last = SIDE - 2

    @pl.loop(0, CHUNKS)
    def _(i):
        for q in routes:
            hop1(q, last, i).wait_recv()
            got1[q, last, i] = added(got1[q, last, i], partial[q, i, torus.at[ROUTES[q][0]]])
            hop2(q, 0, i).start()

    for hop in range(SIDE - 2):

        @pl.loop(0, CHUNKS)
        def _(i):
            for q in routes:
                hop2(q, hop, i).wait_recv()
                got2[q, hop, i] = added(got2[q, hop, i], got1[q, last, i, block(q, 2, hop + 1)])
                hop2(q, hop + 1, i).start()

    @pl.loop(0, CHUNKS)
    def _(i):
        for q in routes:
            hop2(q, last, i).wait_recv()
            mine = got1[q, last, i, torus.at[other(ROUTES[q][0])]]
            first = (q * CHUNKS + i) * per_chunk
            out_ref[pl.ds(first, per_chunk)] = added(got2[q, last, i], mine)

    @pl.loop(0, CHUNKS)
    def _(i):
        for q in routes:
            for hop in range(SIDE - 1):
                hop1(q, hop, i).wait_send()
                hop2(q, hop, i).wait_send()


def summed_slices(images, posterior, share):
    groups, particles, width = images.shape
    orients = posterior.shape[0]
    routes = len(ROUTES)
    per_chunk = groups // (routes * CHUNKS)
    hops = SIDE - 1
    piece = (per_chunk, share, width)
    sems = pltpu.SemaphoreType.DMA((routes, hops, CHUNKS))
    return pl.pallas_call(
        sum_kernel,
        out_shape=jax.ShapeDtypeStruct((groups, share, width), jnp.bfloat16),
        in_specs=[
            pl.BlockSpec(memory_space=pl.ANY),
            pl.BlockSpec(memory_space=pltpu.VMEM),
        ],
        out_specs=pl.BlockSpec(memory_space=pltpu.VMEM),
        scratch_shapes=[
            pltpu.VMEM((routes, CHUNKS, per_chunk, particles, width), jnp.bfloat16),
            pltpu.VMEM((routes, CHUNKS, SIDE, SIDE) + piece, jnp.bfloat16),
            pltpu.VMEM((routes, hops, CHUNKS, SIDE) + piece, jnp.bfloat16),
            pltpu.VMEM((routes, hops, CHUNKS) + piece, jnp.bfloat16),
            pltpu.SemaphoreType.DMA((routes, CHUNKS)),
            sems,
            sems,
            sems,
            sems,
        ],
        compiler_params=pltpu.CompilerParams(
            collective_id=0, has_side_effects=True, vmem_limit_bytes=48 * 1024 * 1024
        ),
        name="sum_slices",
    )(images, posterior)


def send_slots(dests, devices):
    count = dests.shape[0]
    onehot = dests[:, None] == jnp.arange(devices, dtype=jnp.int32)[None, :]
    place = jnp.arange(count, dtype=jnp.int32)
    before = (place[None, :] < place[:, None]).astype(jnp.bfloat16)
    counts = jnp.dot(before, onehot.astype(jnp.bfloat16), preferred_element_type=jnp.float32)
    rank = jnp.sum(jnp.where(onehot, counts, 0.0), axis=1).astype(jnp.int32)
    return dests * CAP + rank


def received_slots(tables, dests, me):
    count = dests.shape[1]
    mask = dests == me
    place = jnp.arange(count, dtype=jnp.int32)
    before = (place[:, None] < place[None, :]).astype(jnp.bfloat16)
    rank = jnp.dot(mask.astype(jnp.bfloat16), before, preferred_element_type=jnp.float32)
    rank = jnp.where(mask, rank.astype(jnp.int32), -1)
    chosen = rank[:, None, :] == jnp.arange(CAP, dtype=jnp.int32)[None, :, None]
    found = [jnp.sum(jnp.where(chosen, t[:, None, :], 0), axis=2).reshape(-1) for t in tables]
    filled = jnp.any(chosen, axis=2).reshape(-1)
    return found, filled


def shards(particles, blocks, references, inv_noise, destination, row_index, fraction):
    particle_count, groups, row_width = particles.shape
    orients = references.shape[0]
    dom_size = lax.axis_size("dom")
    slab_size = lax.axis_size("slab")
    devices = dom_size * slab_size
    dom_pos = lax.axis_index("dom")
    slab_pos = lax.axis_index("slab")
    me = dom_pos * slab_size + slab_pos
    share = orients // dom_size
    weighted = (references.astype(jnp.float32) * inv_noise[None, :, None]).astype(jnp.bfloat16)
    partial_value = lax.dot_general(
        weighted, particles, (((1, 2), (1, 2)), ((), ())), preferred_element_type=jnp.float32
    )
    scores = lax.psum(partial_value, "slab")
    block_of = jnp.arange(orients, dtype=jnp.int32) // OB
    allowed = jnp.any(blocks.T[:, None, :] == block_of[None, :, None], axis=0)
    masked = jnp.where(allowed, scores, -jnp.inf)
    highest = jnp.max(masked, axis=0, keepdims=True)
    weights = jnp.where(allowed, jnp.exp(masked - highest), 0.0)
    posterior = (weights / jnp.sum(weights, axis=0, keepdims=True)).astype(jnp.bfloat16)
    pieces = summed_slices(particles.transpose(1, 0, 2), posterior, share)
    pieces = pieces.reshape(groups * share, row_width)

    my_dest = lax.dynamic_slice(
        destination, (slab_pos * groups, dom_pos * share), (groups, share)
    )
    slot = send_slots(my_dest.reshape(-1), devices)
    pack = jnp.arange(devices * CAP, dtype=jnp.int32)[:, None] == slot[None, :]
    packed = jnp.dot(
        pack.astype(jnp.bfloat16), pieces, preferred_element_type=jnp.float32
    ).astype(jnp.bfloat16)

    def by_source(table):
        table = table.reshape(slab_size, groups, dom_size, share).transpose(2, 0, 1, 3)
        return table.reshape(devices, share * groups)

    (row, part), filled = received_slots(
        (by_source(row_index), by_source(fraction)), by_source(destination), me
    )
    row = jnp.where(filled, row, -2)
    rows = jnp.arange(RD, dtype=jnp.int32)[:, None]
    insert = jnp.where(row[None, :] == rows, 1.0 - part[None, :], 0.0)
    insert = insert + jnp.where(row[None, :] + 1 == rows, part[None, :], 0.0)
    insert_high = insert.astype(jnp.bfloat16)
    insert_low = (insert - insert_high.astype(jnp.float32)).astype(jnp.bfloat16)

    got = lax.all_to_all(
        packed.reshape(devices, CAP, row_width), ("dom", "slab"), 0, 0, tiled=True
    ).reshape(devices * CAP, row_width)
    volume = jnp.dot(insert_high, got, preferred_element_type=jnp.float32)
    volume = volume + jnp.dot(insert_low, got, preferred_element_type=jnp.float32)
    next_slab = lax.all_gather(volume.astype(jnp.bfloat16), "dom", axis=0, tiled=True)
    return (volume, next_slab)


def solution(mesh):
    return jax.shard_map(
        shards,
        mesh=mesh,
        in_specs=(
            P("dom", "slab", None),
            P("dom", None),
            P(None, "slab", None),
            P("slab"),
            P(),
            P(),
            P(),
        ),
        out_specs=(P(("dom", "slab"), None), P(None, "slab")),
        check_vma=False,
    )
```

```python
import functools

import jax
import jax.numpy as jnp
from jax import lax
from jax.experimental import pallas as pl
from jax.experimental.pallas import tpu as pltpu
from jax.sharding import PartitionSpec as P

MESH = pl.DeviceIdType.MESH
OB = 128
RD = 256
CAP = 16
SIDE = 4
CHUNKS = 5
ROUTES = (("x", 1), ("x", -1), ("y", 1), ("y", -1))


class Torus:
    def __init__(self):
        dom = lax.axis_index("dom")
        self.slab = lax.axis_index("slab")
        self.at = {"y": lax.div(dom, SIDE), "x": lax.rem(dom, SIDE)}

    def neighbour(self, axis, step):
        at = dict(self.at)
        at[axis] = lax.rem(at[axis] + step + SIDE, SIDE)
        return (at["y"] * SIDE + at["x"], self.slab)


def other(axis):
    return "y" if axis == "x" else "x"


def sum_kernel(x_ref, post_ref, out_ref, images, partial, got1, got2, in_sem, send1, recv1, send2, recv2):
    torus = Torus()
    per_chunk = x_ref.shape[0] // (len(ROUTES) * CHUNKS)
    share = out_ref.shape[1]

    def fetch(q, i):
        first = (q * CHUNKS + i) * per_chunk
        return pltpu.make_async_copy(
            x_ref.at[pl.ds(first, per_chunk)], images.at[q, i], in_sem.at[q, i]
        )

    def block(q, stage, hop):
        axis, sign = ROUTES[q]
        axis = axis if stage == 1 else other(axis)
        return lax.rem(torus.at[axis] - sign * (1 + hop) + 2 * SIDE, SIDE)

    def hop1(q, hop, i):
        axis, sign = ROUTES[q]
        source = partial.at[q, i, block(q, 1, 0)] if hop == 0 else got1.at[q, hop - 1, i]
        return pltpu.make_async_remote_copy(
            src_ref=source,
            dst_ref=got1.at[q, hop, i],
            send_sem=send1.at[q, hop, i],
            recv_sem=recv1.at[q, hop, i],
            device_id=torus.neighbour(axis, sign),
            device_id_type=MESH,
        )

    def hop2(q, hop, i):
        axis, sign = ROUTES[q]
        source = got1.at[q, SIDE - 2, i, block(q, 2, 0)] if hop == 0 else got2.at[q, hop - 1, i]
        return pltpu.make_async_remote_copy(
            src_ref=source,
            dst_ref=got2.at[q, hop, i],
            send_sem=send2.at[q, hop, i],
            recv_sem=recv2.at[q, hop, i],
            device_id=torus.neighbour(other(axis), sign),
            device_id_type=MESH,
        )

    def added(a, b):
        return (a.astype(jnp.float32) + b.astype(jnp.float32)).astype(jnp.bfloat16)

    routes = range(len(ROUTES))
    for i in range(CHUNKS):
        for q in routes:
            fetch(q, i).start()
    barrier = pltpu.get_barrier_semaphore()
    for axis, sign in ROUTES:
        pl.semaphore_signal(
            barrier, inc=1, device_id=torus.neighbour(axis, sign), device_id_type=MESH
        )
    pl.semaphore_wait(barrier, len(ROUTES))

    @pl.loop(0, CHUNKS)
    def _(i):
        for q in routes:
            fetch(q, i).wait()
            for j in range(per_chunk):
                value = jnp.dot(
                    post_ref[...], images[q, i, j], preferred_element_type=jnp.float32
                ).astype(jnp.bfloat16)
                for yy in range(SIDE):
                    for xx in range(SIDE):
                        first, second = (xx, yy) if ROUTES[q][0] == "x" else (yy, xx)
                        begin = (yy * SIDE + xx) * share
                        partial[q, i, first, second, j] = value[begin : begin + share]
            hop1(q, 0, i).start()

    for hop in range(SIDE - 2):

        @pl.loop(0, CHUNKS)
        def _(i):
            for q in routes:
                hop1(q, hop, i).wait_recv()
                got1[q, hop, i] = added(got1[q, hop, i], partial[q, i, block(q, 1, hop + 1)])
                hop1(q, hop + 1, i).start()

    last = SIDE - 2

    @pl.loop(0, CHUNKS)
    def _(i):
        for q in routes:
            hop1(q, last, i).wait_recv()
            got1[q, last, i] = added(got1[q, last, i], partial[q, i, torus.at[ROUTES[q][0]]])
            hop2(q, 0, i).start()

    for hop in range(SIDE - 2):

        @pl.loop(0, CHUNKS)
        def _(i):
            for q in routes:
                hop2(q, hop, i).wait_recv()
                got2[q, hop, i] = added(got2[q, hop, i], got1[q, last, i, block(q, 2, hop + 1)])
                hop2(q, hop + 1, i).start()

    @pl.loop(0, CHUNKS)
    def _(i):
        for q in routes:
            hop2(q, last, i).wait_recv()
            mine = got1[q, last, i, torus.at[other(ROUTES[q][0])]]
            first = (q * CHUNKS + i) * per_chunk
            out_ref[pl.ds(first, per_chunk)] = added(got2[q, last, i], mine)

    @pl.loop(0, CHUNKS)
    def _(i):
        for q in routes:
            for hop in range(SIDE - 1):
                hop1(q, hop, i).wait_send()
                hop2(q, hop, i).wait_send()


def summed_slices(images, posterior, share):
    groups, particles, width = images.shape
    orients = posterior.shape[0]
    routes = len(ROUTES)
    per_chunk = groups // (routes * CHUNKS)
    hops = SIDE - 1
    piece = (per_chunk, share, width)
    sems = pltpu.SemaphoreType.DMA((routes, hops, CHUNKS))
    return pl.pallas_call(
        sum_kernel,
        out_shape=jax.ShapeDtypeStruct((groups, share, width), jnp.bfloat16),
        in_specs=[
            pl.BlockSpec(memory_space=pl.ANY),
            pl.BlockSpec(memory_space=pltpu.VMEM),
        ],
        out_specs=pl.BlockSpec(memory_space=pltpu.VMEM),
        scratch_shapes=[
            pltpu.VMEM((routes, CHUNKS, per_chunk, particles, width), jnp.bfloat16),
            pltpu.VMEM((routes, CHUNKS, SIDE, SIDE) + piece, jnp.bfloat16),
            pltpu.VMEM((routes, hops, CHUNKS, SIDE) + piece, jnp.bfloat16),
            pltpu.VMEM((routes, hops, CHUNKS) + piece, jnp.bfloat16),
            pltpu.SemaphoreType.DMA((routes, CHUNKS)),
            sems,
            sems,
            sems,
            sems,
        ],
        compiler_params=pltpu.CompilerParams(
            collective_id=0, has_side_effects=True, vmem_limit_bytes=48 * 1024 * 1024
        ),
        name="sum_slices",
    )(images, posterior)


def exchange_kernel(
    pieces_ref, slot_ref, row_ref, part_ref, volume_ref, next_ref,
    packed, got, insert, own_sem, out_sem, in_sem, send_a, recv_a, send_b, recv_b,
):
    torus = Torus()
    slabs = lax.axis_size("slab")
    devices = lax.axis_size("dom") * slabs
    me = (torus.at["y"] * SIDE + torus.at["x"]) * slabs + torus.slab
    width = pieces_ref.shape[1]
    routes = range(len(ROUTES))

    def device(number):
        return (lax.div(number, slabs), lax.rem(number, slabs))

    barrier = pltpu.get_barrier_semaphore()

    @pl.loop(1, devices)
    def _(k):
        to = lax.rem(me + k, devices)
        pl.semaphore_signal(barrier, inc=1, device_id=device(to), device_id_type=MESH)

    block = RD
    owners = block // CAP
    numbers = lax.broadcasted_iota(jnp.int32, (block, pieces_ref.shape[0]), 0)
    for b in range(devices // owners):
        pick = (numbers + b * block == slot_ref[...]).astype(jnp.float32).astype(jnp.bfloat16)
        value = jnp.dot(pick, pieces_ref[...], preferred_element_type=jnp.float32)
        packed[b * owners : (b + 1) * owners] = value.astype(jnp.bfloat16).reshape(owners, CAP, width)
    pl.semaphore_wait(barrier, devices - 1)

    @pl.loop(1, devices)
    def _(k):
        to = lax.rem(me + k, devices)
        pltpu.make_async_remote_copy(
            src_ref=packed.at[to],
            dst_ref=got.at[me],
            send_sem=out_sem,
            recv_sem=in_sem,
            device_id=device(to),
            device_id_type=MESH,
        ).start()

    own = pltpu.make_async_copy(packed.at[me], got.at[me], own_sem)
    own.start()
    lanes = row_ref.shape[1]
    rows = lax.broadcasted_iota(jnp.int32, (RD, lanes), 0)
    for b in range(row_ref.shape[0]):
        row = row_ref[b : b + 1, :]
        part = part_ref[b : b + 1, :]
        weight = jnp.where(rows == row, 1.0 - part, 0.0) + jnp.where(rows == row + 1, part, 0.0)
        high = weight.astype(jnp.bfloat16)
        insert[0, :, b * lanes : (b + 1) * lanes] = high
        insert[1, :, b * lanes : (b + 1) * lanes] = (weight - high.astype(jnp.float32)).astype(jnp.bfloat16)
    own.wait()
    others = got.at[pl.ds(0, devices - 1)]
    pltpu.make_async_copy(others, others, in_sem).wait()
    pieces = got[...].reshape(devices * CAP, width)
    volume = jnp.dot(insert[0], pieces, preferred_element_type=jnp.float32)
    volume = volume + jnp.dot(insert[1], pieces, preferred_element_type=jnp.float32)
    volume_ref[...] = volume
    part_rows = RD // len(ROUTES)
    for q in routes:
        next_ref[torus.at["y"], torus.at["x"], q] = volume[
            q * part_rows : (q + 1) * part_rows
        ].astype(jnp.bfloat16)

    def origin(q, stage, hop):
        axis, sign = ROUTES[q]
        axis = axis if stage == 1 else other(axis)
        return lax.rem(torus.at[axis] - sign * hop + 2 * SIDE, SIDE)

    def place(q, first, second):
        y, x = (second, first) if ROUTES[q][0] == "x" else (first, second)
        return next_ref.at[y, x, q]

    def hop_a(q, hop):
        axis, sign = ROUTES[q]
        spot = place(q, origin(q, 1, hop), torus.at[other(axis)])
        return pltpu.make_async_remote_copy(
            src_ref=spot,
            dst_ref=spot,
            send_sem=send_a.at[q, hop],
            recv_sem=recv_a.at[q, hop],
            device_id=torus.neighbour(axis, sign),
            device_id_type=MESH,
        )

    def hop_b(q, hop, j):
        axis, sign = ROUTES[q]
        spot = place(q, origin(q, 1, j), origin(q, 2, hop))
        return pltpu.make_async_remote_copy(
            src_ref=spot,
            dst_ref=spot,
            send_sem=send_b.at[q, hop, j],
            recv_sem=recv_b.at[q, hop, j],
            device_id=torus.neighbour(other(axis), sign),
            device_id_type=MESH,
        )

    for q in routes:
        hop_a(q, 0).start()
        hop_b(q, 0, 0).start()
    for step in range(1, 2 * SIDE - 1):
        for q in routes:
            if step < SIDE:
                hop_a(q, step - 1).wait_recv()
                if step < SIDE - 1:
                    hop_a(q, step).start()
                hop_b(q, 0, step).start()
        for q in routes:
            for hop in range(SIDE - 1):
                j = step - 1 - hop
                if 0 <= j < SIDE:
                    hop_b(q, hop, j).wait_recv()
                    if hop < SIDE - 2:
                        hop_b(q, hop + 1, j).start()
    for q in routes:
        for hop in range(SIDE - 1):
            hop_a(q, hop).wait_send()
            for j in range(SIDE):
                hop_b(q, hop, j).wait_send()
    sent = packed.at[pl.ds(0, devices - 1)]
    pltpu.make_async_copy(sent, sent, out_sem).wait()


def exchanged(pieces, slot, row, part, devices):
    width = pieces.shape[1]
    routes = len(ROUTES)
    hops = SIDE - 1
    part_rows = RD // routes
    vmem = pl.BlockSpec(memory_space=pltpu.VMEM)
    sems_a = pltpu.SemaphoreType.DMA((routes, hops))
    sems_b = pltpu.SemaphoreType.DMA((routes, hops, SIDE))
    return pl.pallas_call(
        exchange_kernel,
        out_shape=(
            jax.ShapeDtypeStruct((RD, width), jnp.float32),
            jax.ShapeDtypeStruct((SIDE, SIDE, routes, part_rows, width), jnp.bfloat16),
        ),
        in_specs=[vmem] * 4,
        out_specs=(vmem, vmem),
        scratch_shapes=[
            pltpu.VMEM((devices, CAP, width), jnp.bfloat16),
            pltpu.VMEM((devices, CAP, width), jnp.bfloat16),
            pltpu.VMEM((2, RD, devices * CAP), jnp.bfloat16),
            pltpu.SemaphoreType.DMA,
            pltpu.SemaphoreType.DMA,
            pltpu.SemaphoreType.DMA,
            sems_a,
            sems_a,
            sems_b,
            sems_b,
        ],
        compiler_params=pltpu.CompilerParams(
            collective_id=1, has_side_effects=True, vmem_limit_bytes=32 * 1024 * 1024
        ),
        name="exchange_pieces",
    )(pieces, slot, row, part)


def send_slots(dests, devices):
    count = dests.shape[0]
    onehot = dests[:, None] == jnp.arange(devices, dtype=jnp.int32)[None, :]
    place = jnp.arange(count, dtype=jnp.int32)
    before = (place[None, :] < place[:, None]).astype(jnp.bfloat16)
    counts = jnp.dot(before, onehot.astype(jnp.bfloat16), preferred_element_type=jnp.float32)
    rank = jnp.sum(jnp.where(onehot, counts, 0.0), axis=1).astype(jnp.int32)
    return dests * CAP + rank


def received_slots(tables, dests, me):
    count = dests.shape[1]
    mask = dests == me
    place = jnp.arange(count, dtype=jnp.int32)
    before = (place[:, None] < place[None, :]).astype(jnp.bfloat16)
    rank = jnp.dot(mask.astype(jnp.bfloat16), before, preferred_element_type=jnp.float32)
    rank = jnp.where(mask, rank.astype(jnp.int32), -1)
    chosen = rank[:, None, :] == jnp.arange(CAP, dtype=jnp.int32)[None, :, None]
    found = [jnp.sum(jnp.where(chosen, t[:, None, :], 0), axis=2).reshape(-1) for t in tables]
    filled = jnp.any(chosen, axis=2).reshape(-1)
    return found, filled


def shards(particles, blocks, references, inv_noise, destination, row_index, fraction):
    particle_count, groups, row_width = particles.shape
    orients = references.shape[0]
    dom_size = lax.axis_size("dom")
    slab_size = lax.axis_size("slab")
    devices = dom_size * slab_size
    dom_pos = lax.axis_index("dom")
    slab_pos = lax.axis_index("slab")
    me = dom_pos * slab_size + slab_pos
    share = orients // dom_size
    weighted = (references.astype(jnp.float32) * inv_noise[None, :, None]).astype(jnp.bfloat16)
    partial_value = lax.dot_general(
        weighted, particles, (((1, 2), (1, 2)), ((), ())), preferred_element_type=jnp.float32
    )
    scores = lax.psum(partial_value, "slab")
    block_of = jnp.arange(orients, dtype=jnp.int32) // OB
    allowed = jnp.any(blocks.T[:, None, :] == block_of[None, :, None], axis=0)
    masked = jnp.where(allowed, scores, -jnp.inf)
    highest = jnp.max(masked, axis=0, keepdims=True)
    weights = jnp.where(allowed, jnp.exp(masked - highest), 0.0)
    posterior = (weights / jnp.sum(weights, axis=0, keepdims=True)).astype(jnp.bfloat16)
    pieces = summed_slices(particles.transpose(1, 0, 2), posterior, share)
    pieces = pieces.reshape(groups * share, row_width)

    my_dest = lax.dynamic_slice(
        destination, (slab_pos * groups, dom_pos * share), (groups, share)
    )
    slot = send_slots(my_dest.reshape(-1), devices)
    def by_source(table):
        table = table.reshape(slab_size, groups, dom_size, share).transpose(2, 0, 1, 3)
        return table.reshape(devices, share * groups)

    (row, part), filled = received_slots(
        (by_source(row_index), by_source(fraction)), by_source(destination), me
    )
    row = jnp.where(filled, row, -2)
    volume, next_slab = exchanged(
        pieces,
        slot[None, :],
        row.reshape(dom_size, -1),
        part.reshape(dom_size, -1),
        devices,
    )
    next_slab = next_slab.reshape(dom_size * RD, row_width)
    return (volume, next_slab)


def solution(mesh):
    return jax.shard_map(
        shards,
        mesh=mesh,
        in_specs=(
            P("dom", "slab", None),
            P("dom", None),
            P(None, "slab", None),
            P("slab"),
            P(),
            P(),
            P(),
        ),
        out_specs=(P(("dom", "slab"), None), P(None, "slab")),
        check_vma=False,
    )
```

```python
import functools

import jax
import jax.numpy as jnp
from jax import lax
from jax.experimental import pallas as pl
from jax.experimental.pallas import tpu as pltpu
from jax.sharding import PartitionSpec as P

MESH = pl.DeviceIdType.MESH
OB = 128
RD = 256
CAP = 16
SIDE = 4
CHUNKS = 5
ROUTES = (("x", 1), ("x", -1), ("y", 1), ("y", -1))


class Torus:
    def __init__(self):
        dom = lax.axis_index("dom")
        self.slab = lax.axis_index("slab")
        self.at = {"y": lax.div(dom, SIDE), "x": lax.rem(dom, SIDE)}

    def neighbour(self, axis, step):
        at = dict(self.at)
        at[axis] = lax.rem(at[axis] + step + SIDE, SIDE)
        return (at["y"] * SIDE + at["x"], self.slab)


def other(axis):
    return "y" if axis == "x" else "x"


def sum_kernel(x_ref, post_ref, out_ref, images, partial, got1, got2, in_sem, send1, recv1, send2, recv2):
    torus = Torus()
    per_chunk = x_ref.shape[0] // (len(ROUTES) * CHUNKS)
    share = out_ref.shape[1]

    def fetch(q, i):
        first = (q * CHUNKS + i) * per_chunk
        return pltpu.make_async_copy(
            x_ref.at[pl.ds(first, per_chunk)], images.at[q, i], in_sem.at[q, i]
        )

    def block(q, stage, hop):
        axis, sign = ROUTES[q]
        axis = axis if stage == 1 else other(axis)
        return lax.rem(torus.at[axis] - sign * (1 + hop) + 2 * SIDE, SIDE)

    def hop1(q, hop, i):
        axis, sign = ROUTES[q]
        source = partial.at[q, i, block(q, 1, 0)] if hop == 0 else got1.at[q, hop - 1, i]
        return pltpu.make_async_remote_copy(
            src_ref=source,
            dst_ref=got1.at[q, hop, i],
            send_sem=send1.at[q, hop, i],
            recv_sem=recv1.at[q, hop, i],
            device_id=torus.neighbour(axis, sign),
            device_id_type=MESH,
        )

    def hop2(q, hop, i):
        axis, sign = ROUTES[q]
        source = got1.at[q, SIDE - 2, i, block(q, 2, 0)] if hop == 0 else got2.at[q, hop - 1, i]
        return pltpu.make_async_remote_copy(
            src_ref=source,
            dst_ref=got2.at[q, hop, i],
            send_sem=send2.at[q, hop, i],
            recv_sem=recv2.at[q, hop, i],
            device_id=torus.neighbour(other(axis), sign),
            device_id_type=MESH,
        )

    def added(a, b):
        return (a.astype(jnp.float32) + b.astype(jnp.float32)).astype(jnp.bfloat16)

    routes = range(len(ROUTES))
    for i in range(CHUNKS):
        for q in routes:
            fetch(q, i).start()
    barrier = pltpu.get_barrier_semaphore()
    for axis, sign in ROUTES:
        pl.semaphore_signal(
            barrier, inc=1, device_id=torus.neighbour(axis, sign), device_id_type=MESH
        )
    pl.semaphore_wait(barrier, len(ROUTES))

    @pl.loop(0, CHUNKS)
    def _(i):
        for q in routes:
            fetch(q, i).wait()
            for j in range(per_chunk):
                value = jnp.dot(
                    post_ref[...], images[q, i, j], preferred_element_type=jnp.float32
                ).astype(jnp.bfloat16)
                for yy in range(SIDE):
                    for xx in range(SIDE):
                        first, second = (xx, yy) if ROUTES[q][0] == "x" else (yy, xx)
                        begin = (yy * SIDE + xx) * share
                        partial[q, i, first, second, j] = value[begin : begin + share]
            hop1(q, 0, i).start()

    for hop in range(SIDE - 2):

        @pl.loop(0, CHUNKS)
        def _(i):
            for q in routes:
                hop1(q, hop, i).wait_recv()
                got1[q, hop, i] = added(got1[q, hop, i], partial[q, i, block(q, 1, hop + 1)])
                hop1(q, hop + 1, i).start()

    last = SIDE - 2

    @pl.loop(0, CHUNKS)
    def _(i):
        for q in routes:
            hop1(q, last, i).wait_recv()
            got1[q, last, i] = added(got1[q, last, i], partial[q, i, torus.at[ROUTES[q][0]]])
            hop2(q, 0, i).start()

    for hop in range(SIDE - 2):

        @pl.loop(0, CHUNKS)
        def _(i):
            for q in routes:
                hop2(q, hop, i).wait_recv()
                got2[q, hop, i] = added(got2[q, hop, i], got1[q, last, i, block(q, 2, hop + 1)])
                hop2(q, hop + 1, i).start()

    @pl.loop(0, CHUNKS)
    def _(i):
        for q in routes:
            hop2(q, last, i).wait_recv()
            mine = got1[q, last, i, torus.at[other(ROUTES[q][0])]]
            first = (q * CHUNKS + i) * per_chunk
            out_ref[pl.ds(first, per_chunk)] = added(got2[q, last, i], mine)

    @pl.loop(0, CHUNKS)
    def _(i):
        for q in routes:
            for hop in range(SIDE - 1):
                hop1(q, hop, i).wait_send()
                hop2(q, hop, i).wait_send()


def summed_slices(images, posterior, share):
    groups, particles, width = images.shape
    orients = posterior.shape[0]
    routes = len(ROUTES)
    per_chunk = groups // (routes * CHUNKS)
    hops = SIDE - 1
    piece = (per_chunk, share, width)
    sems = pltpu.SemaphoreType.DMA((routes, hops, CHUNKS))
    return pl.pallas_call(
        sum_kernel,
        out_shape=jax.ShapeDtypeStruct((groups, share, width), jnp.bfloat16),
        in_specs=[
            pl.BlockSpec(memory_space=pl.ANY),
            pl.BlockSpec(memory_space=pltpu.VMEM),
        ],
        out_specs=pl.BlockSpec(memory_space=pltpu.VMEM),
        scratch_shapes=[
            pltpu.VMEM((routes, CHUNKS, per_chunk, particles, width), jnp.bfloat16),
            pltpu.VMEM((routes, CHUNKS, SIDE, SIDE) + piece, jnp.bfloat16),
            pltpu.VMEM((routes, hops, CHUNKS, SIDE) + piece, jnp.bfloat16),
            pltpu.VMEM((routes, hops, CHUNKS) + piece, jnp.bfloat16),
            pltpu.SemaphoreType.DMA((routes, CHUNKS)),
            sems,
            sems,
            sems,
            sems,
        ],
        compiler_params=pltpu.CompilerParams(
            collective_id=0, has_side_effects=True, vmem_limit_bytes=48 * 1024 * 1024
        ),
        name="sum_slices",
    )(images, posterior)


def slot_tables(dest_ref, row_ref, part_ref, me, counts, rows_at, parts_at, row_out, part_out):
    slabs = lax.axis_size("slab")
    orients = dest_ref.shape[1]
    groups = dest_ref.shape[0] // slabs
    doms = row_out.shape[0]
    shift = (orients // doms).bit_length() - 1
    here = lax.broadcasted_iota(jnp.int32, (orients, orients), 0)
    there = lax.broadcasted_iota(jnp.int32, (orients, orients), 1)
    same = lax.shift_right_logical(here, shift) == lax.shift_right_logical(there, shift)
    share = same.astype(jnp.float32).astype(jnp.bfloat16)
    before = jnp.where(same & (here < there), 1.0, 0.0).astype(jnp.bfloat16)
    mask = (dest_ref[...] == me).astype(jnp.float32).astype(jnp.bfloat16)
    counts[0] = jnp.dot(mask, before, preferred_element_type=jnp.float32)
    counts[1] = jnp.dot(mask, share, preferred_element_type=jnp.float32)
    lower = lax.broadcasted_iota(jnp.int32, (groups, groups), 0) > lax.broadcasted_iota(
        jnp.int32, (groups, groups), 1
    )
    lower = lower.astype(jnp.float32).astype(jnp.bfloat16)

    @pl.loop(0, slabs)
    def _(s):
        span = pl.ds(pl.multiple_of(s * groups, groups), groups)
        above = jnp.dot(
            lower, counts[1, span].astype(jnp.bfloat16), preferred_element_type=jnp.float32
        )
        rank = jnp.where(dest_ref[span] == me, counts[0, span] + above, -1.0)
        row = row_ref[span].astype(jnp.float32) + 1.0
        part = part_ref[span]
        found_rows = []
        found_parts = []
        for j in range(CAP):
            chosen = rank == j
            found_rows.append(jnp.sum(jnp.where(chosen, row, 0.0), axis=0, keepdims=True))
            found_parts.append(jnp.sum(jnp.where(chosen, part, 0.0), axis=0, keepdims=True))
        slots = pl.ds(pl.multiple_of(s * CAP, CAP), CAP)
        rows_at[slots] = jnp.concatenate(found_rows, axis=0)
        parts_at[slots] = jnp.concatenate(found_parts, axis=0)

    owner = lax.shift_right_logical(lax.broadcasted_iota(jnp.int32, (doms, orients), 1), shift)
    gather = (owner == lax.broadcasted_iota(jnp.int32, (doms, orients), 0)).astype(jnp.float32)
    over_lanes = (((1,), (1,)), ((), ()))
    for found, out in ((rows_at, row_out), (parts_at, part_out)):
        out[...] = lax.dot_general(
            gather, found[...], over_lanes,
            precision=lax.Precision.HIGHEST, preferred_element_type=jnp.float32,
        )
    row_out[...] = row_out[...] - 1.0


def posterior_kernel(
    scores_ref, blocks_ref, dest_ref, row_ref, part_ref, post_ref, row_out, part_out,
    mine, from_mate, total, from_chips, found, counts, rows_at, parts_at,
    mate_send, mate_recv, chip_send, chip_recv, back_send, back_recv, last_send, last_recv,
):
    dom = lax.axis_index("dom")
    slab = lax.axis_index("slab")
    slabs = lax.axis_size("slab")
    chips = slabs // 2
    chip = lax.div(slab, 2)
    core = lax.rem(slab, 2)
    mate = (dom, 2 * chip + 1 - core)
    me = dom * slabs + slab
    count = mine.shape[2]

    def peer(step):
        return (dom, 2 * lax.rem(chip + step, chips) + core)

    barrier = pltpu.get_barrier_semaphore()
    pl.semaphore_signal(barrier, inc=1, device_id=mate, device_id_type=MESH)
    for step in range(1, chips):
        pl.semaphore_signal(barrier, inc=1, device_id=peer(step), device_id_type=MESH)

    def picked(span, which):
        chosen = blocks_ref[span, which : which + 1]
        value = scores_ref[span, 0:OB]
        for b in range(1, scores_ref.shape[1] // OB):
            value = jnp.where(chosen == b, scores_ref[span, b * OB : (b + 1) * OB], value)
        return value

    for s in range(slabs):
        span = pl.ds(s * count, count)
        for which in range(2):
            mine[s % 2, s // 2, :, which * OB : (which + 1) * OB] = picked(span, which)
    pl.semaphore_wait(barrier, chips)
    to_mate = pltpu.make_async_remote_copy(
        src_ref=mine.at[1 - core],
        dst_ref=from_mate,
        send_sem=mate_send,
        recv_sem=mate_recv,
        device_id=mate,
        device_id_type=MESH,
    )
    to_mate.start()
    to_mate.wait_recv()
    total[...] = mine[core] + from_mate[...]

    def to_chip(step):
        return pltpu.make_async_remote_copy(
            src_ref=total.at[lax.rem(chip + step, chips)],
            dst_ref=from_chips.at[step - 1],
            send_sem=chip_send.at[step - 1],
            recv_sem=chip_recv.at[step - 1],
            device_id=peer(step),
            device_id_type=MESH,
        )

    for step in range(1, chips):
        to_chip(step).start()
    slot_tables(dest_ref, row_ref, part_ref, me, counts, rows_at, parts_at, row_out, part_out)
    for step in range(1, chips):
        to_chip(step).wait_recv()
    scores = total[chip]
    for step in range(1, chips):
        scores = scores + from_chips[step - 1]
    weights = jnp.exp(scores - jnp.max(scores, axis=1, keepdims=True))
    found[chip, core] = (weights / jnp.sum(weights, axis=1, keepdims=True)).astype(jnp.bfloat16)

    def back(step):
        return pltpu.make_async_remote_copy(
            src_ref=found.at[chip, core],
            dst_ref=found.at[chip, core],
            send_sem=back_send.at[step - 1],
            recv_sem=back_recv.at[step - 1],
            device_id=peer(step),
            device_id_type=MESH,
        )

    for step in range(1, chips):
        back(step).start()
    for step in range(1, chips):
        back(step).wait_recv()
    last = pltpu.make_async_remote_copy(
        src_ref=found.at[:, core],
        dst_ref=found.at[:, core],
        send_sem=last_send,
        recv_sem=last_recv,
        device_id=mate,
        device_id_type=MESH,
    )
    last.start()
    last.wait_recv()
    everyone = found[...].astype(jnp.float32).reshape(slabs * count, 2 * OB)
    first, second = blocks_ref[:, 0:1], blocks_ref[:, 1:2]
    for b in range(scores_ref.shape[1] // OB):
        value = jnp.where(first == b, everyone[:, :OB], 0.0)
        value = jnp.where(second == b, everyone[:, OB:], value)
        post_ref[b * OB : (b + 1) * OB, :] = value.T.astype(jnp.bfloat16)
    to_mate.wait_send()
    last.wait_send()
    for step in range(1, chips):
        to_chip(step).wait_send()
        back(step).wait_send()


def posteriors(scores, blocks, destination, row_index, fraction, doms, slabs):
    particles, orients = scores.shape
    chips = slabs // 2
    count = particles // slabs
    vmem = pl.BlockSpec(memory_space=pltpu.VMEM)
    table = jax.ShapeDtypeStruct((doms, slabs * CAP), jnp.float32)
    dma = pltpu.SemaphoreType.DMA
    return pl.pallas_call(
        posterior_kernel,
        out_shape=(jax.ShapeDtypeStruct((orients, particles), jnp.bfloat16), table, table),
        in_specs=[vmem] * 5,
        out_specs=(vmem,) * 3,
        scratch_shapes=[
            pltpu.VMEM((2, chips, count, 2 * OB), jnp.float32),
            pltpu.VMEM((chips, count, 2 * OB), jnp.float32),
            pltpu.VMEM((chips, count, 2 * OB), jnp.float32),
            pltpu.VMEM((chips - 1, count, 2 * OB), jnp.float32),
            pltpu.VMEM((chips, 2, count, 2 * OB), jnp.bfloat16),
            pltpu.VMEM((2,) + destination.shape, jnp.float32),
            pltpu.VMEM((slabs * CAP, orients), jnp.float32),
            pltpu.VMEM((slabs * CAP, orients), jnp.float32),
            dma,
            dma,
            dma((chips - 1,)),
            dma((chips - 1,)),
            dma((chips - 1,)),
            dma((chips - 1,)),
            dma,
            dma,
        ],
        compiler_params=pltpu.CompilerParams(
            collective_id=2, has_side_effects=True, vmem_limit_bytes=32 * 1024 * 1024
        ),
        name="posteriors",
    )(scores, blocks, destination, row_index, fraction)


def exchange_kernel(
    pieces_ref, slot_ref, row_ref, part_ref, volume_ref, next_ref,
    packed, got, insert, own_sem, out_sem, in_sem, send_a, recv_a, send_b, recv_b,
):
    torus = Torus()
    slabs = lax.axis_size("slab")
    devices = lax.axis_size("dom") * slabs
    me = (torus.at["y"] * SIDE + torus.at["x"]) * slabs + torus.slab
    width = pieces_ref.shape[1]
    routes = range(len(ROUTES))

    def device(number):
        return (lax.div(number, slabs), lax.rem(number, slabs))

    barrier = pltpu.get_barrier_semaphore()

    @pl.loop(1, devices)
    def _(k):
        to = lax.rem(me + k, devices)
        pl.semaphore_signal(barrier, inc=1, device_id=device(to), device_id_type=MESH)

    block = RD
    owners = block // CAP
    numbers = lax.broadcasted_iota(jnp.int32, (block, pieces_ref.shape[0]), 0)
    for b in range(devices // owners):
        pick = (numbers + b * block == slot_ref[...]).astype(jnp.float32).astype(jnp.bfloat16)
        value = jnp.dot(pick, pieces_ref[...], preferred_element_type=jnp.float32)
        packed[b * owners : (b + 1) * owners] = value.astype(jnp.bfloat16).reshape(owners, CAP, width)
    pl.semaphore_wait(barrier, devices - 1)

    @pl.loop(1, devices)
    def _(k):
        to = lax.rem(me + k, devices)
        pltpu.make_async_remote_copy(
            src_ref=packed.at[to],
            dst_ref=got.at[me],
            send_sem=out_sem,
            recv_sem=in_sem,
            device_id=device(to),
            device_id_type=MESH,
        ).start()

    own = pltpu.make_async_copy(packed.at[me], got.at[me], own_sem)
    own.start()
    lanes = row_ref.shape[1]
    rows = lax.broadcasted_iota(jnp.int32, (RD, lanes), 0).astype(jnp.float32)
    for b in range(row_ref.shape[0]):
        row = row_ref[b : b + 1, :]
        part = part_ref[b : b + 1, :]
        weight = jnp.where(rows == row, 1.0 - part, 0.0) + jnp.where(rows == row + 1, part, 0.0)
        high = weight.astype(jnp.bfloat16)
        insert[0, :, b * lanes : (b + 1) * lanes] = high
        insert[1, :, b * lanes : (b + 1) * lanes] = (weight - high.astype(jnp.float32)).astype(jnp.bfloat16)
    own.wait()
    others = got.at[pl.ds(0, devices - 1)]
    pltpu.make_async_copy(others, others, in_sem).wait()
    pieces = got[...].reshape(devices * CAP, width)
    volume = jnp.dot(insert[0], pieces, preferred_element_type=jnp.float32)
    volume = volume + jnp.dot(insert[1], pieces, preferred_element_type=jnp.float32)
    volume_ref[...] = volume
    part_rows = RD // len(ROUTES)
    for q in routes:
        next_ref[torus.at["y"], torus.at["x"], q] = volume[
            q * part_rows : (q + 1) * part_rows
        ].astype(jnp.bfloat16)

    def origin(q, stage, hop):
        axis, sign = ROUTES[q]
        axis = axis if stage == 1 else other(axis)
        return lax.rem(torus.at[axis] - sign * hop + 2 * SIDE, SIDE)

    def place(q, first, second):
        y, x = (second, first) if ROUTES[q][0] == "x" else (first, second)
        return next_ref.at[y, x, q]

    def hop_a(q, hop):
        axis, sign = ROUTES[q]
        spot = place(q, origin(q, 1, hop), torus.at[other(axis)])
        return pltpu.make_async_remote_copy(
            src_ref=spot,
            dst_ref=spot,
            send_sem=send_a.at[q, hop],
            recv_sem=recv_a.at[q, hop],
            device_id=torus.neighbour(axis, sign),
            device_id_type=MESH,
        )

    def hop_b(q, hop, j):
        axis, sign = ROUTES[q]
        spot = place(q, origin(q, 1, j), origin(q, 2, hop))
        return pltpu.make_async_remote_copy(
            src_ref=spot,
            dst_ref=spot,
            send_sem=send_b.at[q, hop, j],
            recv_sem=recv_b.at[q, hop, j],
            device_id=torus.neighbour(other(axis), sign),
            device_id_type=MESH,
        )

    for q in routes:
        hop_a(q, 0).start()
        hop_b(q, 0, 0).start()
    for step in range(1, 2 * SIDE - 1):
        for q in routes:
            if step < SIDE:
                hop_a(q, step - 1).wait_recv()
                if step < SIDE - 1:
                    hop_a(q, step).start()
                hop_b(q, 0, step).start()
        for q in routes:
            for hop in range(SIDE - 1):
                j = step - 1 - hop
                if 0 <= j < SIDE:
                    hop_b(q, hop, j).wait_recv()
                    if hop < SIDE - 2:
                        hop_b(q, hop + 1, j).start()
    for q in routes:
        for hop in range(SIDE - 1):
            hop_a(q, hop).wait_send()
            for j in range(SIDE):
                hop_b(q, hop, j).wait_send()
    sent = packed.at[pl.ds(0, devices - 1)]
    pltpu.make_async_copy(sent, sent, out_sem).wait()


def exchanged(pieces, slot, row, part, devices):
    width = pieces.shape[1]
    routes = len(ROUTES)
    hops = SIDE - 1
    part_rows = RD // routes
    vmem = pl.BlockSpec(memory_space=pltpu.VMEM)
    sems_a = pltpu.SemaphoreType.DMA((routes, hops))
    sems_b = pltpu.SemaphoreType.DMA((routes, hops, SIDE))
    return pl.pallas_call(
        exchange_kernel,
        out_shape=(
            jax.ShapeDtypeStruct((RD, width), jnp.float32),
            jax.ShapeDtypeStruct((SIDE, SIDE, routes, part_rows, width), jnp.bfloat16),
        ),
        in_specs=[vmem] * 4,
        out_specs=(vmem, vmem),
        scratch_shapes=[
            pltpu.VMEM((devices, CAP, width), jnp.bfloat16),
            pltpu.VMEM((devices, CAP, width), jnp.bfloat16),
            pltpu.VMEM((2, RD, devices * CAP), jnp.bfloat16),
            pltpu.SemaphoreType.DMA,
            pltpu.SemaphoreType.DMA,
            pltpu.SemaphoreType.DMA,
            sems_a,
            sems_a,
            sems_b,
            sems_b,
        ],
        compiler_params=pltpu.CompilerParams(
            collective_id=1, has_side_effects=True, vmem_limit_bytes=32 * 1024 * 1024
        ),
        name="exchange_pieces",
    )(pieces, slot, row, part)


def send_slots(dests, devices):
    count = dests.shape[0]
    onehot = dests[:, None] == jnp.arange(devices, dtype=jnp.int32)[None, :]
    place = jnp.arange(count, dtype=jnp.int32)
    before = (place[None, :] < place[:, None]).astype(jnp.bfloat16)
    counts = jnp.dot(before, onehot.astype(jnp.bfloat16), preferred_element_type=jnp.float32)
    rank = jnp.sum(jnp.where(onehot, counts, 0.0), axis=1).astype(jnp.int32)
    return dests * CAP + rank


def shards(particles, blocks, references, inv_noise, destination, row_index, fraction):
    particle_count, groups, row_width = particles.shape
    orients = references.shape[0]
    dom_size = lax.axis_size("dom")
    slab_size = lax.axis_size("slab")
    devices = dom_size * slab_size
    dom_pos = lax.axis_index("dom")
    slab_pos = lax.axis_index("slab")
    share = orients // dom_size
    weighted = (references.astype(jnp.float32) * inv_noise[None, :, None]).astype(jnp.bfloat16)
    scores = lax.dot_general(
        particles, weighted, (((1, 2), (1, 2)), ((), ())), preferred_element_type=jnp.float32
    )
    posterior, row, part = posteriors(
        scores, blocks, destination, row_index, fraction, dom_size, slab_size
    )
    pieces = summed_slices(particles.transpose(1, 0, 2), posterior, share)
    pieces = pieces.reshape(groups * share, row_width)

    my_dest = lax.dynamic_slice(
        destination, (slab_pos * groups, dom_pos * share), (groups, share)
    )
    slot = send_slots(my_dest.reshape(-1), devices)
    volume, next_slab = exchanged(pieces, slot[None, :], row, part, devices)
    next_slab = next_slab.reshape(dom_size * RD, row_width)
    return (volume, next_slab)


def solution(mesh):
    return jax.shard_map(
        shards,
        mesh=mesh,
        in_specs=(
            P("dom", "slab", None),
            P("dom", None),
            P(None, "slab", None),
            P("slab"),
            P(),
            P(),
            P(),
        ),
        out_specs=(P(("dom", "slab"), None), P(None, "slab")),
        check_vma=False,
    )
```

```python
import functools

import jax
import jax.numpy as jnp
from jax import lax
from jax.experimental import pallas as pl
from jax.experimental.pallas import tpu as pltpu
from jax.sharding import PartitionSpec as P

MESH = pl.DeviceIdType.MESH
OB = 128
RD = 256
CAP = 16
SIDE = 4
CHUNKS = 5
TILE = 8
ROWS = 16
BAND = 256
ROUTES = (("x", 1), ("x", -1), ("y", 1), ("y", -1))


class Torus:
    def __init__(self):
        dom = lax.axis_index("dom")
        self.slab = lax.axis_index("slab")
        self.at = {"y": lax.div(dom, SIDE), "x": lax.rem(dom, SIDE)}

    def neighbour(self, axis, step):
        at = dict(self.at)
        at[axis] = lax.rem(at[axis] + step + SIDE, SIDE)
        return (at["y"] * SIDE + at["x"], self.slab)


def other(axis):
    return "y" if axis == "x" else "x"


def partial_scores(x_ref, r_ref, noise_ref, images, scores, raw_x, raw_r, weighted, x_sem, r_sem):
    particles, groups, _ = x_ref.shape
    orients = r_ref.shape[0]
    tile = raw_x.shape[2]
    tiles = groups // tile
    over_lanes = (((1,), (1,)), ((), ()))

    def fetch(ref, raw, sem, t):
        slot = lax.rem(t, 2)
        groups_of = pl.ds(pl.multiple_of(t * tile, tile), tile)
        return pltpu.make_async_copy(ref.at[:, groups_of], raw.at[slot], sem.at[slot])

    def start(t):
        fetch(x_ref, raw_x, x_sem, t).start()
        fetch(r_ref, raw_r, r_sem, t).start()

    start(0)
    start(1)
    scores[...] = jnp.zeros_like(scores)

    @pl.loop(0, tiles)
    def _(t):
        slot = lax.rem(t, 2)
        first = t * tile
        fetch(x_ref, raw_x, x_sem, t).wait()

        @pl.loop(0, particles // ROWS)
        def _(b):
            span = pl.ds(pl.multiple_of(b * ROWS, ROWS), ROWS)
            images[pl.ds(first, tile), span] = jnp.swapaxes(raw_x[slot, span], 0, 1)

        fetch(r_ref, raw_r, r_sem, t).wait()

        @pl.loop(0, orients // ROWS)
        def _(b):
            span = pl.ds(pl.multiple_of(b * ROWS, ROWS), ROWS)
            value = jnp.swapaxes(raw_r[slot, span], 0, 1)
            for g in range(tile):
                scaled = value[g].astype(jnp.float32) * noise_ref[first + g]
                weighted[g, span] = scaled.astype(jnp.bfloat16)

        @pl.when(t + 2 < tiles)
        def _():
            start(t + 2)

        for m in range(0, particles, BAND):
            acc = scores[m : m + BAND]
            for g in range(tile):
                acc = acc + lax.dot_general(
                    images[first + g, m : m + BAND], weighted[g], over_lanes,
                    preferred_element_type=jnp.float32,
                )
            scores[m : m + BAND] = acc


def slot_tables(dest_ref, row_ref, part_ref, me, counts, rows_at, parts_at, row_out, part_out):
    slabs = lax.axis_size("slab")
    orients = dest_ref.shape[1]
    groups = dest_ref.shape[0] // slabs
    doms = row_out.shape[0]
    shift = (orients // doms).bit_length() - 1
    here = lax.broadcasted_iota(jnp.int32, (orients, orients), 0)
    there = lax.broadcasted_iota(jnp.int32, (orients, orients), 1)
    same = lax.shift_right_logical(here, shift) == lax.shift_right_logical(there, shift)
    share = same.astype(jnp.float32).astype(jnp.bfloat16)
    before = jnp.where(same & (here < there), 1.0, 0.0).astype(jnp.bfloat16)
    mask = (dest_ref[...] == me).astype(jnp.float32).astype(jnp.bfloat16)
    counts[0] = jnp.dot(mask, before, preferred_element_type=jnp.float32)
    counts[1] = jnp.dot(mask, share, preferred_element_type=jnp.float32)
    lower = lax.broadcasted_iota(jnp.int32, (groups, groups), 0) > lax.broadcasted_iota(
        jnp.int32, (groups, groups), 1
    )
    lower = lower.astype(jnp.float32).astype(jnp.bfloat16)

    @pl.loop(0, slabs)
    def _(s):
        span = pl.ds(pl.multiple_of(s * groups, groups), groups)
        above = jnp.dot(
            lower, counts[1, span].astype(jnp.bfloat16), preferred_element_type=jnp.float32
        )
        rank = jnp.where(dest_ref[span] == me, counts[0, span] + above, -1.0)
        row = row_ref[span].astype(jnp.float32) + 1.0
        part = part_ref[span]
        found_rows = []
        found_parts = []
        for j in range(CAP):
            chosen = rank == j
            found_rows.append(jnp.sum(jnp.where(chosen, row, 0.0), axis=0, keepdims=True))
            found_parts.append(jnp.sum(jnp.where(chosen, part, 0.0), axis=0, keepdims=True))
        slots = pl.ds(pl.multiple_of(s * CAP, CAP), CAP)
        rows_at[slots] = jnp.concatenate(found_rows, axis=0)
        parts_at[slots] = jnp.concatenate(found_parts, axis=0)

    owner = lax.shift_right_logical(lax.broadcasted_iota(jnp.int32, (doms, orients), 1), shift)
    gather = (owner == lax.broadcasted_iota(jnp.int32, (doms, orients), 0)).astype(jnp.float32)
    over_lanes = (((1,), (1,)), ((), ()))
    for found, out in ((rows_at, row_out), (parts_at, part_out)):
        out[...] = lax.dot_general(
            gather, found[...], over_lanes,
            precision=lax.Precision.HIGHEST, preferred_element_type=jnp.float32,
        )
    row_out[...] = row_out[...] - 1.0


class Column:
    def __init__(self):
        self.dom = lax.axis_index("dom")
        self.slab = lax.axis_index("slab")
        self.slabs = lax.axis_size("slab")
        self.chips = self.slabs // 2
        self.chip = lax.div(self.slab, 2)
        self.core = lax.rem(self.slab, 2)
        self.mate = (self.dom, 2 * self.chip + 1 - self.core)

    def peer(self, step):
        return (self.dom, 2 * lax.rem(self.chip + step, self.chips) + self.core)


def posteriors(
    column, scores_ref, blocks_ref, post_ref, meanwhile,
    mine, from_mate, total, from_chips, found,
    mate_send, mate_recv, chip_send, chip_recv, back_send, back_recv, last_send, last_recv,
):
    slabs, chips, chip, core = column.slabs, column.chips, column.chip, column.core
    mate, peer = column.mate, column.peer
    count = mine.shape[2]

    def picked(span, which):
        chosen = blocks_ref[span, which : which + 1]
        value = scores_ref[span, 0:OB]
        for b in range(1, scores_ref.shape[1] // OB):
            value = jnp.where(chosen == b, scores_ref[span, b * OB : (b + 1) * OB], value)
        return value

    for s in range(slabs):
        span = pl.ds(s * count, count)
        for which in range(2):
            mine[s % 2, s // 2, :, which * OB : (which + 1) * OB] = picked(span, which)
    to_mate = pltpu.make_async_remote_copy(
        src_ref=mine.at[1 - core],
        dst_ref=from_mate,
        send_sem=mate_send,
        recv_sem=mate_recv,
        device_id=mate,
        device_id_type=MESH,
    )
    to_mate.start()
    to_mate.wait_recv()
    total[...] = mine[core] + from_mate[...]

    def to_chip(step):
        return pltpu.make_async_remote_copy(
            src_ref=total.at[lax.rem(chip + step, chips)],
            dst_ref=from_chips.at[step - 1],
            send_sem=chip_send.at[step - 1],
            recv_sem=chip_recv.at[step - 1],
            device_id=peer(step),
            device_id_type=MESH,
        )

    for step in range(1, chips):
        to_chip(step).start()
    meanwhile()
    for step in range(1, chips):
        to_chip(step).wait_recv()
    scores = total[chip]
    for step in range(1, chips):
        scores = scores + from_chips[step - 1]
    weights = jnp.exp(scores - jnp.max(scores, axis=1, keepdims=True))
    found[chip, core] = (weights / jnp.sum(weights, axis=1, keepdims=True)).astype(jnp.bfloat16)

    def back(step):
        return pltpu.make_async_remote_copy(
            src_ref=found.at[chip, core],
            dst_ref=found.at[chip, core],
            send_sem=back_send.at[step - 1],
            recv_sem=back_recv.at[step - 1],
            device_id=peer(step),
            device_id_type=MESH,
        )

    for step in range(1, chips):
        back(step).start()
    for step in range(1, chips):
        back(step).wait_recv()
    last = pltpu.make_async_remote_copy(
        src_ref=found.at[:, core],
        dst_ref=found.at[:, core],
        send_sem=last_send,
        recv_sem=last_recv,
        device_id=mate,
        device_id_type=MESH,
    )
    last.start()
    last.wait_recv()
    everyone = found[...].astype(jnp.float32).reshape(slabs * count, 2 * OB)
    first, second = blocks_ref[:, 0:1], blocks_ref[:, 1:2]
    for b in range(scores_ref.shape[1] // OB):
        value = jnp.where(first == b, everyone[:, :OB], 0.0)
        value = jnp.where(second == b, everyone[:, OB:], value)
        post_ref[b * OB : (b + 1) * OB, :] = value.T.astype(jnp.bfloat16)
    to_mate.wait_send()
    last.wait_send()
    for step in range(1, chips):
        to_chip(step).wait_send()
        back(step).wait_send()


def sum_over_dom(torus, images, post_ref, out_ref, partial, got1, got2, send1, recv1, send2, recv2):
    per_chunk = images.shape[0] // (len(ROUTES) * CHUNKS)
    share = out_ref.shape[1]

    def first_group(q, i):
        return (i * len(ROUTES) + q) * per_chunk

    def block(q, stage, hop):
        axis, sign = ROUTES[q]
        axis = axis if stage == 1 else other(axis)
        return lax.rem(torus.at[axis] - sign * (1 + hop) + 2 * SIDE, SIDE)

    def hop1(q, hop, i):
        axis, sign = ROUTES[q]
        source = partial.at[q, i, block(q, 1, 0)] if hop == 0 else got1.at[q, hop - 1, i]
        return pltpu.make_async_remote_copy(
            src_ref=source,
            dst_ref=got1.at[q, hop, i],
            send_sem=send1.at[q, hop, i],
            recv_sem=recv1.at[q, hop, i],
            device_id=torus.neighbour(axis, sign),
            device_id_type=MESH,
        )

    def hop2(q, hop, i):
        axis, sign = ROUTES[q]
        source = got1.at[q, SIDE - 2, i, block(q, 2, 0)] if hop == 0 else got2.at[q, hop - 1, i]
        return pltpu.make_async_remote_copy(
            src_ref=source,
            dst_ref=got2.at[q, hop, i],
            send_sem=send2.at[q, hop, i],
            recv_sem=recv2.at[q, hop, i],
            device_id=torus.neighbour(other(axis), sign),
            device_id_type=MESH,
        )

    def added(a, b):
        return (a.astype(jnp.float32) + b.astype(jnp.float32)).astype(jnp.bfloat16)

    routes = range(len(ROUTES))

    @pl.loop(0, CHUNKS)
    def _(i):
        for q in routes:
            for j in range(per_chunk):
                value = jnp.dot(
                    post_ref[...], images[first_group(q, i) + j], preferred_element_type=jnp.float32
                ).astype(jnp.bfloat16)
                for yy in range(SIDE):
                    for xx in range(SIDE):
                        first, second = (xx, yy) if ROUTES[q][0] == "x" else (yy, xx)
                        begin = (yy * SIDE + xx) * share
                        partial[q, i, first, second, j] = value[begin : begin + share]
            hop1(q, 0, i).start()

    for hop in range(SIDE - 2):

        @pl.loop(0, CHUNKS)
        def _(i):
            for q in routes:
                hop1(q, hop, i).wait_recv()
                got1[q, hop, i] = added(got1[q, hop, i], partial[q, i, block(q, 1, hop + 1)])
                hop1(q, hop + 1, i).start()

    last = SIDE - 2

    @pl.loop(0, CHUNKS)
    def _(i):
        for q in routes:
            hop1(q, last, i).wait_recv()
            got1[q, last, i] = added(got1[q, last, i], partial[q, i, torus.at[ROUTES[q][0]]])
            hop2(q, 0, i).start()

    for hop in range(SIDE - 2):

        @pl.loop(0, CHUNKS)
        def _(i):
            for q in routes:
                hop2(q, hop, i).wait_recv()
                got2[q, hop, i] = added(got2[q, hop, i], got1[q, last, i, block(q, 2, hop + 1)])
                hop2(q, hop + 1, i).start()

    @pl.loop(0, CHUNKS)
    def _(i):
        for q in routes:
            hop2(q, last, i).wait_recv()
            mine = got1[q, last, i, torus.at[other(ROUTES[q][0])]]
            out_ref[pl.ds(first_group(q, i), per_chunk)] = added(got2[q, last, i], mine)

    @pl.loop(0, CHUNKS)
    def _(i):
        for q in routes:
            for hop in range(SIDE - 1):
                hop1(q, hop, i).wait_send()
                hop2(q, hop, i).wait_send()


def project_kernel(
    x_ref, r_ref, noise_ref, blocks_ref, dest_ref, row_ref, part_ref,
    out_ref, row_out, part_out,
    images, scores, raw_x, raw_r, weighted, post, *rest
):
    x_sem, r_sem = rest[:2]
    post_scratch = rest[2:7]
    counts, rows_at, parts_at = rest[7:10]
    post_sems = rest[10:18]
    sum_scratch = rest[18:]
    torus = Torus()
    column = Column()
    me = column.dom * column.slabs + column.slab
    barrier = pltpu.get_barrier_semaphore()
    others = [column.mate] + [column.peer(step) for step in range(1, column.chips)]
    others = others + [torus.neighbour(axis, sign) for axis, sign in ROUTES]
    for device in others:
        pl.semaphore_signal(barrier, inc=1, device_id=device, device_id_type=MESH)
    partial_scores(x_ref, r_ref, noise_ref, images, scores, raw_x, raw_r, weighted, x_sem, r_sem)
    pl.semaphore_wait(barrier, len(others))

    def meanwhile():
        slot_tables(dest_ref, row_ref, part_ref, me, counts, rows_at, parts_at, row_out, part_out)

    posteriors(column, scores, blocks_ref, post, meanwhile, *post_scratch, *post_sems)
    sum_over_dom(torus, images, post, out_ref, *sum_scratch)


def summed_slices(particles, references, inv_noise, blocks, destination, row_index, fraction, doms, slabs):
    count, groups, width = particles.shape
    orients = references.shape[0]
    share = orients // doms
    chips = slabs // 2
    part = count // slabs
    routes = len(ROUTES)
    hops = SIDE - 1
    piece = (groups // (routes * CHUNKS), share, width)
    vmem = pl.BlockSpec(memory_space=pltpu.VMEM)
    hbm = pl.BlockSpec(memory_space=pl.ANY)
    dma = pltpu.SemaphoreType.DMA
    table = jax.ShapeDtypeStruct((doms, slabs * CAP), jnp.float32)
    return pl.pallas_call(
        project_kernel,
        out_shape=(jax.ShapeDtypeStruct((groups, share, width), jnp.bfloat16), table, table),
        in_specs=[hbm, hbm, pl.BlockSpec(memory_space=pltpu.SMEM)] + [vmem] * 4,
        out_specs=(vmem,) * 3,
        scratch_shapes=[
            pltpu.VMEM((groups, count, width), jnp.bfloat16),
            pltpu.VMEM((count, orients), jnp.float32),
            pltpu.VMEM((2, count, TILE, width), jnp.bfloat16),
            pltpu.VMEM((2, orients, TILE, width), jnp.bfloat16),
            pltpu.VMEM((TILE, orients, width), jnp.bfloat16),
            pltpu.VMEM((orients, count), jnp.bfloat16),
            dma((2,)),
            dma((2,)),
            pltpu.VMEM((2, chips, part, 2 * OB), jnp.float32),
            pltpu.VMEM((chips, part, 2 * OB), jnp.float32),
            pltpu.VMEM((chips, part, 2 * OB), jnp.float32),
            pltpu.VMEM((chips - 1, part, 2 * OB), jnp.float32),
            pltpu.VMEM((chips, 2, part, 2 * OB), jnp.bfloat16),
            pltpu.VMEM((2,) + destination.shape, jnp.float32),
            pltpu.VMEM((slabs * CAP, orients), jnp.float32),
            pltpu.VMEM((slabs * CAP, orients), jnp.float32),
            dma,
            dma,
            dma((chips - 1,)),
            dma((chips - 1,)),
            dma((chips - 1,)),
            dma((chips - 1,)),
            dma,
            dma,
            pltpu.VMEM((routes, CHUNKS, SIDE, SIDE) + piece, jnp.bfloat16),
            pltpu.VMEM((routes, hops, CHUNKS, SIDE) + piece, jnp.bfloat16),
            pltpu.VMEM((routes, hops, CHUNKS) + piece, jnp.bfloat16),
        ]
        + [dma((routes, hops, CHUNKS))] * 4,
        compiler_params=pltpu.CompilerParams(
            collective_id=0, has_side_effects=True, vmem_limit_bytes=58 * 1024 * 1024
        ),
        name="project",
    )(particles, references, inv_noise, blocks, destination, row_index, fraction)


def exchange_kernel(
    pieces_ref, slot_ref, row_ref, part_ref, volume_ref, next_ref,
    packed, got, insert, own_sem, out_sem, in_sem, send_a, recv_a, send_b, recv_b,
):
    torus = Torus()
    slabs = lax.axis_size("slab")
    devices = lax.axis_size("dom") * slabs
    me = (torus.at["y"] * SIDE + torus.at["x"]) * slabs + torus.slab
    width = pieces_ref.shape[1]
    routes = range(len(ROUTES))

    def device(number):
        return (lax.div(number, slabs), lax.rem(number, slabs))

    barrier = pltpu.get_barrier_semaphore()

    @pl.loop(1, devices)
    def _(k):
        to = lax.rem(me + k, devices)
        pl.semaphore_signal(barrier, inc=1, device_id=device(to), device_id_type=MESH)

    block = RD
    owners = block // CAP
    numbers = lax.broadcasted_iota(jnp.int32, (block, pieces_ref.shape[0]), 0)
    for b in range(devices // owners):
        pick = (numbers + b * block == slot_ref[...]).astype(jnp.float32).astype(jnp.bfloat16)
        value = jnp.dot(pick, pieces_ref[...], preferred_element_type=jnp.float32)
        packed[b * owners : (b + 1) * owners] = value.astype(jnp.bfloat16).reshape(owners, CAP, width)
    pl.semaphore_wait(barrier, devices - 1)

    @pl.loop(1, devices)
    def _(k):
        to = lax.rem(me + k, devices)
        pltpu.make_async_remote_copy(
            src_ref=packed.at[to],
            dst_ref=got.at[me],
            send_sem=out_sem,
            recv_sem=in_sem,
            device_id=device(to),
            device_id_type=MESH,
        ).start()

    own = pltpu.make_async_copy(packed.at[me], got.at[me], own_sem)
    own.start()
    lanes = row_ref.shape[1]
    rows = lax.broadcasted_iota(jnp.int32, (RD, lanes), 0).astype(jnp.float32)
    for b in range(row_ref.shape[0]):
        row = row_ref[b : b + 1, :]
        part = part_ref[b : b + 1, :]
        weight = jnp.where(rows == row, 1.0 - part, 0.0) + jnp.where(rows == row + 1, part, 0.0)
        high = weight.astype(jnp.bfloat16)
        insert[0, :, b * lanes : (b + 1) * lanes] = high
        insert[1, :, b * lanes : (b + 1) * lanes] = (weight - high.astype(jnp.float32)).astype(jnp.bfloat16)
    own.wait()
    others = got.at[pl.ds(0, devices - 1)]
    pltpu.make_async_copy(others, others, in_sem).wait()
    pieces = got[...].reshape(devices * CAP, width)
    volume = jnp.dot(insert[0], pieces, preferred_element_type=jnp.float32)
    volume = volume + jnp.dot(insert[1], pieces, preferred_element_type=jnp.float32)
    volume_ref[...] = volume
    part_rows = RD // len(ROUTES)
    for q in routes:
        next_ref[torus.at["y"], torus.at["x"], q] = volume[
            q * part_rows : (q + 1) * part_rows
        ].astype(jnp.bfloat16)

    def origin(q, stage, hop):
        axis, sign = ROUTES[q]
        axis = axis if stage == 1 else other(axis)
        return lax.rem(torus.at[axis] - sign * hop + 2 * SIDE, SIDE)

    def place(q, first, second):
        y, x = (second, first) if ROUTES[q][0] == "x" else (first, second)
        return next_ref.at[y, x, q]

    def hop_a(q, hop):
        axis, sign = ROUTES[q]
        spot = place(q, origin(q, 1, hop), torus.at[other(axis)])
        return pltpu.make_async_remote_copy(
            src_ref=spot,
            dst_ref=spot,
            send_sem=send_a.at[q, hop],
            recv_sem=recv_a.at[q, hop],
            device_id=torus.neighbour(axis, sign),
            device_id_type=MESH,
        )

    def hop_b(q, hop, j):
        axis, sign = ROUTES[q]
        spot = place(q, origin(q, 1, j), origin(q, 2, hop))
        return pltpu.make_async_remote_copy(
            src_ref=spot,
            dst_ref=spot,
            send_sem=send_b.at[q, hop, j],
            recv_sem=recv_b.at[q, hop, j],
            device_id=torus.neighbour(other(axis), sign),
            device_id_type=MESH,
        )

    for q in routes:
        hop_a(q, 0).start()
        hop_b(q, 0, 0).start()
    for step in range(1, 2 * SIDE - 1):
        for q in routes:
            if step < SIDE:
                hop_a(q, step - 1).wait_recv()
                if step < SIDE - 1:
                    hop_a(q, step).start()
                hop_b(q, 0, step).start()
        for q in routes:
            for hop in range(SIDE - 1):
                j = step - 1 - hop
                if 0 <= j < SIDE:
                    hop_b(q, hop, j).wait_recv()
                    if hop < SIDE - 2:
                        hop_b(q, hop + 1, j).start()
    for q in routes:
        for hop in range(SIDE - 1):
            hop_a(q, hop).wait_send()
            for j in range(SIDE):
                hop_b(q, hop, j).wait_send()
    sent = packed.at[pl.ds(0, devices - 1)]
    pltpu.make_async_copy(sent, sent, out_sem).wait()


def exchanged(pieces, slot, row, part, devices):
    width = pieces.shape[1]
    routes = len(ROUTES)
    hops = SIDE - 1
    part_rows = RD // routes
    vmem = pl.BlockSpec(memory_space=pltpu.VMEM)
    sems_a = pltpu.SemaphoreType.DMA((routes, hops))
    sems_b = pltpu.SemaphoreType.DMA((routes, hops, SIDE))
    return pl.pallas_call(
        exchange_kernel,
        out_shape=(
            jax.ShapeDtypeStruct((RD, width), jnp.float32),
            jax.ShapeDtypeStruct((SIDE, SIDE, routes, part_rows, width), jnp.bfloat16),
        ),
        in_specs=[vmem] * 4,
        out_specs=(vmem, vmem),
        scratch_shapes=[
            pltpu.VMEM((devices, CAP, width), jnp.bfloat16),
            pltpu.VMEM((devices, CAP, width), jnp.bfloat16),
            pltpu.VMEM((2, RD, devices * CAP), jnp.bfloat16),
            pltpu.SemaphoreType.DMA,
            pltpu.SemaphoreType.DMA,
            pltpu.SemaphoreType.DMA,
            sems_a,
            sems_a,
            sems_b,
            sems_b,
        ],
        compiler_params=pltpu.CompilerParams(
            collective_id=1, has_side_effects=True, vmem_limit_bytes=32 * 1024 * 1024
        ),
        name="exchange_pieces",
    )(pieces, slot, row, part)


def send_slots(dests, devices):
    count = dests.shape[0]
    onehot = dests[:, None] == jnp.arange(devices, dtype=jnp.int32)[None, :]
    place = jnp.arange(count, dtype=jnp.int32)
    before = (place[None, :] < place[:, None]).astype(jnp.bfloat16)
    counts = jnp.dot(before, onehot.astype(jnp.bfloat16), preferred_element_type=jnp.float32)
    rank = jnp.sum(jnp.where(onehot, counts, 0.0), axis=1).astype(jnp.int32)
    return dests * CAP + rank


def shards(particles, blocks, references, inv_noise, destination, row_index, fraction):
    _, groups, row_width = particles.shape
    orients = references.shape[0]
    dom_size = lax.axis_size("dom")
    slab_size = lax.axis_size("slab")
    devices = dom_size * slab_size
    dom_pos = lax.axis_index("dom")
    slab_pos = lax.axis_index("slab")
    share = orients // dom_size
    pieces, row, part = summed_slices(
        particles, references, inv_noise, blocks, destination, row_index, fraction, dom_size, slab_size
    )
    pieces = pieces.reshape(groups * share, row_width)

    my_dest = lax.dynamic_slice(
        destination, (slab_pos * groups, dom_pos * share), (groups, share)
    )
    slot = send_slots(my_dest.reshape(-1), devices)
    volume, next_slab = exchanged(pieces, slot[None, :], row, part, devices)
    next_slab = next_slab.reshape(dom_size * RD, row_width)
    return (volume, next_slab)


def solution(mesh):
    return jax.shard_map(
        shards,
        mesh=mesh,
        in_specs=(
            P("dom", "slab", None),
            P("dom", None),
            P(None, "slab", None),
            P("slab"),
            P(),
            P(),
            P(),
        ),
        out_specs=(P(("dom", "slab"), None), P(None, "slab")),
        check_vma=False,
    )
```

```python
import functools

import jax
import jax.numpy as jnp
from jax import lax
from jax.experimental import pallas as pl
from jax.experimental.pallas import tpu as pltpu
from jax.sharding import PartitionSpec as P

MESH = pl.DeviceIdType.MESH
OB = 128
RD = 256
CAP = 16
SIDE = 4
CHUNKS = 5
TILE = 8
ROWS = 16
BAND = 256
ROUTES = (("x", 1), ("x", -1), ("y", 1), ("y", -1))


class Torus:
    def __init__(self):
        dom = lax.axis_index("dom")
        self.slab = lax.axis_index("slab")
        self.at = {"y": lax.div(dom, SIDE), "x": lax.rem(dom, SIDE)}

    def neighbour(self, axis, step):
        at = dict(self.at)
        at[axis] = lax.rem(at[axis] + step + SIDE, SIDE)
        return (at["y"] * SIDE + at["x"], self.slab)


def other(axis):
    return "y" if axis == "x" else "x"


def partial_scores(x_ref, r_ref, noise_ref, images, scores, raw_x, raw_r, weighted, x_sem, r_sem):
    particles, groups, _ = x_ref.shape
    orients = r_ref.shape[0]
    tile = raw_x.shape[2]
    tiles = groups // tile
    over_lanes = (((1,), (1,)), ((), ()))

    def fetch(ref, raw, sem, t):
        slot = lax.rem(t, 2)
        groups_of = pl.ds(pl.multiple_of(t * tile, tile), tile)
        return pltpu.make_async_copy(ref.at[:, groups_of], raw.at[slot], sem.at[slot])

    def start(t):
        fetch(x_ref, raw_x, x_sem, t).start()
        fetch(r_ref, raw_r, r_sem, t).start()

    start(0)
    start(1)
    scores[...] = jnp.zeros_like(scores)

    @pl.loop(0, tiles)
    def _(t):
        slot = lax.rem(t, 2)
        first = t * tile
        fetch(x_ref, raw_x, x_sem, t).wait()

        @pl.loop(0, particles // ROWS)
        def _(b):
            span = pl.ds(pl.multiple_of(b * ROWS, ROWS), ROWS)
            images[pl.ds(first, tile), span] = jnp.swapaxes(raw_x[slot, span], 0, 1)

        fetch(r_ref, raw_r, r_sem, t).wait()

        @pl.loop(0, orients // ROWS)
        def _(b):
            span = pl.ds(pl.multiple_of(b * ROWS, ROWS), ROWS)
            value = jnp.swapaxes(raw_r[slot, span], 0, 1)
            for g in range(tile):
                scaled = value[g].astype(jnp.float32) * noise_ref[first + g]
                weighted[g, span] = scaled.astype(jnp.bfloat16)

        @pl.when(t + 2 < tiles)
        def _():
            start(t + 2)

        for m in range(0, particles, BAND):
            acc = scores[m : m + BAND]
            for g in range(tile):
                acc = acc + lax.dot_general(
                    images[first + g, m : m + BAND], weighted[g], over_lanes,
                    preferred_element_type=jnp.float32,
                )
            scores[m : m + BAND] = acc


def slot_tables(dest_ref, row_ref, part_ref, me, counts, rows_at, parts_at, row_out, part_out):
    slabs = lax.axis_size("slab")
    orients = dest_ref.shape[1]
    groups = dest_ref.shape[0] // slabs
    doms = row_out.shape[0]
    shift = (orients // doms).bit_length() - 1
    here = lax.broadcasted_iota(jnp.int32, (orients, orients), 0)
    there = lax.broadcasted_iota(jnp.int32, (orients, orients), 1)
    same = lax.shift_right_logical(here, shift) == lax.shift_right_logical(there, shift)
    share = same.astype(jnp.float32).astype(jnp.bfloat16)
    before = jnp.where(same & (here < there), 1.0, 0.0).astype(jnp.bfloat16)
    mask = (dest_ref[...] == me).astype(jnp.float32).astype(jnp.bfloat16)
    counts[0] = jnp.dot(mask, before, preferred_element_type=jnp.float32)
    counts[1] = jnp.dot(mask, share, preferred_element_type=jnp.float32)
    lower = lax.broadcasted_iota(jnp.int32, (groups, groups), 0) > lax.broadcasted_iota(
        jnp.int32, (groups, groups), 1
    )
    lower = lower.astype(jnp.float32).astype(jnp.bfloat16)

    @pl.loop(0, slabs)
    def _(s):
        span = pl.ds(pl.multiple_of(s * groups, groups), groups)
        above = jnp.dot(
            lower, counts[1, span].astype(jnp.bfloat16), preferred_element_type=jnp.float32
        )
        rank = jnp.where(dest_ref[span] == me, counts[0, span] + above, -1.0)
        row = row_ref[span].astype(jnp.float32) + 1.0
        part = part_ref[span]
        found_rows = []
        found_parts = []
        for j in range(CAP):
            chosen = rank == j
            found_rows.append(jnp.sum(jnp.where(chosen, row, 0.0), axis=0, keepdims=True))
            found_parts.append(jnp.sum(jnp.where(chosen, part, 0.0), axis=0, keepdims=True))
        slots = pl.ds(pl.multiple_of(s * CAP, CAP), CAP)
        rows_at[slots] = jnp.concatenate(found_rows, axis=0)
        parts_at[slots] = jnp.concatenate(found_parts, axis=0)

    owner = lax.shift_right_logical(lax.broadcasted_iota(jnp.int32, (doms, orients), 1), shift)
    gather = (owner == lax.broadcasted_iota(jnp.int32, (doms, orients), 0)).astype(jnp.float32)
    over_lanes = (((1,), (1,)), ((), ()))
    for found, out in ((rows_at, row_out), (parts_at, part_out)):
        out[...] = lax.dot_general(
            gather, found[...], over_lanes,
            precision=lax.Precision.HIGHEST, preferred_element_type=jnp.float32,
        )
    row_out[...] = row_out[...] - 1.0


class Column:
    def __init__(self):
        self.dom = lax.axis_index("dom")
        self.slab = lax.axis_index("slab")
        self.slabs = lax.axis_size("slab")
        self.chips = self.slabs // 2
        self.chip = lax.div(self.slab, 2)
        self.core = lax.rem(self.slab, 2)
        self.mate = (self.dom, 2 * self.chip + 1 - self.core)

    def peer(self, step):
        return (self.dom, 2 * lax.rem(self.chip + step, self.chips) + self.core)


def posteriors(
    column, scores_ref, chosen_ref, post_ref, meanwhile, afterwards,
    mine, from_mate, total, from_chips, found,
    mate_send, mate_recv, chip_send, chip_recv, back_send, back_recv, last_send, last_recv,
):
    slabs, chips, chip, core = column.slabs, column.chips, column.chip, column.core
    mate, peer = column.mate, column.peer
    count = mine.shape[2]

    def picked(span, which):
        chosen = chosen_ref[span, SIDE * which : SIDE * which + 1]
        value = scores_ref[span, 0:OB]
        for b in range(1, scores_ref.shape[1] // OB):
            value = jnp.where(chosen == b, scores_ref[span, b * OB : (b + 1) * OB], value)
        return value

    for s in range(slabs):
        span = pl.ds(s * count, count)
        for which in range(2):
            mine[s % 2, s // 2, :, which * OB : (which + 1) * OB] = picked(span, which)
    to_mate = pltpu.make_async_remote_copy(
        src_ref=mine.at[1 - core],
        dst_ref=from_mate,
        send_sem=mate_send,
        recv_sem=mate_recv,
        device_id=mate,
        device_id_type=MESH,
    )
    to_mate.start()
    to_mate.wait_recv()
    total[...] = mine[core] + from_mate[...]

    def to_chip(step):
        return pltpu.make_async_remote_copy(
            src_ref=total.at[lax.rem(chip + step, chips)],
            dst_ref=from_chips.at[step - 1],
            send_sem=chip_send.at[step - 1],
            recv_sem=chip_recv.at[step - 1],
            device_id=peer(step),
            device_id_type=MESH,
        )

    for step in range(1, chips):
        to_chip(step).start()
    meanwhile()
    for step in range(1, chips):
        to_chip(step).wait_recv()
    scores = total[chip]
    for step in range(1, chips):
        scores = scores + from_chips[step - 1]
    weights = jnp.exp(scores - jnp.max(scores, axis=1, keepdims=True))
    found[chip, core] = (weights / jnp.sum(weights, axis=1, keepdims=True)).astype(jnp.bfloat16)

    def back(step):
        return pltpu.make_async_remote_copy(
            src_ref=found.at[chip, core],
            dst_ref=found.at[chip, core],
            send_sem=back_send.at[step - 1],
            recv_sem=back_recv.at[step - 1],
            device_id=peer(step),
            device_id_type=MESH,
        )

    for step in range(1, chips):
        back(step).start()
    afterwards()
    for step in range(1, chips):
        back(step).wait_recv()
    last = pltpu.make_async_remote_copy(
        src_ref=found.at[:, core],
        dst_ref=found.at[:, core],
        send_sem=last_send,
        recv_sem=last_recv,
        device_id=mate,
        device_id_type=MESH,
    )
    last.start()
    last.wait_recv()
    everyone = found[...].astype(jnp.float32).reshape(slabs * count, 2 * OB)
    first, second = chosen_ref[:, 0:1], chosen_ref[:, SIDE : SIDE + 1]
    for b in range(scores_ref.shape[1] // OB):
        value = jnp.where(first == b, everyone[:, :OB], 0.0)
        value = jnp.where(second == b, everyone[:, OB:], value)
        post_ref[b * OB : (b + 1) * OB, :] = value.T.astype(jnp.bfloat16)
    to_mate.wait_send()
    last.wait_send()
    for step in range(1, chips):
        to_chip(step).wait_send()
        back(step).wait_send()


def sum_over_dom(torus, images, post_ref, out_ref, partial, got1, got2, send1, recv1, send2, recv2):
    per_chunk = images.shape[0] // (len(ROUTES) * CHUNKS)
    share = out_ref.shape[1]

    def first_group(q, i):
        return (i * len(ROUTES) + q) * per_chunk

    def block(q, stage, hop):
        axis, sign = ROUTES[q]
        axis = axis if stage == 1 else other(axis)
        return lax.rem(torus.at[axis] - sign * (1 + hop) + 2 * SIDE, SIDE)

    def hop1(q, hop, i):
        axis, sign = ROUTES[q]
        source = partial.at[q, i, block(q, 1, 0)] if hop == 0 else got1.at[q, hop - 1, i]
        return pltpu.make_async_remote_copy(
            src_ref=source,
            dst_ref=got1.at[q, hop, i],
            send_sem=send1.at[q, hop, i],
            recv_sem=recv1.at[q, hop, i],
            device_id=torus.neighbour(axis, sign),
            device_id_type=MESH,
        )

    def hop2(q, hop, i):
        axis, sign = ROUTES[q]
        source = got1.at[q, SIDE - 2, i, block(q, 2, 0)] if hop == 0 else got2.at[q, hop - 1, i]
        return pltpu.make_async_remote_copy(
            src_ref=source,
            dst_ref=got2.at[q, hop, i],
            send_sem=send2.at[q, hop, i],
            recv_sem=recv2.at[q, hop, i],
            device_id=torus.neighbour(other(axis), sign),
            device_id_type=MESH,
        )

    def added(a, b):
        return (a.astype(jnp.float32) + b.astype(jnp.float32)).astype(jnp.bfloat16)

    routes = range(len(ROUTES))

    @pl.loop(0, CHUNKS)
    def _(i):
        for q in routes:
            for j in range(per_chunk):
                value = jnp.dot(
                    post_ref[...], images[first_group(q, i) + j], preferred_element_type=jnp.float32
                ).astype(jnp.bfloat16)
                for yy in range(SIDE):
                    for xx in range(SIDE):
                        first, second = (xx, yy) if ROUTES[q][0] == "x" else (yy, xx)
                        begin = (yy * SIDE + xx) * share
                        partial[q, i, first, second, j] = value[begin : begin + share]
            hop1(q, 0, i).start()

    for hop in range(SIDE - 2):

        @pl.loop(0, CHUNKS)
        def _(i):
            for q in routes:
                hop1(q, hop, i).wait_recv()
                got1[q, hop, i] = added(got1[q, hop, i], partial[q, i, block(q, 1, hop + 1)])
                hop1(q, hop + 1, i).start()

    last = SIDE - 2

    @pl.loop(0, CHUNKS)
    def _(i):
        for q in routes:
            hop1(q, last, i).wait_recv()
            got1[q, last, i] = added(got1[q, last, i], partial[q, i, torus.at[ROUTES[q][0]]])
            hop2(q, 0, i).start()

    for hop in range(SIDE - 2):

        @pl.loop(0, CHUNKS)
        def _(i):
            for q in routes:
                hop2(q, hop, i).wait_recv()
                got2[q, hop, i] = added(got2[q, hop, i], got1[q, last, i, block(q, 2, hop + 1)])
                hop2(q, hop + 1, i).start()

    @pl.loop(0, CHUNKS)
    def _(i):
        for q in routes:
            hop2(q, last, i).wait_recv()
            mine = got1[q, last, i, torus.at[other(ROUTES[q][0])]]
            out_ref[pl.ds(first_group(q, i), per_chunk)] = added(got2[q, last, i], mine)

    @pl.loop(0, CHUNKS)
    def _(i):
        for q in routes:
            for hop in range(SIDE - 1):
                hop1(q, hop, i).wait_send()
                hop2(q, hop, i).wait_send()


def insertion_weights(row_ref, part_ref, insert):
    lanes = row_ref.shape[1]
    rows = lax.broadcasted_iota(jnp.int32, (RD, lanes), 0).astype(jnp.float32)
    for b in range(row_ref.shape[0]):
        row = row_ref[b : b + 1, :]
        part = part_ref[b : b + 1, :]
        weight = jnp.where(rows == row, 1.0 - part, 0.0) + jnp.where(rows == row + 1, part, 0.0)
        high = weight.astype(jnp.bfloat16)
        insert[0, :, b * lanes : (b + 1) * lanes] = high
        insert[1, :, b * lanes : (b + 1) * lanes] = (weight - high.astype(jnp.float32)).astype(jnp.bfloat16)


def insert_pieces(torus, pieces_ref, slot_ref, insert, volume_ref, packed, got, own_sem, out_sem, in_sem):
    slabs = lax.axis_size("slab")
    devices = lax.axis_size("dom") * slabs
    me = (torus.at["y"] * SIDE + torus.at["x"]) * slabs + torus.slab
    width = pieces_ref.shape[2]
    count = pieces_ref.shape[0] * pieces_ref.shape[1]
    block = RD
    owners = block // CAP
    numbers = lax.broadcasted_iota(jnp.int32, (block, count), 0)
    pieces = pieces_ref[...].reshape(count, width)

    @pl.loop(0, devices // owners)
    def _(k):
        b = lax.rem(lax.div(me, owners) + k, devices // owners)
        first = b * owners
        pick = (numbers + b * block == slot_ref[...]).astype(jnp.float32).astype(jnp.bfloat16)
        value = jnp.dot(pick, pieces, preferred_element_type=jnp.float32)
        packed[pl.ds(first, owners)] = value.astype(jnp.bfloat16).reshape(owners, CAP, width)

        @pl.loop(0, owners)
        def _(j):
            to = first + lax.rem(me + j, owners)

            @pl.when(to != me)
            def _():
                pltpu.make_async_remote_copy(
                    src_ref=packed.at[to],
                    dst_ref=got.at[me],
                    send_sem=out_sem,
                    recv_sem=in_sem,
                    device_id=(lax.div(to, slabs), lax.rem(to, slabs)),
                    device_id_type=MESH,
                ).start()

    own = pltpu.make_async_copy(packed.at[me], got.at[me], own_sem)
    own.start()
    own.wait()
    others = got.at[pl.ds(0, devices - 1)]
    pltpu.make_async_copy(others, others, in_sem).wait()
    received = got[...].reshape(devices * CAP, width)
    volume = jnp.dot(insert[0], received, preferred_element_type=jnp.float32)
    volume_ref[...] = volume + jnp.dot(insert[1], received, preferred_element_type=jnp.float32)
    sent = packed.at[pl.ds(0, devices - 1)]
    return pltpu.make_async_copy(sent, sent, out_sem)


def gather_rows(torus, volume_ref, next_ref, send_a, recv_a, send_b, recv_b):
    axes = ("x", "y")
    steps = (1, -1)
    rows = next_ref.shape[4]
    for c in range(2):
        for half in range(2):
            first = (2 * c + half) * rows
            next_ref[torus.at["y"], torus.at["x"], c, half] = volume_ref[
                first : first + rows
            ].astype(jnp.bfloat16)

    def spot(c, back1, back2, half=None):
        along = lax.rem(torus.at[axes[c]] + back1 + SIDE, SIDE)
        across = lax.rem(torus.at[axes[1 - c]] + back2 + SIDE, SIDE)
        y, x = (across, along) if c == 0 else (along, across)
        return next_ref.at[y, x, c] if half is None else next_ref.at[y, x, c, half]

    def copy(where, axis, step, send, recv):
        return pltpu.make_async_remote_copy(
            src_ref=where,
            dst_ref=where,
            send_sem=send,
            recv_sem=recv,
            device_id=torus.neighbour(axis, step),
            device_id_type=MESH,
        )

    def first_a(c, way):
        return copy(spot(c, 0, 0), axes[c], steps[way], send_a.at[0, c, way], recv_a.at[0, c, way])

    def second_a(c, way):
        where = spot(c, -steps[way], 0, way)
        return copy(where, axes[c], steps[way], send_a.at[1, c, way], recv_a.at[1, c, way])

    def first_b(c, j, way):
        where = spot(c, (0, -1, 1, 2)[j], 0)
        return copy(
            where, axes[1 - c], steps[way], send_b.at[0, c, j, way], recv_b.at[0, c, j, way]
        )

    def second_b(c, j, way):
        where = spot(c, (0, -1, 1, 2)[j], -steps[way], way)
        return copy(
            where, axes[1 - c], steps[way], send_b.at[1, c, j, way], recv_b.at[1, c, j, way]
        )

    both = range(2)
    for c in both:
        for way in both:
            first_a(c, way).start()
    for c in both:
        for way in both:
            first_b(c, 0, way).start()
    for way in both:
        for c in both:
            first_a(c, way).wait_recv()
            second_a(c, way).start()
            for out in both:
                first_b(c, 1 + way, out).start()

    def forward(j):
        for c in both:
            for way in both:
                first_b(c, j, way).wait_recv()
                second_b(c, j, way).start()

    forward(0)
    for c in both:
        for way in both:
            second_a(c, way).wait_recv()
        for out in both:
            first_b(c, 3, out).start()
    for j in range(1, SIDE):
        forward(j)
    for j in range(SIDE):
        for c in both:
            for way in both:
                second_b(c, j, way).wait_recv()
    for c in both:
        for way in both:
            first_a(c, way).wait_send()
            second_a(c, way).wait_send()
            for j in range(SIDE):
                first_b(c, j, way).wait_send()
                second_b(c, j, way).wait_send()


def project_kernel(
    x_ref, r_ref, noise_ref, blocks_ref, dest_ref, row_ref, part_ref, slot_ref,
    volume_ref, next_ref,
    images, scores, raw_x, raw_r, weighted, post, chosen, row_at, part_at, insert, pieces, *rest
):
    x_sem, r_sem = rest[:2]
    post_scratch = rest[2:7]
    counts, rows_at, parts_at = rest[7:10]
    post_sems = rest[10:18]
    sum_scratch = rest[18:25]
    insert_scratch = rest[25:30]
    gather_sems = rest[30:]
    torus = Torus()
    column = Column()
    me = column.dom * column.slabs + column.slab
    barrier = pltpu.get_barrier_semaphore()
    others = [column.mate] + [column.peer(step) for step in range(1, column.chips)]
    others = others + [torus.neighbour(axis, sign) for axis, sign in ROUTES]
    for device in others:
        pl.semaphore_signal(barrier, inc=1, device_id=device, device_id_type=MESH)
    both = blocks_ref[...].astype(jnp.float32)
    half = chosen.shape[1] // 2
    both = jnp.concatenate([both[0:1]] * half + [both[1:2]] * half, axis=0)
    chosen[...] = both.T
    partial_scores(x_ref, r_ref, noise_ref, images, scores, raw_x, raw_r, weighted, x_sem, r_sem)
    pl.semaphore_wait(barrier, len(others))

    def tables():
        slot_tables(dest_ref, row_ref, part_ref, me, counts, rows_at, parts_at, row_at, part_at)

    def weights():
        insertion_weights(row_at, part_at, insert)

    posteriors(column, scores, chosen, post, tables, weights, *post_scratch, *post_sems)
    sum_over_dom(torus, images, post, pieces, *sum_scratch)
    sent = insert_pieces(torus, pieces, slot_ref, insert, volume_ref, *insert_scratch)
    gather_rows(torus, volume_ref, next_ref, *gather_sems)
    sent.wait()


def project(particles, references, inv_noise, blocks, destination, row_index, fraction, slot, doms, slabs):
    count, groups, width = particles.shape
    orients = references.shape[0]
    share = orients // doms
    chips = slabs // 2
    part = count // slabs
    devices = doms * slabs
    routes = len(ROUTES)
    hops = SIDE - 1
    piece = (groups // (routes * CHUNKS), share, width)
    vmem = pl.BlockSpec(memory_space=pltpu.VMEM)
    hbm = pl.BlockSpec(memory_space=pl.ANY)
    dma = pltpu.SemaphoreType.DMA
    table = pltpu.VMEM((doms, slabs * CAP), jnp.float32)
    return pl.pallas_call(
        project_kernel,
        out_shape=(
            jax.ShapeDtypeStruct((RD, width), jnp.float32),
            jax.ShapeDtypeStruct((SIDE, SIDE, 2, 2, RD // 4, width), jnp.bfloat16),
        ),
        in_specs=[hbm, hbm, pl.BlockSpec(memory_space=pltpu.SMEM)] + [vmem] * 5,
        out_specs=(vmem, vmem),
        scratch_shapes=[
            pltpu.VMEM((groups, count, width), jnp.bfloat16),
            pltpu.VMEM((count, orients), jnp.float32),
            pltpu.VMEM((2, count, TILE, width), jnp.bfloat16),
            pltpu.VMEM((2, orients, TILE, width), jnp.bfloat16),
            pltpu.VMEM((TILE, orients, width), jnp.bfloat16),
            pltpu.VMEM((orients, count), jnp.bfloat16),
            pltpu.VMEM((count, 8), jnp.float32),
            table,
            table,
            pltpu.VMEM((2, RD, devices * CAP), jnp.bfloat16),
            pltpu.VMEM((groups, share, width), jnp.bfloat16),
            dma((2,)),
            dma((2,)),
            pltpu.VMEM((2, chips, part, 2 * OB), jnp.float32),
            pltpu.VMEM((chips, part, 2 * OB), jnp.float32),
            pltpu.VMEM((chips, part, 2 * OB), jnp.float32),
            pltpu.VMEM((chips - 1, part, 2 * OB), jnp.float32),
            pltpu.VMEM((chips, 2, part, 2 * OB), jnp.bfloat16),
            pltpu.VMEM((2,) + destination.shape, jnp.float32),
            pltpu.VMEM((slabs * CAP, orients), jnp.float32),
            pltpu.VMEM((slabs * CAP, orients), jnp.float32),
            dma,
            dma,
            dma((chips - 1,)),
            dma((chips - 1,)),
            dma((chips - 1,)),
            dma((chips - 1,)),
            dma,
            dma,
            pltpu.VMEM((routes, CHUNKS, SIDE, SIDE) + piece, jnp.bfloat16),
            pltpu.VMEM((routes, hops, CHUNKS, SIDE) + piece, jnp.bfloat16),
            pltpu.VMEM((routes, hops, CHUNKS) + piece, jnp.bfloat16),
            dma((routes, hops, CHUNKS)),
            dma((routes, hops, CHUNKS)),
            dma((routes, hops, CHUNKS)),
            dma((routes, hops, CHUNKS)),
            pltpu.VMEM((devices, CAP, width), jnp.bfloat16),
            pltpu.VMEM((devices, CAP, width), jnp.bfloat16),
            dma,
            dma,
            dma,
            dma((2, 2, 2)),
            dma((2, 2, 2)),
            dma((2, 2, SIDE, 2)),
            dma((2, 2, SIDE, 2)),
        ],
        compiler_params=pltpu.CompilerParams(
            collective_id=0, has_side_effects=True, vmem_limit_bytes=60 * 1024 * 1024
        ),
        name="project",
    )(particles, references, inv_noise, blocks.T, destination, row_index, fraction, slot)


def send_slots(dests, devices):
    count = dests.shape[0]
    onehot = dests[:, None] == jnp.arange(devices, dtype=jnp.int32)[None, :]
    place = jnp.arange(count, dtype=jnp.int32)
    before = (place[None, :] < place[:, None]).astype(jnp.bfloat16)
    counts = jnp.dot(before, onehot.astype(jnp.bfloat16), preferred_element_type=jnp.float32)
    rank = jnp.sum(jnp.where(onehot, counts, 0.0), axis=1).astype(jnp.int32)
    return dests * CAP + rank


def shards(particles, blocks, references, inv_noise, destination, row_index, fraction):
    _, groups, row_width = particles.shape
    orients = references.shape[0]
    dom_size = lax.axis_size("dom")
    slab_size = lax.axis_size("slab")
    devices = dom_size * slab_size
    dom_pos = lax.axis_index("dom")
    slab_pos = lax.axis_index("slab")
    share = orients // dom_size
    my_dest = lax.dynamic_slice(
        destination, (slab_pos * groups, dom_pos * share), (groups, share)
    )
    slot = send_slots(my_dest.reshape(-1), devices)
    volume, next_slab = project(
        particles, references, inv_noise, blocks, destination, row_index, fraction,
        slot[None, :], dom_size, slab_size,
    )
    next_slab = next_slab.reshape(dom_size * RD, row_width)
    return (volume, next_slab)


def solution(mesh):
    return jax.shard_map(
        shards,
        mesh=mesh,
        in_specs=(
            P("dom", "slab", None),
            P("dom", None),
            P(None, "slab", None),
            P("slab"),
            P(),
            P(),
            P(),
        ),
        out_specs=(P(("dom", "slab"), None), P(None, "slab")),
        check_vma=False,
    )
```

```python
import functools

import jax
import jax.numpy as jnp
from jax import lax
from jax.experimental import pallas as pl
from jax.experimental.pallas import tpu as pltpu
from jax.sharding import PartitionSpec as P

MESH = pl.DeviceIdType.MESH
OB = 128
RD = 256
CAP = 16
SIDE = 4
CHUNKS = 5
VMEM_MIB = 56
TILE = 8
ROWS = 32
BAND = 256
ROUTES = (("x", 1), ("x", -1), ("y", 1), ("y", -1))


class Torus:
    def __init__(self):
        dom = lax.axis_index("dom")
        self.slab = lax.axis_index("slab")
        self.at = {"y": lax.div(dom, SIDE), "x": lax.rem(dom, SIDE)}

    def neighbour(self, axis, step):
        at = dict(self.at)
        at[axis] = lax.rem(at[axis] + step + SIDE, SIDE)
        return (at["y"] * SIDE + at["x"], self.slab)


def other(axis):
    return "y" if axis == "x" else "x"


def held(torus, q):
    return lax.rem(torus.at[other(ROUTES[q][0])], 2)


def partner(torus, q):
    axis, sign = ROUTES[q]
    return torus.neighbour(other(axis), sign * (1 - 2 * held(torus, q)))


def group_of(q, i, which):
    return (i * len(ROUTES) + q) * 2 + which


def partial_scores(x_ref, r_ref, noise_ref, images, scores, begin, ready, raw_x, raw_r, weighted, x_sem, r_sem):
    particles, groups, _ = x_ref.shape
    orients = r_ref.shape[0]
    tile = raw_x.shape[2]
    tiles = groups // tile
    over_lanes = (((1,), (1,)), ((), ()))

    def fetch(ref, raw, sem, t):
        slot = lax.rem(t, 2)
        groups_of = pl.ds(pl.multiple_of(t * tile, tile), tile)
        return pltpu.make_async_copy(ref.at[:, groups_of], raw.at[slot], sem.at[slot])

    def start(t):
        fetch(x_ref, raw_x, x_sem, t).start()
        fetch(r_ref, raw_r, r_sem, t).start()

    start(0)
    start(1)
    begin()
    scores[...] = jnp.zeros_like(scores)

    @pl.loop(0, tiles)
    def _(t):
        slot = lax.rem(t, 2)
        first = t * tile
        fetch(x_ref, raw_x, x_sem, t).wait()

        @pl.loop(0, particles // ROWS)
        def _(b):
            span = pl.ds(pl.multiple_of(b * ROWS, ROWS), ROWS)
            images[pl.ds(first, tile), span] = jnp.swapaxes(raw_x[slot, span], 0, 1)

        fetch(r_ref, raw_r, r_sem, t).wait()

        @pl.loop(0, orients // ROWS)
        def _(b):
            span = pl.ds(pl.multiple_of(b * ROWS, ROWS), ROWS)
            value = jnp.swapaxes(raw_r[slot, span], 0, 1)
            for g in range(tile):
                scaled = value[g].astype(jnp.float32) * noise_ref[first + g]
                weighted[g, span] = scaled.astype(jnp.bfloat16)

        @pl.when(t + 2 < tiles)
        def _():
            start(t + 2)

        ready(t)

        for m in range(0, particles, BAND):
            acc = scores[m : m + BAND]
            for g in range(tile):
                acc = acc + lax.dot_general(
                    images[first + g, m : m + BAND], weighted[g], over_lanes,
                    preferred_element_type=jnp.float32,
                )
            scores[m : m + BAND] = acc


def slot_tables(dest_ref, row_ref, part_ref, me, counts, rows_at, parts_at, row_out, part_out):
    slabs = lax.axis_size("slab")
    orients = dest_ref.shape[1]
    groups = dest_ref.shape[0] // slabs
    doms = row_out.shape[0]
    shift = (orients // doms).bit_length() - 1
    here = lax.broadcasted_iota(jnp.int32, (orients, orients), 0)
    there = lax.broadcasted_iota(jnp.int32, (orients, orients), 1)
    same = lax.shift_right_logical(here, shift) == lax.shift_right_logical(there, shift)
    share = same.astype(jnp.float32).astype(jnp.bfloat16)
    before = jnp.where(same & (here < there), 1.0, 0.0).astype(jnp.bfloat16)
    mask = (dest_ref[...] == me).astype(jnp.float32).astype(jnp.bfloat16)
    counts[0] = jnp.dot(mask, before, preferred_element_type=jnp.float32)
    counts[1] = jnp.dot(mask, share, preferred_element_type=jnp.float32)
    lower = lax.broadcasted_iota(jnp.int32, (groups, groups), 0) > lax.broadcasted_iota(
        jnp.int32, (groups, groups), 1
    )
    lower = lower.astype(jnp.float32).astype(jnp.bfloat16)

    @pl.loop(0, slabs)
    def _(s):
        span = pl.ds(pl.multiple_of(s * groups, groups), groups)
        above = jnp.dot(
            lower, counts[1, span].astype(jnp.bfloat16), preferred_element_type=jnp.float32
        )
        rank = jnp.where(dest_ref[span] == me, counts[0, span] + above, -1.0)
        row = row_ref[span].astype(jnp.float32) + 1.0
        part = part_ref[span]
        found_rows = []
        found_parts = []
        for j in range(CAP):
            chosen = rank == j
            found_rows.append(jnp.sum(jnp.where(chosen, row, 0.0), axis=0, keepdims=True))
            found_parts.append(jnp.sum(jnp.where(chosen, part, 0.0), axis=0, keepdims=True))
        slots = pl.ds(pl.multiple_of(s * CAP, CAP), CAP)
        rows_at[slots] = jnp.concatenate(found_rows, axis=0)
        parts_at[slots] = jnp.concatenate(found_parts, axis=0)

    owner = lax.shift_right_logical(lax.broadcasted_iota(jnp.int32, (doms, orients), 1), shift)
    gather = (owner == lax.broadcasted_iota(jnp.int32, (doms, orients), 0)).astype(jnp.float32)
    over_lanes = (((1,), (1,)), ((), ()))
    for found, out in ((rows_at, row_out), (parts_at, part_out)):
        out[...] = lax.dot_general(
            gather, found[...], over_lanes,
            precision=lax.Precision.HIGHEST, preferred_element_type=jnp.float32,
        )
    row_out[...] = row_out[...] - 1.0


def spread(compact, blocks, post_ref):
    values = compact[...].astype(jnp.float32)
    half = blocks.shape[0] // 2
    first, second = blocks[0:1], blocks[half : half + 1]
    for b in range(post_ref.shape[0] // OB):
        value = jnp.where(first == b, values[:OB], 0.0)
        value = jnp.where(second == b, values[OB:], value)
        post_ref[b * OB : (b + 1) * OB] = value.astype(jnp.bfloat16)


class Column:
    def __init__(self):
        self.dom = lax.axis_index("dom")
        self.slab = lax.axis_index("slab")
        self.slabs = lax.axis_size("slab")
        self.chips = self.slabs // 2
        self.chip = lax.div(self.slab, 2)
        self.core = lax.rem(self.slab, 2)
        self.mate = (self.dom, 2 * self.chip + 1 - self.core)

    def peer(self, step):
        return (self.dom, 2 * lax.rem(self.chip + step, self.chips) + self.core)


def posteriors(
    column, scores_ref, chosen_ref, own_blocks, compact, post_ref, meanwhile, afterwards, done,
    mine, from_mate, total, from_chips, found,
    mate_send, mate_recv, chip_send, chip_recv, back_send, back_recv, last_send, last_recv,
):
    slabs, chips, chip, core = column.slabs, column.chips, column.chip, column.core
    mate, peer = column.mate, column.peer
    count = mine.shape[2]

    def picked(span, which):
        chosen = chosen_ref[span, SIDE * which : SIDE * which + 1]
        value = scores_ref[span, 0:OB]
        for b in range(1, scores_ref.shape[1] // OB):
            value = jnp.where(chosen == b, scores_ref[span, b * OB : (b + 1) * OB], value)
        return value

    for s in range(slabs):
        span = pl.ds(s * count, count)
        for which in range(2):
            mine[s % 2, s // 2, :, which * OB : (which + 1) * OB] = picked(span, which)
    to_mate = pltpu.make_async_remote_copy(
        src_ref=mine.at[1 - core],
        dst_ref=from_mate,
        send_sem=mate_send,
        recv_sem=mate_recv,
        device_id=mate,
        device_id_type=MESH,
    )
    to_mate.start()
    to_mate.wait_recv()
    total[...] = mine[core] + from_mate[...]

    def to_chip(step):
        return pltpu.make_async_remote_copy(
            src_ref=total.at[lax.rem(chip + step, chips)],
            dst_ref=from_chips.at[step - 1],
            send_sem=chip_send.at[step - 1],
            recv_sem=chip_recv.at[step - 1],
            device_id=peer(step),
            device_id_type=MESH,
        )

    for step in range(1, chips):
        to_chip(step).start()
    meanwhile()
    for step in range(1, chips):
        to_chip(step).wait_recv()
    scores = total[chip]
    for step in range(1, chips):
        scores = scores + from_chips[step - 1]
    weights = jnp.exp(scores - jnp.max(scores, axis=1, keepdims=True))
    found[chip, core] = (weights / jnp.sum(weights, axis=1, keepdims=True)).astype(jnp.bfloat16)

    def back(step):
        return pltpu.make_async_remote_copy(
            src_ref=found.at[chip, core],
            dst_ref=found.at[chip, core],
            send_sem=back_send.at[step - 1],
            recv_sem=back_recv.at[step - 1],
            device_id=peer(step),
            device_id_type=MESH,
        )

    for step in range(1, chips):
        back(step).start()
    afterwards()
    for step in range(1, chips):
        back(step).wait_recv()
    last = pltpu.make_async_remote_copy(
        src_ref=found.at[:, core],
        dst_ref=found.at[:, core],
        send_sem=last_send,
        recv_sem=last_recv,
        device_id=mate,
        device_id_type=MESH,
    )
    last.start()
    last.wait_recv()
    everyone = found[...].astype(jnp.float32).reshape(slabs * count, 2 * OB)
    compact[...] = everyone.T.astype(jnp.bfloat16)
    done()
    spread(compact, own_blocks, post_ref)
    to_mate.wait_send()
    last.wait_send()
    for step in range(1, chips):
        to_chip(step).wait_send()
        back(step).wait_send()


def sum_over_dom(
    torus, images, post_ref, swapped, other_post, other_ready, swap, out_ref,
    partial, got1, got2, send1, recv1, send2, recv2,
):
    share = out_ref.shape[1]
    last = SIDE - 2
    steps = (1, -1, 2)

    def hop1(q, hop, i):
        axis, sign = ROUTES[q]
        block = lax.rem(torus.at[axis] - sign + SIDE, SIDE)
        source = partial.at[q, i, block] if hop == 0 else got1.at[q, hop - 1, i]
        return pltpu.make_async_remote_copy(
            src_ref=source,
            dst_ref=got1.at[q, hop, i],
            send_sem=send1.at[q, hop, i],
            recv_sem=recv1.at[q, hop, i],
            device_id=torus.neighbour(axis, sign),
            device_id_type=MESH,
        )

    def hop2(q, k, i):
        axis = other(ROUTES[q][0])
        block = lax.rem(torus.at[axis] + steps[k] + SIDE, SIDE)
        return pltpu.make_async_remote_copy(
            src_ref=got1.at[q, last, i, block],
            dst_ref=got2.at[q, k, i],
            send_sem=send2.at[q, k, i],
            recv_sem=recv2.at[q, k, i],
            device_id=torus.neighbour(axis, steps[k]),
            device_id_type=MESH,
        )

    def added(a, b):
        return (a.astype(jnp.float32) + b.astype(jnp.float32)).astype(jnp.bfloat16)

    routes = range(len(ROUTES))
    for q in routes:
        other_ready(q)

    @pl.loop(0, CHUNKS)
    def _(i):
        for q in routes:
            swap(q, i).wait_recv()
            value = jnp.dot(
                post_ref[...], images[group_of(q, i, held(torus, q))], preferred_element_type=jnp.float32
            )
            value = value + jnp.dot(other_post[q], swapped[q, i], preferred_element_type=jnp.float32)
            value = value.astype(jnp.bfloat16)
            for yy in range(SIDE):
                for xx in range(SIDE):
                    first, second = (xx, yy) if ROUTES[q][0] == "x" else (yy, xx)
                    begin = (yy * SIDE + xx) * share
                    partial[q, i, first, second] = value[begin : begin + share]
            hop1(q, 0, i).start()

    for hop in range(SIDE - 1):

        @pl.loop(0, CHUNKS)
        def _(i):
            for q in routes:
                axis, sign = ROUTES[q]
                block = lax.rem(torus.at[axis] - sign * (2 + hop) + 2 * SIDE, SIDE)
                hop1(q, hop, i).wait_recv()
                got1[q, hop, i] = added(got1[q, hop, i], partial[q, i, block])
                if hop < last:
                    hop1(q, hop + 1, i).start()
                else:
                    for k in range(len(steps)):
                        hop2(q, k, i).start()

    @pl.loop(0, CHUNKS)
    def _(i):
        for q in routes:
            for k in range(len(steps)):
                hop2(q, k, i).wait_recv()
            kept = held(torus, q)
            mine = got1[q, last, i, torus.at[other(ROUTES[q][0])]]
            out_ref[group_of(q, i, kept)] = added(got2[q, 2, i], mine)
            out_ref[group_of(q, i, 1 - kept)] = added(got2[q, 0, i], got2[q, 1, i])

    @pl.loop(0, CHUNKS)
    def _(i):
        for q in routes:
            swap(q, i).wait_send()
            for hop in range(SIDE - 1):
                hop1(q, hop, i).wait_send()
                hop2(q, hop, i).wait_send()


def insertion_weights(row_ref, part_ref, insert):
    lanes = row_ref.shape[1]
    rows = lax.broadcasted_iota(jnp.int32, (RD, lanes), 0).astype(jnp.float32)
    for b in range(row_ref.shape[0]):
        row = row_ref[b : b + 1, :]
        part = part_ref[b : b + 1, :]
        weight = jnp.where(rows == row, 1.0 - part, 0.0) + jnp.where(rows == row + 1, part, 0.0)
        high = weight.astype(jnp.bfloat16)
        insert[0, :, b * lanes : (b + 1) * lanes] = high
        insert[1, :, b * lanes : (b + 1) * lanes] = (weight - high.astype(jnp.float32)).astype(jnp.bfloat16)


def insert_pieces(torus, pieces_ref, slot_ref, insert, volume_ref, packed, got, own_sem, out_sem, in_sem):
    slabs = lax.axis_size("slab")
    devices = lax.axis_size("dom") * slabs
    me = (torus.at["y"] * SIDE + torus.at["x"]) * slabs + torus.slab
    width = pieces_ref.shape[2]
    count = pieces_ref.shape[0] * pieces_ref.shape[1]
    block = RD
    owners = block // CAP
    numbers = lax.broadcasted_iota(jnp.int32, (block, count), 0)
    pieces = pieces_ref[...].reshape(count, width)

    @pl.loop(0, devices // owners)
    def _(k):
        b = lax.rem(lax.div(me, owners) + k, devices // owners)
        first = b * owners
        pick = (numbers + b * block == slot_ref[...]).astype(jnp.float32).astype(jnp.bfloat16)
        value = jnp.dot(pick, pieces, preferred_element_type=jnp.float32)
        packed[pl.ds(first, owners)] = value.astype(jnp.bfloat16).reshape(owners, CAP, width)

        @pl.loop(0, owners)
        def _(j):
            to = first + lax.rem(me + j, owners)

            @pl.when(to != me)
            def _():
                pltpu.make_async_remote_copy(
                    src_ref=packed.at[to],
                    dst_ref=got.at[me],
                    send_sem=out_sem,
                    recv_sem=in_sem,
                    device_id=(lax.div(to, slabs), lax.rem(to, slabs)),
                    device_id_type=MESH,
                ).start()

    own = pltpu.make_async_copy(packed.at[me], got.at[me], own_sem)
    own.start()
    own.wait()
    others = got.at[pl.ds(0, devices - 1)]
    pltpu.make_async_copy(others, others, in_sem).wait()
    received = got[...].reshape(devices * CAP, width)
    volume = jnp.dot(insert[0], received, preferred_element_type=jnp.float32)
    volume_ref[...] = volume + jnp.dot(insert[1], received, preferred_element_type=jnp.float32)
    sent = packed.at[pl.ds(0, devices - 1)]
    return pltpu.make_async_copy(sent, sent, out_sem)


def gather_rows(torus, volume_ref, next_ref, send_a, recv_a, send_b, recv_b):
    axes = ("x", "y")
    steps = (1, -1)
    rows = next_ref.shape[4]
    for c in range(2):
        for half in range(2):
            first = (2 * c + half) * rows
            next_ref[torus.at["y"], torus.at["x"], c, half] = volume_ref[
                first : first + rows
            ].astype(jnp.bfloat16)

    def spot(c, back1, back2, half=None):
        along = lax.rem(torus.at[axes[c]] + back1 + SIDE, SIDE)
        across = lax.rem(torus.at[axes[1 - c]] + back2 + SIDE, SIDE)
        y, x = (across, along) if c == 0 else (along, across)
        return next_ref.at[y, x, c] if half is None else next_ref.at[y, x, c, half]

    def copy(where, axis, step, send, recv):
        return pltpu.make_async_remote_copy(
            src_ref=where,
            dst_ref=where,
            send_sem=send,
            recv_sem=recv,
            device_id=torus.neighbour(axis, step),
            device_id_type=MESH,
        )

    def first_a(c, way):
        return copy(spot(c, 0, 0), axes[c], steps[way], send_a.at[0, c, way], recv_a.at[0, c, way])

    def second_a(c, way):
        where = spot(c, -steps[way], 0, way)
        return copy(where, axes[c], steps[way], send_a.at[1, c, way], recv_a.at[1, c, way])

    def first_b(c, j, way):
        where = spot(c, (0, -1, 1, 2)[j], 0)
        return copy(
            where, axes[1 - c], steps[way], send_b.at[0, c, j, way], recv_b.at[0, c, j, way]
        )

    def second_b(c, j, way):
        where = spot(c, (0, -1, 1, 2)[j], -steps[way], way)
        return copy(
            where, axes[1 - c], steps[way], send_b.at[1, c, j, way], recv_b.at[1, c, j, way]
        )

    both = range(2)
    for c in both:
        for way in both:
            first_a(c, way).start()
    for c in both:
        for way in both:
            first_b(c, 0, way).start()
    for way in both:
        for c in both:
            first_a(c, way).wait_recv()
            second_a(c, way).start()
            for out in both:
                first_b(c, 1 + way, out).start()

    def forward(j):
        for c in both:
            for way in both:
                first_b(c, j, way).wait_recv()
                second_b(c, j, way).start()

    forward(0)
    for c in both:
        for way in both:
            second_a(c, way).wait_recv()
        for out in both:
            first_b(c, 3, out).start()
    for j in range(1, SIDE):
        forward(j)
    for j in range(SIDE):
        for c in both:
            for way in both:
                second_b(c, j, way).wait_recv()
    for c in both:
        for way in both:
            first_a(c, way).wait_send()
            second_a(c, way).wait_send()
            for j in range(SIDE):
                first_b(c, j, way).wait_send()
                second_b(c, j, way).wait_send()


def project_kernel(
    x_ref, r_ref, noise_ref, blocks_ref, dest_ref, row_ref, part_ref, slot_ref,
    volume_ref, next_ref,
    images, scores, raw_x, raw_r, weighted, post, chosen, row_at, part_at, insert, pieces,
    swapped, own_blocks, other_blocks, compact, other_compact, other_post,
    swap_send, swap_recv, block_send, block_recv, compact_send, compact_recv, *rest
):
    x_sem, r_sem = rest[:2]
    post_scratch = rest[2:7]
    counts, rows_at, parts_at = rest[7:10]
    post_sems = rest[10:18]
    sum_scratch = rest[18:25]
    insert_scratch = rest[25:30]
    gather_sems = rest[30:]
    torus = Torus()
    column = Column()
    me = column.dom * column.slabs + column.slab
    barrier = pltpu.get_barrier_semaphore()
    others = [column.mate] + [column.peer(step) for step in range(1, column.chips)]
    others = others + [torus.neighbour(axis, sign) for axis, sign in ROUTES]
    for device in others:
        pl.semaphore_signal(barrier, inc=1, device_id=device, device_id_type=MESH)
    both = blocks_ref[...].astype(jnp.float32)
    half = chosen.shape[1] // 2
    both = jnp.concatenate([both[0:1]] * half + [both[1:2]] * half, axis=0)
    own_blocks[...] = both
    chosen[...] = both.T
    routes = range(len(ROUTES))

    def to_partner(q, source, target, send, recv):
        return pltpu.make_async_remote_copy(
            src_ref=source,
            dst_ref=target,
            send_sem=send,
            recv_sem=recv,
            device_id=partner(torus, q),
            device_id_type=MESH,
        )

    def swap(q, i):
        away = images.at[group_of(q, i, 1 - held(torus, q))]
        return to_partner(q, away, swapped.at[q, i], swap_send.at[q, i], swap_recv.at[q, i])

    def share_blocks(q):
        return to_partner(q, own_blocks, other_blocks.at[q], block_send.at[q], block_recv.at[q])

    def share_post(q):
        return to_partner(q, compact, other_compact.at[q], compact_send.at[q], compact_recv.at[q])

    def begin():
        pl.semaphore_wait(barrier, len(others))
        for q in routes:
            share_blocks(q).start()

    def ready(t):
        for q in routes:
            swap(q, t).start()

    def done():
        for q in routes:
            share_post(q).start()

    def other_ready(q):
        share_blocks(q).wait_recv()
        share_post(q).wait_recv()
        spread(other_compact.at[q], other_blocks.at[q], other_post.at[q])

    partial_scores(
        x_ref, r_ref, noise_ref, images, scores, begin, ready, raw_x, raw_r, weighted, x_sem, r_sem
    )

    def tables():
        slot_tables(dest_ref, row_ref, part_ref, me, counts, rows_at, parts_at, row_at, part_at)

    def weights():
        insertion_weights(row_at, part_at, insert)

    posteriors(
        column, scores, chosen, own_blocks, compact, post, tables, weights, done,
        *post_scratch, *post_sems,
    )
    sum_over_dom(torus, images, post, swapped, other_post, other_ready, swap, pieces, *sum_scratch)
    sent = insert_pieces(torus, pieces, slot_ref, insert, volume_ref, *insert_scratch)
    gather_rows(torus, volume_ref, next_ref, *gather_sems)
    sent.wait()
    for q in routes:
        share_blocks(q).wait_send()
        share_post(q).wait_send()


def project(particles, references, inv_noise, blocks, destination, row_index, fraction, slot, doms, slabs):
    count, groups, width = particles.shape
    orients = references.shape[0]
    share = orients // doms
    chips = slabs // 2
    part = count // slabs
    devices = doms * slabs
    routes = len(ROUTES)
    hops = SIDE - 1
    piece = (share, width)
    vmem = pl.BlockSpec(memory_space=pltpu.VMEM)
    hbm = pl.BlockSpec(memory_space=pl.ANY)
    dma = pltpu.SemaphoreType.DMA
    table = pltpu.VMEM((doms, slabs * CAP), jnp.float32)
    return pl.pallas_call(
        project_kernel,
        out_shape=(
            jax.ShapeDtypeStruct((RD, width), jnp.float32),
            jax.ShapeDtypeStruct((SIDE, SIDE, 2, 2, RD // 4, width), jnp.bfloat16),
        ),
        in_specs=[hbm, hbm, pl.BlockSpec(memory_space=pltpu.SMEM)] + [vmem] * 5,
        out_specs=(vmem, vmem),
        scratch_shapes=[
            pltpu.VMEM((groups, count, width), jnp.bfloat16),
            pltpu.VMEM((count, orients), jnp.float32),
            pltpu.VMEM((2, count, TILE, width), jnp.bfloat16),
            pltpu.VMEM((2, orients, TILE, width), jnp.bfloat16),
            pltpu.VMEM((TILE, orients, width), jnp.bfloat16),
            pltpu.VMEM((orients, count), jnp.bfloat16),
            pltpu.VMEM((count, 8), jnp.float32),
            table,
            table,
            pltpu.VMEM((2, RD, devices * CAP), jnp.bfloat16),
            pltpu.VMEM((groups, share, width), jnp.bfloat16),
            pltpu.VMEM((routes, CHUNKS, count, width), jnp.bfloat16),
            pltpu.VMEM((8, count), jnp.float32),
            pltpu.VMEM((routes, 8, count), jnp.float32),
            pltpu.VMEM((2 * OB, count), jnp.bfloat16),
            pltpu.VMEM((routes, 2 * OB, count), jnp.bfloat16),
            pltpu.VMEM((routes, orients, count), jnp.bfloat16),
            dma((routes, CHUNKS)),
            dma((routes, CHUNKS)),
            dma((routes,)),
            dma((routes,)),
            dma((routes,)),
            dma((routes,)),
            dma((2,)),
            dma((2,)),
            pltpu.VMEM((2, chips, part, 2 * OB), jnp.float32),
            pltpu.VMEM((chips, part, 2 * OB), jnp.float32),
            pltpu.VMEM((chips, part, 2 * OB), jnp.float32),
            pltpu.VMEM((chips - 1, part, 2 * OB), jnp.float32),
            pltpu.VMEM((chips, 2, part, 2 * OB), jnp.bfloat16),
            pltpu.VMEM((2,) + destination.shape, jnp.float32),
            pltpu.VMEM((slabs * CAP, orients), jnp.float32),
            pltpu.VMEM((slabs * CAP, orients), jnp.float32),
            dma,
            dma,
            dma((chips - 1,)),
            dma((chips - 1,)),
            dma((chips - 1,)),
            dma((chips - 1,)),
            dma,
            dma,
            pltpu.VMEM((routes, CHUNKS, SIDE, SIDE) + piece, jnp.bfloat16),
            pltpu.VMEM((routes, hops, CHUNKS, SIDE) + piece, jnp.bfloat16),
            pltpu.VMEM((routes, hops, CHUNKS) + piece, jnp.bfloat16),
            dma((routes, hops, CHUNKS)),
            dma((routes, hops, CHUNKS)),
            dma((routes, hops, CHUNKS)),
            dma((routes, hops, CHUNKS)),
            pltpu.VMEM((devices, CAP, width), jnp.bfloat16),
            pltpu.VMEM((devices, CAP, width), jnp.bfloat16),
            dma,
            dma,
            dma,
            dma((2, 2, 2)),
            dma((2, 2, 2)),
            dma((2, 2, SIDE, 2)),
            dma((2, 2, SIDE, 2)),
        ],
        compiler_params=pltpu.CompilerParams(
            collective_id=0, has_side_effects=True, vmem_limit_bytes=VMEM_MIB * 1024 * 1024
        ),
        name="project",
    )(particles, references, inv_noise, blocks.T, destination, row_index, fraction, slot)


def send_slots(dests, devices):
    count = dests.shape[0]
    onehot = dests[:, None] == jnp.arange(devices, dtype=jnp.int32)[None, :]
    place = jnp.arange(count, dtype=jnp.int32)
    before = (place[None, :] < place[:, None]).astype(jnp.bfloat16)
    counts = jnp.dot(before, onehot.astype(jnp.bfloat16), preferred_element_type=jnp.float32)
    rank = jnp.sum(jnp.where(onehot, counts, 0.0), axis=1).astype(jnp.int32)
    return dests * CAP + rank


def shards(particles, blocks, references, inv_noise, destination, row_index, fraction):
    _, groups, row_width = particles.shape
    orients = references.shape[0]
    dom_size = lax.axis_size("dom")
    slab_size = lax.axis_size("slab")
    devices = dom_size * slab_size
    dom_pos = lax.axis_index("dom")
    slab_pos = lax.axis_index("slab")
    share = orients // dom_size
    my_dest = lax.dynamic_slice(
        destination, (slab_pos * groups, dom_pos * share), (groups, share)
    )
    slot = send_slots(my_dest.reshape(-1), devices)
    volume, next_slab = project(
        particles, references, inv_noise, blocks, destination, row_index, fraction,
        slot[None, :], dom_size, slab_size,
    )
    next_slab = next_slab.reshape(dom_size * RD, row_width)
    return (volume, next_slab)


def solution(mesh):
    return jax.shard_map(
        shards,
        mesh=mesh,
        in_specs=(
            P("dom", "slab", None),
            P("dom", None),
            P(None, "slab", None),
            P("slab"),
            P(),
            P(),
            P(),
        ),
        out_specs=(P(("dom", "slab"), None), P(None, "slab")),
        check_vma=False,
    )
```

```python
import functools

import jax
import jax.numpy as jnp
from jax import lax
from jax.experimental import pallas as pl
from jax.experimental.pallas import tpu as pltpu
from jax.sharding import PartitionSpec as P

MESH = pl.DeviceIdType.MESH
OB = 128
RD = 256
CAP = 16
SIDE = 4
CHUNKS = 5
VMEM_MIB = 49
LATE = 1
TILE = 8
ROWS = 32
BAND = 256
ROUTES = (("x", 1), ("x", -1), ("y", 1), ("y", -1))


class Torus:
    def __init__(self):
        dom = lax.axis_index("dom")
        self.slab = lax.axis_index("slab")
        self.at = {"y": lax.div(dom, SIDE), "x": lax.rem(dom, SIDE)}

    def neighbour(self, axis, step):
        at = dict(self.at)
        at[axis] = lax.rem(at[axis] + step + SIDE, SIDE)
        return (at["y"] * SIDE + at["x"], self.slab)


def other(axis):
    return "y" if axis == "x" else "x"


def held(torus, q):
    return lax.rem(torus.at[other(ROUTES[q][0])], 2)


def partner(torus, q):
    axis, sign = ROUTES[q]
    return torus.neighbour(other(axis), sign * (1 - 2 * held(torus, q)))


def group_of(q, i, which):
    return (i * len(ROUTES) + q) * 2 + which


def partial_scores(x_ref, r_ref, noise_ref, images, scores, begin, ready, raw_x, raw_r, weighted, x_sem, r_sem):
    particles, groups, _ = x_ref.shape
    orients = r_ref.shape[0]
    tile = raw_x.shape[2]
    tiles = groups // tile
    over_lanes = (((1,), (1,)), ((), ()))

    def fetch(ref, raw, sem, t):
        slot = lax.rem(t, 2)
        groups_of = pl.ds(pl.multiple_of(t * tile, tile), tile)
        return pltpu.make_async_copy(ref.at[:, groups_of], raw.at[slot], sem.at[slot])

    def start(t):
        fetch(x_ref, raw_x, x_sem, t).start()
        fetch(r_ref, raw_r, r_sem, t).start()

    start(0)
    start(1)
    begin()
    scores[...] = jnp.zeros_like(scores)

    @pl.loop(0, tiles)
    def _(t):
        slot = lax.rem(t, 2)
        first = t * tile
        fetch(x_ref, raw_x, x_sem, t).wait()

        @pl.loop(0, particles // ROWS)
        def _(b):
            span = pl.ds(pl.multiple_of(b * ROWS, ROWS), ROWS)
            images[pl.ds(first, tile), span] = jnp.swapaxes(raw_x[slot, span], 0, 1)

        fetch(r_ref, raw_r, r_sem, t).wait()

        @pl.loop(0, orients // ROWS)
        def _(b):
            span = pl.ds(pl.multiple_of(b * ROWS, ROWS), ROWS)
            value = jnp.swapaxes(raw_r[slot, span], 0, 1)
            for g in range(tile):
                scaled = value[g].astype(jnp.float32) * noise_ref[first + g]
                weighted[g, span] = scaled.astype(jnp.bfloat16)

        @pl.when(t + 2 < tiles)
        def _():
            start(t + 2)

        ready(t)

        for m in range(0, particles, BAND):
            acc = scores[m : m + BAND]
            for g in range(tile):
                acc = acc + lax.dot_general(
                    images[first + g, m : m + BAND], weighted[g], over_lanes,
                    preferred_element_type=jnp.float32,
                )
            scores[m : m + BAND] = acc


def slot_tables(dest_ref, row_ref, part_ref, me, counts, rows_at, parts_at, row_out, part_out):
    slabs = lax.axis_size("slab")
    orients = dest_ref.shape[1]
    groups = dest_ref.shape[0] // slabs
    doms = row_out.shape[0]
    shift = (orients // doms).bit_length() - 1
    here = lax.broadcasted_iota(jnp.int32, (orients, orients), 0)
    there = lax.broadcasted_iota(jnp.int32, (orients, orients), 1)
    same = lax.shift_right_logical(here, shift) == lax.shift_right_logical(there, shift)
    share = same.astype(jnp.float32).astype(jnp.bfloat16)
    before = jnp.where(same & (here < there), 1.0, 0.0).astype(jnp.bfloat16)
    mask = (dest_ref[...] == me).astype(jnp.float32).astype(jnp.bfloat16)
    counts[0] = jnp.dot(mask, before, preferred_element_type=jnp.float32)
    counts[1] = jnp.dot(mask, share, preferred_element_type=jnp.float32)
    lower = lax.broadcasted_iota(jnp.int32, (groups, groups), 0) > lax.broadcasted_iota(
        jnp.int32, (groups, groups), 1
    )
    lower = lower.astype(jnp.float32).astype(jnp.bfloat16)

    @pl.loop(0, slabs)
    def _(s):
        span = pl.ds(pl.multiple_of(s * groups, groups), groups)
        above = jnp.dot(
            lower, counts[1, span].astype(jnp.bfloat16), preferred_element_type=jnp.float32
        )
        rank = jnp.where(dest_ref[span] == me, counts[0, span] + above, -1.0)
        row = row_ref[span].astype(jnp.float32) + 1.0
        part = part_ref[span]
        found_rows = []
        found_parts = []
        for j in range(CAP):
            chosen = rank == j
            found_rows.append(jnp.sum(jnp.where(chosen, row, 0.0), axis=0, keepdims=True))
            found_parts.append(jnp.sum(jnp.where(chosen, part, 0.0), axis=0, keepdims=True))
        slots = pl.ds(pl.multiple_of(s * CAP, CAP), CAP)
        rows_at[slots] = jnp.concatenate(found_rows, axis=0)
        parts_at[slots] = jnp.concatenate(found_parts, axis=0)

    owner = lax.shift_right_logical(lax.broadcasted_iota(jnp.int32, (doms, orients), 1), shift)
    gather = (owner == lax.broadcasted_iota(jnp.int32, (doms, orients), 0)).astype(jnp.float32)
    over_lanes = (((1,), (1,)), ((), ()))
    for found, out in ((rows_at, row_out), (parts_at, part_out)):
        out[...] = lax.dot_general(
            gather, found[...], over_lanes,
            precision=lax.Precision.HIGHEST, preferred_element_type=jnp.float32,
        )
    row_out[...] = row_out[...] - 1.0


def spread(compact, blocks, post_ref):
    half = blocks.shape[0] // 2
    first, second = blocks[0:1], blocks[half : half + 1]
    for b in range(post_ref.shape[0] // OB):
        value = jnp.where(first == b, compact[0].astype(jnp.float32), 0.0)
        value = jnp.where(second == b, compact[1].astype(jnp.float32), value)
        post_ref[b * OB : (b + 1) * OB] = value.astype(jnp.bfloat16)


class Column:
    def __init__(self):
        self.dom = lax.axis_index("dom")
        self.slab = lax.axis_index("slab")
        self.slabs = lax.axis_size("slab")
        self.chips = self.slabs // 2
        self.chip = lax.div(self.slab, 2)
        self.core = lax.rem(self.slab, 2)
        self.mate = (self.dom, 2 * self.chip + 1 - self.core)

    def peer(self, step):
        return (self.dom, 2 * lax.rem(self.chip + step, self.chips) + self.core)


def posteriors(
    column, scores_ref, chosen_ref, own_blocks, compact, post_ref, meanwhile, afterwards, done,
    mine, from_mate, total, from_chips, found,
    mate_send, mate_recv, chip_send, chip_recv, back_send, back_recv, last_send, last_recv,
):
    slabs, chips, chip, core = column.slabs, column.chips, column.chip, column.core
    mate, peer = column.mate, column.peer
    count = mine.shape[2]

    def picked(span, which):
        chosen = chosen_ref[span, SIDE * which : SIDE * which + 1]
        value = scores_ref[span, 0:OB]
        for b in range(1, scores_ref.shape[1] // OB):
            value = jnp.where(chosen == b, scores_ref[span, b * OB : (b + 1) * OB], value)
        return value

    for s in range(slabs):
        span = pl.ds(s * count, count)
        for which in range(2):
            mine[s % 2, s // 2, :, which * OB : (which + 1) * OB] = picked(span, which)
    to_mate = pltpu.make_async_remote_copy(
        src_ref=mine.at[1 - core],
        dst_ref=from_mate,
        send_sem=mate_send,
        recv_sem=mate_recv,
        device_id=mate,
        device_id_type=MESH,
    )
    to_mate.start()
    to_mate.wait_recv()
    total[...] = mine[core] + from_mate[...]

    def to_chip(step):
        return pltpu.make_async_remote_copy(
            src_ref=total.at[lax.rem(chip + step, chips)],
            dst_ref=from_chips.at[step - 1],
            send_sem=chip_send.at[step - 1],
            recv_sem=chip_recv.at[step - 1],
            device_id=peer(step),
            device_id_type=MESH,
        )

    for step in range(1, chips):
        to_chip(step).start()
    meanwhile()
    for step in range(1, chips):
        to_chip(step).wait_recv()
    scores = total[chip]
    for step in range(1, chips):
        scores = scores + from_chips[step - 1]
    weights = jnp.exp(scores - jnp.max(scores, axis=1, keepdims=True))
    found[chip, core] = (weights / jnp.sum(weights, axis=1, keepdims=True)).astype(jnp.bfloat16)

    def back(step):
        return pltpu.make_async_remote_copy(
            src_ref=found.at[chip, core],
            dst_ref=found.at[chip, core],
            send_sem=back_send.at[step - 1],
            recv_sem=back_recv.at[step - 1],
            device_id=peer(step),
            device_id_type=MESH,
        )

    for step in range(1, chips):
        back(step).start()
    afterwards()
    for step in range(1, chips):
        back(step).wait_recv()
    last = pltpu.make_async_remote_copy(
        src_ref=found.at[:, core],
        dst_ref=found.at[:, core],
        send_sem=last_send,
        recv_sem=last_recv,
        device_id=mate,
        device_id_type=MESH,
    )
    last.start()
    last.wait_recv()
    everyone = found[...].astype(jnp.float32).reshape(slabs * count, 2 * OB)
    for which in range(2):
        compact[which] = everyone[:, which * OB : (which + 1) * OB].T.astype(jnp.bfloat16)
    done()
    spread(compact, own_blocks, post_ref)
    to_mate.wait_send()
    last.wait_send()
    for step in range(1, chips):
        to_chip(step).wait_send()
        back(step).wait_send()


def sum_over_dom(
    torus, images, post_ref, swapped, other_post, others_ready, swap, out_ref,
    partial, got1, got2, send1, recv1, send2, recv2,
):
    share = out_ref.shape[1]
    last = SIDE - 2
    steps = (1, -1, 2)

    def hop1(q, hop, i):
        axis, sign = ROUTES[q]
        block = lax.rem(torus.at[axis] - sign + SIDE, SIDE)
        source = partial.at[q, i, block] if hop == 0 else got1.at[q, hop - 1, i]
        return pltpu.make_async_remote_copy(
            src_ref=source,
            dst_ref=got1.at[q, hop, i],
            send_sem=send1.at[q, hop, i],
            recv_sem=recv1.at[q, hop, i],
            device_id=torus.neighbour(axis, sign),
            device_id_type=MESH,
        )

    def hop2(q, k, i):
        axis = other(ROUTES[q][0])
        block = lax.rem(torus.at[axis] + steps[k] + SIDE, SIDE)
        return pltpu.make_async_remote_copy(
            src_ref=got1.at[q, last, i, block],
            dst_ref=got2.at[q, k, i],
            send_sem=send2.at[q, k, i],
            recv_sem=recv2.at[q, k, i],
            device_id=torus.neighbour(axis, steps[k]),
            device_id_type=MESH,
        )

    def added(a, b):
        return (a.astype(jnp.float32) + b.astype(jnp.float32)).astype(jnp.bfloat16)

    routes = range(len(ROUTES))
    others_ready()

    @pl.loop(0, CHUNKS)
    def _(i):
        for q in routes:
            swap(q, i).wait_recv()
            value = jnp.dot(
                post_ref[...], images[group_of(q, i, held(torus, q))], preferred_element_type=jnp.float32
            )
            value = value + jnp.dot(other_post[q], swapped[q, i], preferred_element_type=jnp.float32)
            value = value.astype(jnp.bfloat16)
            for yy in range(SIDE):
                for xx in range(SIDE):
                    first, second = (xx, yy) if ROUTES[q][0] == "x" else (yy, xx)
                    begin = (yy * SIDE + xx) * share
                    partial[q, i, first, second] = value[begin : begin + share]
            hop1(q, 0, i).start()

    for hop in range(SIDE - 1):

        @pl.loop(0, CHUNKS)
        def _(i):
            for q in routes:
                axis, sign = ROUTES[q]
                block = lax.rem(torus.at[axis] - sign * (2 + hop) + 2 * SIDE, SIDE)
                hop1(q, hop, i).wait_recv()
                got1[q, hop, i] = added(got1[q, hop, i], partial[q, i, block])
                if hop < last:
                    hop1(q, hop + 1, i).start()
                else:
                    for k in range(len(steps)):
                        hop2(q, k, i).start()

    @pl.loop(0, CHUNKS)
    def _(i):
        for q in routes:
            for k in range(len(steps)):
                hop2(q, k, i).wait_recv()
            kept = held(torus, q)
            mine = got1[q, last, i, torus.at[other(ROUTES[q][0])]]
            out_ref[group_of(q, i, kept)] = added(got2[q, 2, i], mine)
            out_ref[group_of(q, i, 1 - kept)] = added(got2[q, 0, i], got2[q, 1, i])

    @pl.loop(0, CHUNKS)
    def _(i):
        for q in routes:
            swap(q, i).wait_send()
            for hop in range(SIDE - 1):
                hop1(q, hop, i).wait_send()
                hop2(q, hop, i).wait_send()


def insertion_weights(row_ref, part_ref, insert):
    lanes = row_ref.shape[1]
    rows = lax.broadcasted_iota(jnp.int32, (RD, lanes), 0).astype(jnp.float32)
    for b in range(row_ref.shape[0]):
        row = row_ref[b : b + 1, :]
        part = part_ref[b : b + 1, :]
        weight = jnp.where(rows == row, 1.0 - part, 0.0) + jnp.where(rows == row + 1, part, 0.0)
        high = weight.astype(jnp.bfloat16)
        insert[0, :, b * lanes : (b + 1) * lanes] = high
        insert[1, :, b * lanes : (b + 1) * lanes] = (weight - high.astype(jnp.float32)).astype(jnp.bfloat16)


def insert_pieces(torus, pieces_ref, slot_ref, insert, volume_ref, buffers, own_sem, out_sem, in_sem):
    slabs = lax.axis_size("slab")
    devices = lax.axis_size("dom") * slabs
    me = (torus.at["y"] * SIDE + torus.at["x"]) * slabs + torus.slab
    width = pieces_ref.shape[2]
    count = pieces_ref.shape[0] * pieces_ref.shape[1]
    block = RD
    owners = block // CAP
    numbers = lax.broadcasted_iota(jnp.int32, (block, count), 0)
    folds = CAP // TILE

    def packed(first, number=1):
        return buffers.at[0, pl.ds(first * folds, number * folds)]

    def got(first, number=1):
        return buffers.at[1, pl.ds(first * folds, number * folds)]

    pieces = pieces_ref[...].reshape(count, width)

    @pl.loop(0, devices // owners)
    def _(k):
        b = lax.rem(lax.div(me, owners) + k, devices // owners)
        first = b * owners
        pick = (numbers + b * block == slot_ref[...]).astype(jnp.float32).astype(jnp.bfloat16)
        value = jnp.dot(pick, pieces, preferred_element_type=jnp.float32)
        value = value.astype(jnp.bfloat16).reshape(owners * folds, TILE, width)
        buffers[0, pl.ds(first * folds, owners * folds)] = value

        @pl.loop(0, owners)
        def _(j):
            to = first + lax.rem(me + j, owners)

            @pl.when(to != me)
            def _():
                pltpu.make_async_remote_copy(
                    src_ref=packed(to),
                    dst_ref=got(me),
                    send_sem=out_sem,
                    recv_sem=in_sem,
                    device_id=(lax.div(to, slabs), lax.rem(to, slabs)),
                    device_id_type=MESH,
                ).start()

    own = pltpu.make_async_copy(packed(me), got(me), own_sem)
    own.start()
    own.wait()
    others = got(0, devices - 1)
    pltpu.make_async_copy(others, others, in_sem).wait()
    received = buffers[1, 0 : devices * folds].reshape(devices * CAP, width)
    volume = jnp.dot(insert[0], received, preferred_element_type=jnp.float32)
    volume_ref[...] = volume + jnp.dot(insert[1], received, preferred_element_type=jnp.float32)
    sent = packed(0, devices - 1)
    return pltpu.make_async_copy(sent, sent, out_sem)


def gather_rows(torus, volume_ref, next_ref, send_a, recv_a, send_b, recv_b):
    axes = ("x", "y")
    steps = (1, -1)
    rows = next_ref.shape[4]
    for c in range(2):
        for half in range(2):
            first = (2 * c + half) * rows
            next_ref[torus.at["y"], torus.at["x"], c, half] = volume_ref[
                first : first + rows
            ].astype(jnp.bfloat16)

    def spot(c, back1, back2, half=None):
        along = lax.rem(torus.at[axes[c]] + back1 + SIDE, SIDE)
        across = lax.rem(torus.at[axes[1 - c]] + back2 + SIDE, SIDE)
        y, x = (across, along) if c == 0 else (along, across)
        return next_ref.at[y, x, c] if half is None else next_ref.at[y, x, c, half]

    def copy(where, axis, step, send, recv):
        return pltpu.make_async_remote_copy(
            src_ref=where,
            dst_ref=where,
            send_sem=send,
            recv_sem=recv,
            device_id=torus.neighbour(axis, step),
            device_id_type=MESH,
        )

    def first_a(c, way):
        return copy(spot(c, 0, 0), axes[c], steps[way], send_a.at[0, c, way], recv_a.at[0, c, way])

    def second_a(c, way):
        where = spot(c, -steps[way], 0, way)
        return copy(where, axes[c], steps[way], send_a.at[1, c, way], recv_a.at[1, c, way])

    def first_b(c, j, way):
        where = spot(c, (0, -1, 1, 2)[j], 0)
        return copy(
            where, axes[1 - c], steps[way], send_b.at[0, c, j, way], recv_b.at[0, c, j, way]
        )

    def second_b(c, j, way):
        where = spot(c, (0, -1, 1, 2)[j], -steps[way], way)
        return copy(
            where, axes[1 - c], steps[way], send_b.at[1, c, j, way], recv_b.at[1, c, j, way]
        )

    both = range(2)
    for c in both:
        for way in both:
            first_a(c, way).start()
    for c in both:
        for way in both:
            first_b(c, 0, way).start()
    for way in both:
        for c in both:
            first_a(c, way).wait_recv()
            second_a(c, way).start()
            for out in both:
                first_b(c, 1 + way, out).start()

    def forward(j):
        for c in both:
            for way in both:
                first_b(c, j, way).wait_recv()
                second_b(c, j, way).start()

    forward(0)
    for c in both:
        for way in both:
            second_a(c, way).wait_recv()
        for out in both:
            first_b(c, 3, out).start()
    for j in range(1, SIDE):
        forward(j)
    for j in range(SIDE):
        for c in both:
            for way in both:
                second_b(c, j, way).wait_recv()
    for c in both:
        for way in both:
            first_a(c, way).wait_send()
            second_a(c, way).wait_send()
            for j in range(SIDE):
                first_b(c, j, way).wait_send()
                second_b(c, j, way).wait_send()


def project_kernel(
    x_ref, r_ref, noise_ref, blocks_ref, dest_ref, row_ref, part_ref, slot_ref,
    volume_ref, next_ref,
    images, scores, raw_x, raw_r, weighted, post, chosen, row_at, part_at, insert, pieces,
    swapped, own_blocks, other_blocks, compact, other_compact, other_post,
    swap_send, swap_recv, block_send, block_recv, compact_send, compact_recv, pass_send, pass_recv,
    *rest
):
    x_sem, r_sem = rest[:2]
    post_scratch = rest[2:7]
    counts, rows_at, parts_at = rest[7:10]
    post_sems = rest[10:18]
    sum_scratch = rest[18:25]
    insert_sems = rest[25:28]
    gather_sems = rest[28:]
    torus = Torus()
    column = Column()
    me = column.dom * column.slabs + column.slab
    barrier = pltpu.get_barrier_semaphore()
    others = [column.mate] + [column.peer(step) for step in range(1, column.chips)]
    others = others + [torus.neighbour(axis, sign) for axis, sign in ROUTES]
    for device in others:
        pl.semaphore_signal(barrier, inc=1, device_id=device, device_id_type=MESH)
    both = blocks_ref[...].astype(jnp.float32)
    half = chosen.shape[1] // 2
    both = jnp.concatenate([both[0:1]] * half + [both[1:2]] * half, axis=0)
    own_blocks[...] = both
    chosen[...] = both.T
    routes = range(len(ROUTES))

    def to_partner(q, source, target, send, recv):
        return pltpu.make_async_remote_copy(
            src_ref=source,
            dst_ref=target,
            send_sem=send,
            recv_sem=recv,
            device_id=partner(torus, q),
            device_id_type=MESH,
        )

    def swap(q, i):
        away = images.at[group_of(q, i, 1 - held(torus, q))]
        return to_partner(q, away, swapped.at[q, i], swap_send.at[q, i], swap_recv.at[q, i])

    def share_blocks(q):
        return to_partner(q, own_blocks, other_blocks.at[q], block_send.at[q], block_recv.at[q])

    core = column.core

    def share_post(q):
        target = other_compact.at[q, core]
        return to_partner(q, compact.at[core], target, compact_send.at[q], compact_recv.at[q])

    def pass_post(q):
        half_of = other_compact.at[q, core]
        return pltpu.make_async_remote_copy(
            src_ref=half_of,
            dst_ref=half_of,
            send_sem=pass_send.at[q],
            recv_sem=pass_recv.at[q],
            device_id=column.mate,
            device_id_type=MESH,
        )

    def begin():
        pl.semaphore_wait(barrier, len(others))
        for q in routes:
            share_blocks(q).start()

    def ready(t):
        @pl.when(t < CHUNKS - LATE)
        def _():
            for q in routes:
                swap(q, t).start()

    def done():
        for q in routes:
            share_post(q).start()
        for i in range(CHUNKS - LATE, CHUNKS):
            for q in routes:
                swap(q, i).start()

    def others_ready():
        for q in routes:
            share_post(q).wait_recv()
            pass_post(q).start()
        for q in routes:
            share_blocks(q).wait_recv()
            pass_post(q).wait_recv()
            spread(other_compact.at[q], other_blocks.at[q], other_post.at[q])

    partial_scores(
        x_ref, r_ref, noise_ref, images, scores, begin, ready, raw_x, raw_r, weighted, x_sem, r_sem
    )

    def tables():
        slot_tables(dest_ref, row_ref, part_ref, me, counts, rows_at, parts_at, row_at, part_at)

    def weights():
        insertion_weights(row_at, part_at, insert)

    posteriors(
        column, scores, chosen, own_blocks, compact, post, tables, weights, done,
        *post_scratch, *post_sems,
    )
    sum_over_dom(torus, images, post, swapped, other_post, others_ready, swap, pieces, *sum_scratch)
    sent = insert_pieces(torus, pieces, slot_ref, insert, volume_ref, raw_x, *insert_sems)
    gather_rows(torus, volume_ref, next_ref, *gather_sems)
    sent.wait()
    for q in routes:
        share_blocks(q).wait_send()
        share_post(q).wait_send()
        pass_post(q).wait_send()


def project(particles, references, inv_noise, blocks, destination, row_index, fraction, slot, doms, slabs):
    count, groups, width = particles.shape
    orients = references.shape[0]
    share = orients // doms
    chips = slabs // 2
    part = count // slabs
    devices = doms * slabs
    routes = len(ROUTES)
    hops = SIDE - 1
    piece = (share, width)
    vmem = pl.BlockSpec(memory_space=pltpu.VMEM)
    hbm = pl.BlockSpec(memory_space=pl.ANY)
    dma = pltpu.SemaphoreType.DMA
    table = pltpu.VMEM((doms, slabs * CAP), jnp.float32)
    return pl.pallas_call(
        project_kernel,
        out_shape=(
            jax.ShapeDtypeStruct((RD, width), jnp.float32),
            jax.ShapeDtypeStruct((SIDE, SIDE, 2, 2, RD // 4, width), jnp.bfloat16),
        ),
        in_specs=[hbm, hbm, pl.BlockSpec(memory_space=pltpu.SMEM)] + [vmem] * 5,
        out_specs=(vmem, vmem),
        scratch_shapes=[
            pltpu.VMEM((groups, count, width), jnp.bfloat16),
            pltpu.VMEM((count, orients), jnp.float32),
            pltpu.VMEM((2, count, TILE, width), jnp.bfloat16),
            pltpu.VMEM((2, orients, TILE, width), jnp.bfloat16),
            pltpu.VMEM((TILE, orients, width), jnp.bfloat16),
            pltpu.VMEM((orients, count), jnp.bfloat16),
            pltpu.VMEM((count, 8), jnp.float32),
            table,
            table,
            pltpu.VMEM((2, RD, devices * CAP), jnp.bfloat16),
            pltpu.VMEM((groups, share, width), jnp.bfloat16),
            pltpu.VMEM((routes, CHUNKS, count, width), jnp.bfloat16),
            pltpu.VMEM((8, count), jnp.float32),
            pltpu.VMEM((routes, 8, count), jnp.float32),
            pltpu.VMEM((2, OB, count), jnp.bfloat16),
            pltpu.VMEM((routes, 2, OB, count), jnp.bfloat16),
            pltpu.VMEM((routes, orients, count), jnp.bfloat16),
            dma((routes, CHUNKS)),
            dma((routes, CHUNKS)),
            dma((routes,)),
            dma((routes,)),
            dma((routes,)),
            dma((routes,)),
            dma((routes,)),
            dma((routes,)),
            dma((2,)),
            dma((2,)),
            pltpu.VMEM((2, chips, part, 2 * OB), jnp.float32),
            pltpu.VMEM((chips, part, 2 * OB), jnp.float32),
            pltpu.VMEM((chips, part, 2 * OB), jnp.float32),
            pltpu.VMEM((chips - 1, part, 2 * OB), jnp.float32),
            pltpu.VMEM((chips, 2, part, 2 * OB), jnp.bfloat16),
            pltpu.VMEM((2,) + destination.shape, jnp.float32),
            pltpu.VMEM((slabs * CAP, orients), jnp.float32),
            pltpu.VMEM((slabs * CAP, orients), jnp.float32),
            dma,
            dma,
            dma((chips - 1,)),
            dma((chips - 1,)),
            dma((chips - 1,)),
            dma((chips - 1,)),
            dma,
            dma,
            pltpu.VMEM((routes, CHUNKS, SIDE, SIDE) + piece, jnp.bfloat16),
            pltpu.VMEM((routes, hops, CHUNKS, SIDE) + piece, jnp.bfloat16),
            pltpu.VMEM((routes, hops, CHUNKS) + piece, jnp.bfloat16),
            dma((routes, hops, CHUNKS)),
            dma((routes, hops, CHUNKS)),
            dma((routes, hops, CHUNKS)),
            dma((routes, hops, CHUNKS)),
            dma,
            dma,
            dma,
            dma((2, 2, 2)),
            dma((2, 2, 2)),
            dma((2, 2, SIDE, 2)),
            dma((2, 2, SIDE, 2)),
        ],
        compiler_params=pltpu.CompilerParams(
            collective_id=0, has_side_effects=True, vmem_limit_bytes=VMEM_MIB * 1024 * 1024
        ),
        name="project",
    )(particles, references, inv_noise, blocks.T, destination, row_index, fraction, slot)


def send_slots(dests, devices):
    count = dests.shape[0]
    onehot = dests[:, None] == jnp.arange(devices, dtype=jnp.int32)[None, :]
    place = jnp.arange(count, dtype=jnp.int32)
    before = (place[None, :] < place[:, None]).astype(jnp.bfloat16)
    counts = jnp.dot(before, onehot.astype(jnp.bfloat16), preferred_element_type=jnp.float32)
    rank = jnp.sum(jnp.where(onehot, counts, 0.0), axis=1).astype(jnp.int32)
    return dests * CAP + rank


def shards(particles, blocks, references, inv_noise, destination, row_index, fraction):
    _, groups, row_width = particles.shape
    orients = references.shape[0]
    dom_size = lax.axis_size("dom")
    slab_size = lax.axis_size("slab")
    devices = dom_size * slab_size
    dom_pos = lax.axis_index("dom")
    slab_pos = lax.axis_index("slab")
    share = orients // dom_size
    my_dest = lax.dynamic_slice(
        destination, (slab_pos * groups, dom_pos * share), (groups, share)
    )
    slot = send_slots(my_dest.reshape(-1), devices)
    volume, next_slab = project(
        particles, references, inv_noise, blocks, destination, row_index, fraction,
        slot[None, :], dom_size, slab_size,
    )
    next_slab = next_slab.reshape(dom_size * RD, row_width)
    return (volume, next_slab)


def solution(mesh):
    return jax.shard_map(
        shards,
        mesh=mesh,
        in_specs=(
            P("dom", "slab", None),
            P("dom", None),
            P(None, "slab", None),
            P("slab"),
            P(),
            P(),
            P(),
        ),
        out_specs=(P(("dom", "slab"), None), P(None, "slab")),
        check_vma=False,
    )
```

```python
import functools

import jax
import jax.numpy as jnp
from jax import lax
from jax.experimental import pallas as pl
from jax.experimental.pallas import tpu as pltpu
from jax.sharding import PartitionSpec as P

MESH = pl.DeviceIdType.MESH
OB = 128
RD = 256
CAP = 16
SIDE = 4
CHUNKS = 5
VMEM_MIB = 49
LATE = 2
TILE = 8
ROWS = 64
BAND = 256
ROUTES = (("x", 1), ("x", -1), ("y", 1), ("y", -1))


class Torus:
    def __init__(self):
        dom = lax.axis_index("dom")
        self.slab = lax.axis_index("slab")
        self.at = {"y": lax.div(dom, SIDE), "x": lax.rem(dom, SIDE)}

    def neighbour(self, axis, step):
        at = dict(self.at)
        at[axis] = lax.rem(at[axis] + step + SIDE, SIDE)
        return (at["y"] * SIDE + at["x"], self.slab)


def other(axis):
    return "y" if axis == "x" else "x"


def held(torus, q):
    return lax.rem(torus.at[other(ROUTES[q][0])], 2)


def partner(torus, q):
    axis, sign = ROUTES[q]
    return torus.neighbour(other(axis), sign * (1 - 2 * held(torus, q)))


def group_of(q, i, which):
    return (i * len(ROUTES) + q) * 2 + which


def partial_scores(x_ref, r_ref, noise_ref, images, scores, begin, ready, raw_x, raw_r, weighted, x_sem, r_sem):
    particles, groups, _ = x_ref.shape
    orients = r_ref.shape[0]
    tile = raw_x.shape[2]
    tiles = groups // tile
    over_lanes = (((1,), (1,)), ((), ()))

    def fetch(ref, raw, sem, t):
        slot = lax.rem(t, 2)
        groups_of = pl.ds(pl.multiple_of(t * tile, tile), tile)
        return pltpu.make_async_copy(ref.at[:, groups_of], raw.at[slot], sem.at[slot])

    def start(t):
        fetch(x_ref, raw_x, x_sem, t).start()
        fetch(r_ref, raw_r, r_sem, t).start()

    start(0)
    start(1)
    begin()
    scores[...] = jnp.zeros_like(scores)

    @pl.loop(0, tiles)
    def _(t):
        slot = lax.rem(t, 2)
        first = t * tile
        fetch(x_ref, raw_x, x_sem, t).wait()

        @pl.loop(0, particles // ROWS)
        def _(b):
            span = pl.ds(pl.multiple_of(b * ROWS, ROWS), ROWS)
            images[pl.ds(first, tile), span] = jnp.swapaxes(raw_x[slot, span], 0, 1)

        fetch(r_ref, raw_r, r_sem, t).wait()

        @pl.loop(0, orients // ROWS)
        def _(b):
            span = pl.ds(pl.multiple_of(b * ROWS, ROWS), ROWS)
            value = jnp.swapaxes(raw_r[slot, span], 0, 1)
            for g in range(tile):
                scaled = value[g].astype(jnp.float32) * noise_ref[first + g]
                weighted[g, span] = scaled.astype(jnp.bfloat16)

        @pl.when(t + 2 < tiles)
        def _():
            start(t + 2)

        ready(t)

        for m in range(0, particles, BAND):
            acc = scores[m : m + BAND]
            for g in range(tile):
                acc = acc + lax.dot_general(
                    images[first + g, m : m + BAND], weighted[g], over_lanes,
                    preferred_element_type=jnp.float32,
                )
            scores[m : m + BAND] = acc


def slot_tables(dest_ref, row_ref, part_ref, me, counts, rows_at, parts_at, row_out, part_out):
    slabs = lax.axis_size("slab")
    orients = dest_ref.shape[1]
    groups = dest_ref.shape[0] // slabs
    doms = row_out.shape[0]
    shift = (orients // doms).bit_length() - 1
    here = lax.broadcasted_iota(jnp.int32, (orients, orients), 0)
    there = lax.broadcasted_iota(jnp.int32, (orients, orients), 1)
    same = lax.shift_right_logical(here, shift) == lax.shift_right_logical(there, shift)
    share = same.astype(jnp.float32).astype(jnp.bfloat16)
    before = jnp.where(same & (here < there), 1.0, 0.0).astype(jnp.bfloat16)
    mask = (dest_ref[...] == me).astype(jnp.float32).astype(jnp.bfloat16)
    counts[0] = jnp.dot(mask, before, preferred_element_type=jnp.float32)
    counts[1] = jnp.dot(mask, share, preferred_element_type=jnp.float32)
    lower = lax.broadcasted_iota(jnp.int32, (groups, groups), 0) > lax.broadcasted_iota(
        jnp.int32, (groups, groups), 1
    )
    lower = lower.astype(jnp.float32).astype(jnp.bfloat16)

    @pl.loop(0, slabs)
    def _(s):
        span = pl.ds(pl.multiple_of(s * groups, groups), groups)
        above = jnp.dot(
            lower, counts[1, span].astype(jnp.bfloat16), preferred_element_type=jnp.float32
        )
        rank = jnp.where(dest_ref[span] == me, counts[0, span] + above, -1.0)
        row = row_ref[span].astype(jnp.float32) + 1.0
        part = part_ref[span]
        found_rows = []
        found_parts = []
        for j in range(CAP):
            chosen = rank == j
            found_rows.append(jnp.sum(jnp.where(chosen, row, 0.0), axis=0, keepdims=True))
            found_parts.append(jnp.sum(jnp.where(chosen, part, 0.0), axis=0, keepdims=True))
        slots = pl.ds(pl.multiple_of(s * CAP, CAP), CAP)
        rows_at[slots] = jnp.concatenate(found_rows, axis=0)
        parts_at[slots] = jnp.concatenate(found_parts, axis=0)

    owner = lax.shift_right_logical(lax.broadcasted_iota(jnp.int32, (doms, orients), 1), shift)
    gather = (owner == lax.broadcasted_iota(jnp.int32, (doms, orients), 0)).astype(jnp.float32)
    over_lanes = (((1,), (1,)), ((), ()))
    for found, out in ((rows_at, row_out), (parts_at, part_out)):
        out[...] = lax.dot_general(
            gather, found[...], over_lanes,
            precision=lax.Precision.HIGHEST, preferred_element_type=jnp.float32,
        )
    row_out[...] = row_out[...] - 1.0


def spread(compact, blocks, post_ref):
    half = blocks.shape[0] // 2
    first, second = blocks[0:1], blocks[half : half + 1]
    for b in range(post_ref.shape[0] // OB):
        value = jnp.where(first == b, compact[0].astype(jnp.float32), 0.0)
        value = jnp.where(second == b, compact[1].astype(jnp.float32), value)
        post_ref[b * OB : (b + 1) * OB] = value.astype(jnp.bfloat16)


class Column:
    def __init__(self):
        self.dom = lax.axis_index("dom")
        self.slab = lax.axis_index("slab")
        self.slabs = lax.axis_size("slab")
        self.chips = self.slabs // 2
        self.chip = lax.div(self.slab, 2)
        self.core = lax.rem(self.slab, 2)
        self.mate = (self.dom, 2 * self.chip + 1 - self.core)

    def peer(self, step):
        return (self.dom, 2 * lax.rem(self.chip + step, self.chips) + self.core)


def posteriors(
    column, scores_ref, chosen_ref, own_blocks, compact, post_ref, done,
    mine, from_mate, total, from_chips, found,
    mate_send, mate_recv, chip_send, chip_recv, back_send, back_recv, last_send, last_recv,
):
    slabs, chips, chip, core = column.slabs, column.chips, column.chip, column.core
    mate, peer = column.mate, column.peer
    count = mine.shape[2]

    def picked(span, which):
        chosen = chosen_ref[span, SIDE * which : SIDE * which + 1]
        value = scores_ref[span, 0:OB]
        for b in range(1, scores_ref.shape[1] // OB):
            value = jnp.where(chosen == b, scores_ref[span, b * OB : (b + 1) * OB], value)
        return value

    for s in range(slabs):
        span = pl.ds(s * count, count)
        for which in range(2):
            mine[s % 2, s // 2, :, which * OB : (which + 1) * OB] = picked(span, which)
    to_mate = pltpu.make_async_remote_copy(
        src_ref=mine.at[1 - core],
        dst_ref=from_mate,
        send_sem=mate_send,
        recv_sem=mate_recv,
        device_id=mate,
        device_id_type=MESH,
    )
    to_mate.start()
    to_mate.wait_recv()
    total[...] = mine[core] + from_mate[...]

    def to_chip(step):
        return pltpu.make_async_remote_copy(
            src_ref=total.at[lax.rem(chip + step, chips)],
            dst_ref=from_chips.at[step - 1],
            send_sem=chip_send.at[step - 1],
            recv_sem=chip_recv.at[step - 1],
            device_id=peer(step),
            device_id_type=MESH,
        )

    for step in range(1, chips):
        to_chip(step).start()
    for step in range(1, chips):
        to_chip(step).wait_recv()
    scores = total[chip]
    for step in range(1, chips):
        scores = scores + from_chips[step - 1]
    weights = jnp.exp(scores - jnp.max(scores, axis=1, keepdims=True))
    found[chip, core] = (weights / jnp.sum(weights, axis=1, keepdims=True)).astype(jnp.bfloat16)

    def back(step):
        return pltpu.make_async_remote_copy(
            src_ref=found.at[chip, core],
            dst_ref=found.at[chip, core],
            send_sem=back_send.at[step - 1],
            recv_sem=back_recv.at[step - 1],
            device_id=peer(step),
            device_id_type=MESH,
        )

    for step in range(1, chips):
        back(step).start()
    for step in range(1, chips):
        back(step).wait_recv()
    last = pltpu.make_async_remote_copy(
        src_ref=found.at[:, core],
        dst_ref=found.at[:, core],
        send_sem=last_send,
        recv_sem=last_recv,
        device_id=mate,
        device_id_type=MESH,
    )
    last.start()
    last.wait_recv()
    everyone = found[...].astype(jnp.float32).reshape(slabs * count, 2 * OB)
    for which in range(2):
        compact[which] = everyone[:, which * OB : (which + 1) * OB].T.astype(jnp.bfloat16)
    done()
    spread(compact, own_blocks, post_ref)
    to_mate.wait_send()
    last.wait_send()
    for step in range(1, chips):
        to_chip(step).wait_send()
        back(step).wait_send()


def sum_over_dom(
    torus, images, post_ref, swapped, other_post, others_ready, swap, meanwhile, out_ref,
    partial, got1, got2, send1, recv1, send2, recv2,
):
    share = out_ref.shape[1]
    last = SIDE - 2
    steps = (1, -1, 2)

    def hop1(q, hop, i):
        axis, sign = ROUTES[q]
        block = lax.rem(torus.at[axis] - sign + SIDE, SIDE)
        source = partial.at[q, i, block] if hop == 0 else got1.at[q, hop - 1, i]
        return pltpu.make_async_remote_copy(
            src_ref=source,
            dst_ref=got1.at[q, hop, i],
            send_sem=send1.at[q, hop, i],
            recv_sem=recv1.at[q, hop, i],
            device_id=torus.neighbour(axis, sign),
            device_id_type=MESH,
        )

    def hop2(q, k, i):
        axis = other(ROUTES[q][0])
        block = lax.rem(torus.at[axis] + steps[k] + SIDE, SIDE)
        return pltpu.make_async_remote_copy(
            src_ref=got1.at[q, last, i, block],
            dst_ref=got2.at[q, k, i],
            send_sem=send2.at[q, k, i],
            recv_sem=recv2.at[q, k, i],
            device_id=torus.neighbour(axis, steps[k]),
            device_id_type=MESH,
        )

    def added(a, b):
        return (a.astype(jnp.float32) + b.astype(jnp.float32)).astype(jnp.bfloat16)

    routes = range(len(ROUTES))
    others_ready()

    @pl.loop(0, CHUNKS)
    def _(i):
        for q in routes:
            swap(q, i).wait_recv()
            value = jnp.dot(
                post_ref[...], images[group_of(q, i, held(torus, q))], preferred_element_type=jnp.float32
            )
            value = value + jnp.dot(other_post[q], swapped[q, i], preferred_element_type=jnp.float32)
            value = value.astype(jnp.bfloat16)
            for yy in range(SIDE):
                for xx in range(SIDE):
                    first, second = (xx, yy) if ROUTES[q][0] == "x" else (yy, xx)
                    begin = (yy * SIDE + xx) * share
                    partial[q, i, first, second] = value[begin : begin + share]
            hop1(q, 0, i).start()

    for hop in range(SIDE - 1):

        @pl.loop(0, CHUNKS)
        def _(i):
            for q in routes:
                axis, sign = ROUTES[q]
                block = lax.rem(torus.at[axis] - sign * (2 + hop) + 2 * SIDE, SIDE)
                hop1(q, hop, i).wait_recv()
                got1[q, hop, i] = added(got1[q, hop, i], partial[q, i, block])
                if hop < last:
                    hop1(q, hop + 1, i).start()
                else:
                    for k in range(len(steps)):
                        hop2(q, k, i).start()

        if hop < last:
            meanwhile[hop]()

    @pl.loop(0, CHUNKS)
    def _(i):
        for q in routes:
            for k in range(len(steps)):
                hop2(q, k, i).wait_recv()
            kept = held(torus, q)
            mine = got1[q, last, i, torus.at[other(ROUTES[q][0])]]
            out_ref[group_of(q, i, kept)] = added(got2[q, 2, i], mine)
            out_ref[group_of(q, i, 1 - kept)] = added(got2[q, 0, i], got2[q, 1, i])

    @pl.loop(0, CHUNKS)
    def _(i):
        for q in routes:
            swap(q, i).wait_send()
            for hop in range(SIDE - 1):
                hop1(q, hop, i).wait_send()
                hop2(q, hop, i).wait_send()


def insertion_weights(row_ref, part_ref, insert):
    lanes = row_ref.shape[1]
    rows = lax.broadcasted_iota(jnp.int32, (RD, lanes), 0).astype(jnp.float32)
    for b in range(row_ref.shape[0]):
        row = row_ref[b : b + 1, :]
        part = part_ref[b : b + 1, :]
        weight = jnp.where(rows == row, 1.0 - part, 0.0) + jnp.where(rows == row + 1, part, 0.0)
        high = weight.astype(jnp.bfloat16)
        insert[0, :, b * lanes : (b + 1) * lanes] = high
        insert[1, :, b * lanes : (b + 1) * lanes] = (weight - high.astype(jnp.float32)).astype(jnp.bfloat16)


def insert_pieces(torus, pieces_ref, slot_ref, insert, volume_ref, buffers, own_sem, out_sem, in_sem):
    slabs = lax.axis_size("slab")
    devices = lax.axis_size("dom") * slabs
    me = (torus.at["y"] * SIDE + torus.at["x"]) * slabs + torus.slab
    width = pieces_ref.shape[2]
    count = pieces_ref.shape[0] * pieces_ref.shape[1]
    block = RD
    owners = block // CAP
    numbers = lax.broadcasted_iota(jnp.int32, (block, count), 0)
    shift = CAP.bit_length() - 1
    numbers = lax.shift_right_logical(numbers, shift) * (slabs * CAP) + (numbers & (CAP - 1))
    folds = CAP // TILE

    def packed(first, number=1):
        return buffers.at[0, pl.ds(first * folds, number * folds)]

    def got(first, number=1):
        return buffers.at[1, pl.ds(first * folds, number * folds)]

    pieces = pieces_ref[...].reshape(count, width)

    @pl.loop(0, slabs)
    def _(k):
        b = lax.rem(torus.slab + k, slabs)
        pick = (numbers + b * CAP == slot_ref[...]).astype(jnp.float32).astype(jnp.bfloat16)
        value = jnp.dot(pick, pieces, preferred_element_type=jnp.float32)
        value = value.astype(jnp.bfloat16).reshape(owners * folds, TILE, width)
        for j in range(owners):
            buffers[0, pl.ds((j * slabs + b) * folds, folds)] = value[j * folds : (j + 1) * folds]

        @pl.loop(0, owners)
        def _(j):
            to = lax.rem(lax.div(me, slabs) + j, owners) * slabs + b

            @pl.when(to != me)
            def _():
                pltpu.make_async_remote_copy(
                    src_ref=packed(to),
                    dst_ref=got(me),
                    send_sem=out_sem,
                    recv_sem=in_sem,
                    device_id=(lax.div(to, slabs), lax.rem(to, slabs)),
                    device_id_type=MESH,
                ).start()

    own = pltpu.make_async_copy(packed(me), got(me), own_sem)
    own.start()
    own.wait()
    others = got(0, devices - 1)
    pltpu.make_async_copy(others, others, in_sem).wait()
    received = buffers[1, 0 : devices * folds].reshape(devices * CAP, width)
    volume = jnp.dot(insert[0], received, preferred_element_type=jnp.float32)
    volume_ref[...] = volume + jnp.dot(insert[1], received, preferred_element_type=jnp.float32)
    sent = packed(0, devices - 1)
    return pltpu.make_async_copy(sent, sent, out_sem)


def gather_rows(torus, volume_ref, next_ref, send_a, recv_a, send_b, recv_b):
    axes = ("x", "y")
    steps = (1, -1)
    rows = next_ref.shape[4]
    for c in range(2):
        for half in range(2):
            first = (2 * c + half) * rows
            next_ref[torus.at["y"], torus.at["x"], c, half] = volume_ref[
                first : first + rows
            ].astype(jnp.bfloat16)

    def spot(c, back1, back2, half=None):
        along = lax.rem(torus.at[axes[c]] + back1 + SIDE, SIDE)
        across = lax.rem(torus.at[axes[1 - c]] + back2 + SIDE, SIDE)
        y, x = (across, along) if c == 0 else (along, across)
        return next_ref.at[y, x, c] if half is None else next_ref.at[y, x, c, half]

    def copy(where, axis, step, send, recv):
        return pltpu.make_async_remote_copy(
            src_ref=where,
            dst_ref=where,
            send_sem=send,
            recv_sem=recv,
            device_id=torus.neighbour(axis, step),
            device_id_type=MESH,
        )

    def first_a(c, way):
        return copy(spot(c, 0, 0), axes[c], steps[way], send_a.at[0, c, way], recv_a.at[0, c, way])

    def second_a(c, way):
        where = spot(c, -steps[way], 0, way)
        return copy(where, axes[c], steps[way], send_a.at[1, c, way], recv_a.at[1, c, way])

    def first_b(c, j, way):
        where = spot(c, (0, -1, 1, 2)[j], 0)
        return copy(
            where, axes[1 - c], steps[way], send_b.at[0, c, j, way], recv_b.at[0, c, j, way]
        )

    def second_b(c, j, way):
        where = spot(c, (0, -1, 1, 2)[j], -steps[way], way)
        return copy(
            where, axes[1 - c], steps[way], send_b.at[1, c, j, way], recv_b.at[1, c, j, way]
        )

    both = range(2)
    for c in both:
        for way in both:
            first_a(c, way).start()
    for c in both:
        for way in both:
            first_b(c, 0, way).start()
    for way in both:
        for c in both:
            first_a(c, way).wait_recv()
            second_a(c, way).start()
            for out in both:
                first_b(c, 1 + way, out).start()

    def forward(j):
        for c in both:
            for way in both:
                first_b(c, j, way).wait_recv()
                second_b(c, j, way).start()

    forward(0)
    for c in both:
        for way in both:
            second_a(c, way).wait_recv()
        for out in both:
            first_b(c, 3, out).start()
    for j in range(1, SIDE):
        forward(j)
    for j in range(SIDE):
        for c in both:
            for way in both:
                second_b(c, j, way).wait_recv()
    for c in both:
        for way in both:
            first_a(c, way).wait_send()
            second_a(c, way).wait_send()
            for j in range(SIDE):
                first_b(c, j, way).wait_send()
                second_b(c, j, way).wait_send()


def project_kernel(
    x_ref, r_ref, noise_ref, blocks_ref, dest_ref, row_ref, part_ref, slot_ref,
    volume_ref, next_ref,
    images, scores, raw_x, raw_r, weighted, post, chosen, row_at, part_at, insert, pieces,
    swapped, own_blocks, other_blocks, compact, other_compact, other_post,
    swap_send, swap_recv, block_send, block_recv, compact_send, compact_recv, pass_send, pass_recv,
    *rest
):
    x_sem, r_sem = rest[:2]
    post_scratch = rest[2:7]
    counts, rows_at, parts_at = rest[7:10]
    post_sems = rest[10:18]
    sum_scratch = rest[18:25]
    insert_sems = rest[25:28]
    gather_sems = rest[28:]
    torus = Torus()
    column = Column()
    me = column.dom * column.slabs + column.slab
    barrier = pltpu.get_barrier_semaphore()
    others = [column.mate] + [column.peer(step) for step in range(1, column.chips)]
    others = others + [torus.neighbour(axis, sign) for axis, sign in ROUTES]
    for device in others:
        pl.semaphore_signal(barrier, inc=1, device_id=device, device_id_type=MESH)
    both = blocks_ref[...].astype(jnp.float32)
    half = chosen.shape[1] // 2
    both = jnp.concatenate([both[0:1]] * half + [both[1:2]] * half, axis=0)
    own_blocks[...] = both
    chosen[...] = both.T
    routes = range(len(ROUTES))

    def to_partner(q, source, target, send, recv):
        return pltpu.make_async_remote_copy(
            src_ref=source,
            dst_ref=target,
            send_sem=send,
            recv_sem=recv,
            device_id=partner(torus, q),
            device_id_type=MESH,
        )

    def swap(q, i):
        away = images.at[group_of(q, i, 1 - held(torus, q))]
        return to_partner(q, away, swapped.at[q, i], swap_send.at[q, i], swap_recv.at[q, i])

    def share_blocks(q):
        return to_partner(q, own_blocks, other_blocks.at[q], block_send.at[q], block_recv.at[q])

    core = column.core

    def share_post(q):
        target = other_compact.at[q, core]
        return to_partner(q, compact.at[core], target, compact_send.at[q], compact_recv.at[q])

    def pass_post(q):
        half_of = other_compact.at[q, core]
        return pltpu.make_async_remote_copy(
            src_ref=half_of,
            dst_ref=half_of,
            send_sem=pass_send.at[q],
            recv_sem=pass_recv.at[q],
            device_id=column.mate,
            device_id_type=MESH,
        )

    def begin():
        pl.semaphore_wait(barrier, len(others))
        for q in routes:
            share_blocks(q).start()

    def ready(t):
        @pl.when(t < CHUNKS - LATE)
        def _():
            for q in routes:
                swap(q, t).start()

    def done():
        for q in routes:
            share_post(q).start()
        for i in range(CHUNKS - LATE, CHUNKS):
            for q in routes:
                swap(q, i).start()

    def others_ready():
        for q in routes:
            share_post(q).wait_recv()
            pass_post(q).start()
        for q in routes:
            share_blocks(q).wait_recv()
            pass_post(q).wait_recv()
            spread(other_compact.at[q], other_blocks.at[q], other_post.at[q])

    partial_scores(
        x_ref, r_ref, noise_ref, images, scores, begin, ready, raw_x, raw_r, weighted, x_sem, r_sem
    )

    def tables():
        slot_tables(dest_ref, row_ref, part_ref, me, counts, rows_at, parts_at, row_at, part_at)

    def weights():
        insertion_weights(row_at, part_at, insert)

    posteriors(
        column, scores, chosen, own_blocks, compact, post, done,
        *post_scratch, *post_sems,
    )
    sum_over_dom(torus, images, post, swapped, other_post, others_ready, swap, (tables, weights), pieces, *sum_scratch)
    sent = insert_pieces(torus, pieces, slot_ref, insert, volume_ref, raw_x, *insert_sems)
    gather_rows(torus, volume_ref, next_ref, *gather_sems)
    sent.wait()
    for q in routes:
        share_blocks(q).wait_send()
        share_post(q).wait_send()
        pass_post(q).wait_send()


def project(particles, references, inv_noise, blocks, destination, row_index, fraction, slot, doms, slabs):
    count, groups, width = particles.shape
    orients = references.shape[0]
    share = orients // doms
    chips = slabs // 2
    part = count // slabs
    devices = doms * slabs
    routes = len(ROUTES)
    hops = SIDE - 1
    piece = (share, width)
    vmem = pl.BlockSpec(memory_space=pltpu.VMEM)
    hbm = pl.BlockSpec(memory_space=pl.ANY)
    dma = pltpu.SemaphoreType.DMA
    table = pltpu.VMEM((doms, slabs * CAP), jnp.float32)
    return pl.pallas_call(
        project_kernel,
        out_shape=(
            jax.ShapeDtypeStruct((RD, width), jnp.float32),
            jax.ShapeDtypeStruct((SIDE, SIDE, 2, 2, RD // 4, width), jnp.bfloat16),
        ),
        in_specs=[hbm, hbm, pl.BlockSpec(memory_space=pltpu.SMEM)] + [vmem] * 5,
        out_specs=(vmem, vmem),
        scratch_shapes=[
            pltpu.VMEM((groups, count, width), jnp.bfloat16),
            pltpu.VMEM((count, orients), jnp.float32),
            pltpu.VMEM((2, count, TILE, width), jnp.bfloat16),
            pltpu.VMEM((2, orients, TILE, width), jnp.bfloat16),
            pltpu.VMEM((TILE, orients, width), jnp.bfloat16),
            pltpu.VMEM((orients, count), jnp.bfloat16),
            pltpu.VMEM((count, 8), jnp.float32),
            table,
            table,
            pltpu.VMEM((2, RD, devices * CAP), jnp.bfloat16),
            pltpu.VMEM((groups, share, width), jnp.bfloat16),
            pltpu.VMEM((routes, CHUNKS, count, width), jnp.bfloat16),
            pltpu.VMEM((8, count), jnp.float32),
            pltpu.VMEM((routes, 8, count), jnp.float32),
            pltpu.VMEM((2, OB, count), jnp.bfloat16),
            pltpu.VMEM((routes, 2, OB, count), jnp.bfloat16),
            pltpu.VMEM((routes, orients, count), jnp.bfloat16),
            dma((routes, CHUNKS)),
            dma((routes, CHUNKS)),
            dma((routes,)),
            dma((routes,)),
            dma((routes,)),
            dma((routes,)),
            dma((routes,)),
            dma((routes,)),
            dma((2,)),
            dma((2,)),
            pltpu.VMEM((2, chips, part, 2 * OB), jnp.float32),
            pltpu.VMEM((chips, part, 2 * OB), jnp.float32),
            pltpu.VMEM((chips, part, 2 * OB), jnp.float32),
            pltpu.VMEM((chips - 1, part, 2 * OB), jnp.float32),
            pltpu.VMEM((chips, 2, part, 2 * OB), jnp.bfloat16),
            pltpu.VMEM((2,) + destination.shape, jnp.float32),
            pltpu.VMEM((slabs * CAP, orients), jnp.float32),
            pltpu.VMEM((slabs * CAP, orients), jnp.float32),
            dma,
            dma,
            dma((chips - 1,)),
            dma((chips - 1,)),
            dma((chips - 1,)),
            dma((chips - 1,)),
            dma,
            dma,
            pltpu.VMEM((routes, CHUNKS, SIDE, SIDE) + piece, jnp.bfloat16),
            pltpu.VMEM((routes, hops, CHUNKS, SIDE) + piece, jnp.bfloat16),
            pltpu.VMEM((routes, hops, CHUNKS) + piece, jnp.bfloat16),
            dma((routes, hops, CHUNKS)),
            dma((routes, hops, CHUNKS)),
            dma((routes, hops, CHUNKS)),
            dma((routes, hops, CHUNKS)),
            dma,
            dma,
            dma,
            dma((2, 2, 2)),
            dma((2, 2, 2)),
            dma((2, 2, SIDE, 2)),
            dma((2, 2, SIDE, 2)),
        ],
        compiler_params=pltpu.CompilerParams(
            collective_id=0, has_side_effects=True, vmem_limit_bytes=VMEM_MIB * 1024 * 1024
        ),
        name="project",
    )(particles, references, inv_noise, blocks.T, destination, row_index, fraction, slot)


def send_slots(dests, devices):
    count = dests.shape[0]
    onehot = dests[:, None] == jnp.arange(devices, dtype=jnp.int32)[None, :]
    place = jnp.arange(count, dtype=jnp.int32)
    before = (place[None, :] < place[:, None]).astype(jnp.bfloat16)
    counts = jnp.dot(before, onehot.astype(jnp.bfloat16), preferred_element_type=jnp.float32)
    rank = jnp.sum(jnp.where(onehot, counts, 0.0), axis=1).astype(jnp.int32)
    return dests * CAP + rank


def shards(particles, blocks, references, inv_noise, destination, row_index, fraction):
    _, groups, row_width = particles.shape
    orients = references.shape[0]
    dom_size = lax.axis_size("dom")
    slab_size = lax.axis_size("slab")
    devices = dom_size * slab_size
    dom_pos = lax.axis_index("dom")
    slab_pos = lax.axis_index("slab")
    share = orients // dom_size
    my_dest = lax.dynamic_slice(
        destination, (slab_pos * groups, dom_pos * share), (groups, share)
    )
    slot = send_slots(my_dest.reshape(-1), devices)
    volume, next_slab = project(
        particles, references, inv_noise, blocks, destination, row_index, fraction,
        slot[None, :], dom_size, slab_size,
    )
    next_slab = next_slab.reshape(dom_size * RD, row_width)
    return (volume, next_slab)


def solution(mesh):
    return jax.shard_map(
        shards,
        mesh=mesh,
        in_specs=(
            P("dom", "slab", None),
            P("dom", None),
            P(None, "slab", None),
            P("slab"),
            P(),
            P(),
            P(),
        ),
        out_specs=(P(("dom", "slab"), None), P(None, "slab")),
        check_vma=False,
    )
```
